128 devices in a mesh: rep: 16 (over x, y_lo, core), shard: 8 (over y_hi, z).
Axes of the slice: x: 4, y: 4 (y_hi: 2, y_lo: 2; y = y_hi * 2 + y_lo), z: 4, core: 2. Of those that a mesh axis runs over, the one named last changes fastest.
Arguments:
- x_in: bfloat16 [40960, 1024], P(('rep', 'shard')), may hold values from -6 to 6
- cotangent: float32 [40960, 1024], P(('rep', 'shard')), may hold values from -24 to 24
- ln1_gain: bfloat16 [1024], P('shard'), may hold values from 0.5 to 1.5
- ln1_bias: bfloat16 [1024], P('shard'), may hold values from -3 to 3
- w_qkv: bfloat16 [1024, 3072], P('shard'), may hold values from -8 to 8
- q_bias: bfloat16 [1024], P('shard'), may hold values from -3 to 3
- v_bias: bfloat16 [1024], P('shard'), may hold values from -3 to 3
- w_attn_out: bfloat16 [1024, 1024], P('shard'), may hold values from -0.75 to 0.75
- out_bias: bfloat16 [1024], P('shard'), may hold values from -3 to 3
- ln2_gain: bfloat16 [1024], P('shard'), may hold values from 0.5 to 1.5
- ln2_bias: bfloat16 [1024], P('shard'), may hold values from -3 to 3
- w_up: bfloat16 [1024, 4096], P('shard'), may hold values from -0.1875 to 0.1875
- up_bias: bfloat16 [4096], P('shard'), may hold values from -3 to 3
- w_down: bfloat16 [4096, 1024], P('shard'), may hold values from -0.09375 to 0.09375
- down_bias: bfloat16 [1024], P('shard'), may hold values from -3 to 3
Outputs:
- block_out: bfloat16 [40960, 1024], P(('rep', 'shard'))
- input_grad: float32 [40960, 1024], P(('rep', 'shard'))
- grad_ln1_gain: float32 [1024], P('shard')
- grad_ln1_bias: float32 [1024], P('shard')
- grad_w_qkv: float32 [1024, 3072], P('shard')
- grad_q_bias: float32 [1024], P('shard')
- grad_v_bias: float32 [1024], P('shard')
- grad_w_attn_out: float32 [1024, 1024], P('shard')
- grad_out_bias: float32 [1024], P('shard')
- grad_ln2_gain: float32 [1024], P('shard')
- grad_ln2_bias: float32 [1024], P('shard')
- grad_w_up: float32 [1024, 4096], P('shard')
- grad_up_bias: float32 [4096], P('shard')
- grad_w_down: float32 [4096, 1024], P('shard')
- grad_down_bias: float32 [1024], P('shard')
The draws below stay inside these ranges and needn't reach their ends.
All inputs are finite; a program needn't handle non-finite values.
Results may differ from the reference program's by a relative error of at most 0.023.
Values may be sent and summed in bfloat16 or wider, within the bound.
A program may use at most 192 MiB of HBM per device.

```python
import math
import jax
import jax.numpy as jnp
from jax import lax

D = 1024
HEADS = 16
HEAD_DIM = 64
FF = 4096
SEQ = 320
SEQS = 128
TOKENS = 40960
N_REP = 16
N_SHARD = 8


def draw_w_qkv(key, part):
    base = jax.random.normal(key, (D, 3 * D), jnp.float32) * D ** (-0.5)
    return jnp.clip(base, -8.0, 8.0).astype(jnp.bfloat16)


def spiked(entries, own_key, source, target, parts, factor):
    owner, partner = [(jnp.arange(entries.shape[axis_at]) // (entries.shape[axis_at] // parts)).reshape([-1 if axis == axis_at else 1 for axis in range(entries.ndim)]) for axis_at in (source, target)]
    chosen = jax.random.permutation(own_key, parts)[partner]
    strong = (owner == chosen) | (owner == (partner + parts // 2) % parts)
    return jnp.where(strong, factor * entries, entries)


def levels(rng, extent, split, smallest, high):
    gain, own = 1.0, jax.random.fold_in(rng, 6)
    for axis_at, shards_of in split:
        heights = jnp.exp(jax.random.uniform(jax.random.fold_in(own, axis_at), (shards_of,), jnp.float32, smallest / len(split), high / len(split)))
        gain = gain * jnp.repeat(heights, extent[axis_at] // shards_of).reshape([-1 if axis == axis_at else 1 for axis in range(len(extent))])
    return gain


def gaussian(stream_key, dims, spread, reach, split=(), held_as=jnp.bfloat16):
    level = levels(stream_key, dims, split, -0.22, 0.18) if split else 1.0
    array = jax.random.normal(stream_key, dims, jnp.float32) * spread * level
    return jnp.minimum(jnp.maximum(array, -reach), reach).astype(held_as)


def heavy_noise(key, dims, scale, most, split, heavy, held_as=jnp.bfloat16):
    entries = scale * jax.random.normal(key, dims, jnp.float32)
    if split:
        entries = entries * levels(key, dims, split, -0.22, 0.18)
    return jnp.clip(spiked(entries, jax.random.fold_in(key, 3), *heavy), -most, most).astype(held_as)


def setup_inputs(seed: int = 0) -> dict:
    seeds = jax.random.split(jax.random.key(seed), 16)
    x_in = gaussian(seeds[0], (TOKENS, D), 1.0, 6.0, ((0, 128),))
    cotangent = heavy_noise(seeds[1], (TOKENS, D), 1.0, 24.0, ((0, 128),), (0, 1, 128, 5.5), jnp.float32)
    ln1_gain = jnp.clip(1.0 + 0.1 * jax.random.normal(seeds[2], (D,), jnp.float32), 0.5, 1.5).astype(jnp.bfloat16)
    ln1_bias = gaussian(seeds[3], (D,), 0.5, 3.0, ((0, 8),))
    w_qkv = draw_w_qkv(jax.random.fold_in(seeds[15], 71), 0)
    q_bias = gaussian(seeds[5], (D,), 0.5, 3.0, ((0, 8),))
    v_bias = gaussian(seeds[6], (D,), 0.5, 3.0, ((0, 8),))
    w_attn_out = gaussian(seeds[7], (D, D), (D // 16) ** -0.5, 0.75, ((0, 8),))
    out_bias = gaussian(seeds[8], (D,), 0.5, 3.0, ((0, 8),))
    ln2_gain = jnp.clip(1.0 + 0.1 * jax.random.normal(seeds[9], (D,), jnp.float32), 0.5, 1.5).astype(jnp.bfloat16)
    ln2_bias = gaussian(seeds[10], (D,), 0.5, 3.0, ((0, 8),))
    w_up = gaussian(seeds[11], (D, FF), D ** -0.5, 0.1875, ((0, 8),))
    up_bias = gaussian(seeds[12], (FF,), 0.5, 3.0, ((0, 8),))
    w_down = gaussian(seeds[13], (FF, D), FF ** -0.5, 0.09375, ((0, 8),))
    down_bias = gaussian(seeds[14], (D,), 0.5, 3.0, ((0, 8),))
    return {"x_in": x_in, "cotangent": cotangent, "ln1_gain": ln1_gain, "ln1_bias": ln1_bias, "w_qkv": w_qkv, "q_bias": q_bias, "v_bias": v_bias, "w_attn_out": w_attn_out, "out_bias": out_bias, "ln2_gain": ln2_gain, "ln2_bias": ln2_bias, "w_up": w_up, "up_bias": up_bias, "w_down": w_down, "down_bias": down_bias}


eps_norm = 1e-05
sqrt_two_pi = math.sqrt(2.0 / math.pi)
cubic_coef = 0.044715

def gelu_value(up_projected):
    inner = sqrt_two_pi * (up_projected + cubic_coef * up_projected * up_projected * up_projected)
    return 0.5 * up_projected * (1.0 + jnp.tanh(inner))

def gelu_slope(up_projected):
    tanh_val = jnp.tanh(sqrt_two_pi * (up_projected + cubic_coef * up_projected * up_projected * up_projected))
    return 0.5 * (1.0 + tanh_val) + 0.5 * up_projected * (1.0 - tanh_val * tanh_val) * sqrt_two_pi * (1.0 + 3.0 * cubic_coef * up_projected * up_projected)

def layer_normalize(rows_in, gain_vec, bias_vec):
    center = rows_in - lax.optimization_barrier(jnp.mean(rows_in, axis=-1, keepdims=True))
    inv_std = lax.rsqrt(lax.optimization_barrier(jnp.mean(center * center, axis=-1, keepdims=True)) + eps_norm)
    x_hat = center * inv_std
    return (x_hat * gain_vec.astype(jnp.float32) + bias_vec.astype(jnp.float32), x_hat, inv_std)

def layer_normalize_backward(d_normed, x_hat, inv_std):
    return inv_std * (d_normed - lax.optimization_barrier(jnp.mean(d_normed, axis=-1, keepdims=True)) - x_hat * lax.optimization_barrier(jnp.mean(d_normed * x_hat, axis=-1, keepdims=True)))

def split_heads(rows_in):
    return rows_in.reshape(rows_in.shape[0] // SEQ, SEQ, HEADS, HEAD_DIM)

def merge_heads(heads_in):
    return heads_in.reshape(-1, HEADS * HEAD_DIM)

def alibi_bias():
    positions = jnp.arange(SEQ)
    distance = (positions[:, None] - positions[None, :]).astype(jnp.float32)
    head_ids = jnp.arange(HEADS).astype(jnp.float32)
    slopes = jnp.exp2(-8.0 * (head_ids + 1.0) / HEADS)
    offsets = -slopes[:, None, None] * distance[None, :, :]
    return jnp.where(distance[None, :, :] >= 0.0, offsets, -jnp.inf)

def attn_scores(query_heads, key_heads):
    scores = jnp.einsum('bqhd,bkhd->bhqk', query_heads.astype(jnp.float32), key_heads.astype(jnp.float32))
    return scores * HEAD_DIM ** (-0.5) + alibi_bias()[None]

def layer_forward(x_in, params):
    first_norm_gain, first_norm_bias, w_qkv, q_bias, v_bias, w_attn_out, out_bias, second_norm_gain, second_norm_bias, w_up, up_bias, w_down, down_bias = params
    model_width = x_in.shape[1]
    residual_input = x_in.astype(jnp.float32)
    first_normalized, first_centered_scaled, first_inverse_scale = layer_normalize(residual_input, first_norm_gain, first_norm_bias)
    first_activation = first_normalized.astype(jnp.bfloat16)
    united_proj = jnp.dot(first_activation, w_qkv, preferred_element_type=jnp.float32)
    query_block = (united_proj[:, :model_width] + q_bias.astype(jnp.float32)).astype(jnp.bfloat16)
    key_block = united_proj[:, model_width:2 * model_width].astype(jnp.bfloat16)
    value_block = (united_proj[:, 2 * model_width:] + v_bias.astype(jnp.float32)).astype(jnp.bfloat16)
    scores = attn_scores(split_heads(query_block), split_heads(key_block))
    maximum = lax.optimization_barrier(jnp.max(scores, axis=-1, keepdims=True))
    log_normalizer = maximum + jnp.log(lax.optimization_barrier(jnp.sum(jnp.exp(scores - maximum), axis=-1, keepdims=True)))
    probab = jnp.exp(scores - log_normalizer).astype(jnp.bfloat16)
    attended_context = merge_heads(jnp.einsum('bhqk,bkhd->bqhd', probab.astype(jnp.float32), split_heads(value_block).astype(jnp.float32))).astype(jnp.bfloat16)
    residual_middle = residual_input + jnp.dot(attended_context, w_attn_out, preferred_element_type=jnp.float32) + out_bias.astype(jnp.float32)
    second_normalized, second_centered_scaled, second_inverse_scale = layer_normalize(residual_middle, second_norm_gain, second_norm_bias)
    second_activation = second_normalized.astype(jnp.bfloat16)
    up_projected = jnp.dot(second_activation, w_up, preferred_element_type=jnp.float32) + up_bias.astype(jnp.float32)
    hidden_activations = gelu_value(up_projected).astype(jnp.bfloat16)
    block_out = (residual_middle + jnp.dot(hidden_activations, w_down, preferred_element_type=jnp.float32) + down_bias.astype(jnp.float32)).astype(jnp.bfloat16)
    saved_state = (first_centered_scaled, first_inverse_scale, first_activation, query_block, key_block, value_block, log_normalizer, attended_context, second_centered_scaled, second_inverse_scale, second_activation, up_projected, hidden_activations)
    return (block_out, saved_state)

def layer_backward(cotangent, saved_state, params):
    first_norm_gain, first_norm_bias, w_qkv, q_bias, v_bias, w_attn_out, out_bias, second_norm_gain, second_norm_bias, w_up, up_bias, w_down, down_bias = params
    first_centered_scaled, first_inverse_scale, first_activation, query_block, key_block, value_block, log_normalizer, attended_context, second_centered_scaled, second_inverse_scale, second_activation, up_projected, hidden_activations = saved_state
    cot_b = cotangent.astype(jnp.bfloat16)
    g_down_bias = lax.optimization_barrier(jnp.sum(cotangent, axis=0))
    g_w_down = jnp.dot(hidden_activations.T, cot_b, preferred_element_type=jnp.float32)
    d_up = jnp.dot(cot_b, w_down.T, preferred_element_type=jnp.float32) * gelu_slope(up_projected)
    g_up_bias = lax.optimization_barrier(jnp.sum(d_up, axis=0))
    d_up_b = d_up.astype(jnp.bfloat16)
    g_w_up = jnp.dot(second_activation.T, d_up_b, preferred_element_type=jnp.float32)
    second_activation_grad = jnp.dot(d_up_b, w_up.T, preferred_element_type=jnp.float32)
    second_gain_grad = lax.optimization_barrier(jnp.sum(second_activation_grad * second_centered_scaled, axis=0))
    g_bias_two = lax.optimization_barrier(jnp.sum(second_activation_grad, axis=0))
    middle_residual_grad = cotangent + layer_normalize_backward(second_activation_grad * second_norm_gain.astype(jnp.float32), second_centered_scaled, second_inverse_scale)
    g_out_bias = lax.optimization_barrier(jnp.sum(middle_residual_grad, axis=0))
    d_mid_b = middle_residual_grad.astype(jnp.bfloat16)
    g_w_attn_out = jnp.dot(attended_context.T, d_mid_b, preferred_element_type=jnp.float32)
    d_context = jnp.dot(d_mid_b, w_attn_out.T, preferred_element_type=jnp.float32).astype(jnp.bfloat16)
    query_heads = split_heads(query_block)
    key_heads = split_heads(key_block)
    scores = attn_scores(query_heads, key_heads)
    probab = jnp.exp(scores - log_normalizer)
    probab_b = probab.astype(jnp.bfloat16)
    ctx_heads = split_heads(d_context).astype(jnp.float32)
    d_value = merge_heads(jnp.einsum('bhqk,bqhd->bkhd', probab_b.astype(jnp.float32), ctx_heads))
    d_prob = jnp.einsum('bqhd,bkhd->bhqk', ctx_heads, split_heads(value_block).astype(jnp.float32))
    d_score = probab * (d_prob - lax.optimization_barrier(jnp.sum(probab * d_prob, axis=-1, keepdims=True)))
    d_score_b = d_score.astype(jnp.bfloat16).astype(jnp.float32)
    d_query = merge_heads(jnp.einsum('bhqk,bkhd->bqhd', d_score_b, key_heads.astype(jnp.float32))) * HEAD_DIM ** (-0.5)
    d_key = merge_heads(jnp.einsum('bhqk,bqhd->bkhd', d_score_b, query_heads.astype(jnp.float32))) * HEAD_DIM ** (-0.5)
    g_q_bias = lax.optimization_barrier(jnp.sum(d_query, axis=0))
    g_v_bias = lax.optimization_barrier(jnp.sum(d_value, axis=0))
    d_united = jnp.concatenate([d_query, d_key, d_value], axis=1).astype(jnp.bfloat16)
    g_w_qkv = jnp.dot(first_activation.T, d_united, preferred_element_type=jnp.float32)
    first_activation_grad = jnp.dot(d_united, w_qkv.T, preferred_element_type=jnp.float32)
    first_gain_grad = lax.optimization_barrier(jnp.sum(first_activation_grad * first_centered_scaled, axis=0))
    g_bias_one = lax.optimization_barrier(jnp.sum(first_activation_grad, axis=0))
    layer_input_grad = middle_residual_grad + layer_normalize_backward(first_activation_grad * first_norm_gain.astype(jnp.float32), first_centered_scaled, first_inverse_scale)
    grads = (first_gain_grad, g_bias_one, g_w_qkv, g_q_bias, g_v_bias, g_w_attn_out, g_out_bias, second_gain_grad, g_bias_two, g_w_up, g_up_bias, g_w_down, g_down_bias)
    return (layer_input_grad, grads)

def reference(x_in, cotangent, ln1_gain, ln1_bias, w_qkv, q_bias, v_bias, w_attn_out, out_bias, ln2_gain, ln2_bias, w_up, up_bias, w_down, down_bias):
    params = (ln1_gain, ln1_bias, w_qkv, q_bias, v_bias, w_attn_out, out_bias, ln2_gain, ln2_bias, w_up, up_bias, w_down, down_bias)
    blocks = N_REP * N_SHARD
    rows_dev = x_in.shape[0] // blocks
    x_blocks = x_in.reshape(blocks, rows_dev, D)
    cot_blocks = cotangent.reshape(blocks, rows_dev, D)

    def one_block(running, block_pair):
        block_out, saved_state = layer_forward(block_pair[0], params)
        layer_input_grad, grads = layer_backward(block_pair[1], saved_state, params)
        running = tuple((running_sum + lax.optimization_barrier(block_grad.astype(jnp.bfloat16)).astype(jnp.float32) for running_sum, block_grad in zip(running, grads)))
        return (running, (block_out, layer_input_grad))
    initial = tuple((jnp.zeros(param.shape, jnp.float32) for param in params))
    totals, (outs_all, grads_in) = lax.scan(one_block, initial, (x_blocks, cot_blocks))
    scaled = tuple((running_sum / SEQS for running_sum in totals))
    return (outs_all.reshape(-1, D), grads_in.reshape(-1, D), scaled[0], scaled[1], scaled[2], scaled[3], scaled[4], scaled[5], scaled[6], scaled[7], scaled[8], scaled[9], scaled[10], scaled[11], scaled[12])
```

```python
import math

import jax
import jax.numpy as jnp
from jax import lax
from jax.experimental import pallas as pl
from jax.experimental.pallas import tpu as pltpu
from jax.sharding import PartitionSpec as P

HEADS = 16
HEAD_DIM = 64
SEQ = 320


eps_norm = 1e-05
sqrt_two_pi = math.sqrt(2.0 / math.pi)
cubic_coef = 0.044715


def gelu_value(up_projected):
    inner = sqrt_two_pi * (up_projected + cubic_coef * up_projected * up_projected * up_projected)
    return 0.5 * up_projected * (1.0 + jnp.tanh(inner))


def gelu_slope(up_projected):
    tanh_val = jnp.tanh(
        sqrt_two_pi * (up_projected + cubic_coef * up_projected * up_projected * up_projected)
    )
    return 0.5 * (1.0 + tanh_val) + 0.5 * up_projected * (
        1.0 - tanh_val * tanh_val
    ) * sqrt_two_pi * (1.0 + 3.0 * cubic_coef * up_projected * up_projected)


def layer_normalize(rows_in, gain_vec, bias_vec):
    center = rows_in - jnp.mean(rows_in, axis=-1, keepdims=True)
    inv_std = lax.rsqrt(jnp.mean(center * center, axis=-1, keepdims=True) + eps_norm)
    x_hat = center * inv_std
    return (x_hat * gain_vec.astype(jnp.float32) + bias_vec.astype(jnp.float32), x_hat, inv_std)


def layer_normalize_backward(d_normed, x_hat, inv_std):
    return inv_std * (
        d_normed
        - jnp.mean(d_normed, axis=-1, keepdims=True)
        - x_hat * jnp.mean(d_normed * x_hat, axis=-1, keepdims=True)
    )


def split_heads(rows_in):
    return rows_in.reshape(rows_in.shape[0] // SEQ, SEQ, HEADS, HEAD_DIM)


def merge_heads(heads_in):
    return heads_in.reshape(-1, HEADS * HEAD_DIM)


def alibi_bias():
    positions = jnp.arange(SEQ)
    distance = (positions[:, None] - positions[None, :]).astype(jnp.float32)
    head_ids = jnp.arange(HEADS).astype(jnp.float32)
    slopes = jnp.exp2(-8.0 * (head_ids + 1.0) / HEADS)
    offsets = -slopes[:, None, None] * distance[None, :, :]
    return jnp.where(distance[None, :, :] >= 0.0, offsets, -jnp.inf)


def attn_scores(query_heads, key_heads):
    scores = jnp.einsum(
        "bqhd,bkhd->bhqk", query_heads, key_heads, preferred_element_type=jnp.float32
    )
    return scores * HEAD_DIM ** (-0.5) + alibi_bias()[None]


def layer_forward(x_in, params):
    (
        first_norm_gain,
        first_norm_bias,
        w_qkv,
        q_bias,
        v_bias,
        w_attn_out,
        out_bias,
        second_norm_gain,
        second_norm_bias,
        w_up,
        up_bias,
        w_down,
        down_bias,
    ) = params
    model_width = x_in.shape[1]
    residual_input = x_in.astype(jnp.float32)
    first_normalized, first_centered_scaled, first_inverse_scale = layer_normalize(
        residual_input, first_norm_gain, first_norm_bias
    )
    first_activation = first_normalized.astype(jnp.bfloat16)
    united_proj = jnp.dot(first_activation, w_qkv, preferred_element_type=jnp.float32)
    query_block = (united_proj[:, :model_width] + q_bias.astype(jnp.float32)).astype(jnp.bfloat16)
    key_block = united_proj[:, model_width : 2 * model_width].astype(jnp.bfloat16)
    value_block = (united_proj[:, 2 * model_width :] + v_bias.astype(jnp.float32)).astype(
        jnp.bfloat16
    )
    scores = attn_scores(split_heads(query_block), split_heads(key_block))
    maximum = jnp.max(scores, axis=-1, keepdims=True)
    log_normalizer = maximum + jnp.log(jnp.sum(jnp.exp(scores - maximum), axis=-1, keepdims=True))
    probab = jnp.exp(scores - log_normalizer).astype(jnp.bfloat16)
    attended_context = merge_heads(
        jnp.einsum(
            "bhqk,bkhd->bqhd", probab, split_heads(value_block), preferred_element_type=jnp.float32
        )
    ).astype(jnp.bfloat16)
    residual_middle = (
        residual_input
        + jnp.dot(attended_context, w_attn_out, preferred_element_type=jnp.float32)
        + out_bias.astype(jnp.float32)
    )
    second_normalized, second_centered_scaled, second_inverse_scale = layer_normalize(
        residual_middle, second_norm_gain, second_norm_bias
    )
    second_activation = second_normalized.astype(jnp.bfloat16)
    up_projected = jnp.dot(
        second_activation, w_up, preferred_element_type=jnp.float32
    ) + up_bias.astype(jnp.float32)
    hidden_activations = gelu_value(up_projected).astype(jnp.bfloat16)
    block_out = (
        residual_middle
        + jnp.dot(hidden_activations, w_down, preferred_element_type=jnp.float32)
        + down_bias.astype(jnp.float32)
    ).astype(jnp.bfloat16)
    saved_state = (
        first_centered_scaled,
        first_inverse_scale,
        first_activation,
        query_block,
        key_block,
        value_block,
        log_normalizer,
        attended_context,
        second_centered_scaled,
        second_inverse_scale,
        second_activation,
        up_projected,
        hidden_activations,
    )
    return (block_out, saved_state)


def layer_backward(cotangent, saved_state, params):
    (
        first_norm_gain,
        first_norm_bias,
        w_qkv,
        q_bias,
        v_bias,
        w_attn_out,
        out_bias,
        second_norm_gain,
        second_norm_bias,
        w_up,
        up_bias,
        w_down,
        down_bias,
    ) = params
    (
        first_centered_scaled,
        first_inverse_scale,
        first_activation,
        query_block,
        key_block,
        value_block,
        log_normalizer,
        attended_context,
        second_centered_scaled,
        second_inverse_scale,
        second_activation,
        up_projected,
        hidden_activations,
    ) = saved_state
    cot_b = cotangent.astype(jnp.bfloat16)
    g_down_bias = jnp.sum(cotangent, axis=0)
    g_w_down = jnp.dot(hidden_activations.T, cot_b, preferred_element_type=jnp.float32)
    d_up = jnp.dot(cot_b, w_down.T, preferred_element_type=jnp.float32) * gelu_slope(up_projected)
    g_up_bias = jnp.sum(d_up, axis=0)
    d_up_b = d_up.astype(jnp.bfloat16)
    g_w_up = jnp.dot(second_activation.T, d_up_b, preferred_element_type=jnp.float32)
    second_activation_grad = jnp.dot(d_up_b, w_up.T, preferred_element_type=jnp.float32)
    second_gain_grad = jnp.sum(second_activation_grad * second_centered_scaled, axis=0)
    g_bias_two = jnp.sum(second_activation_grad, axis=0)
    middle_residual_grad = cotangent + layer_normalize_backward(
        second_activation_grad * second_norm_gain.astype(jnp.float32),
        second_centered_scaled,
        second_inverse_scale,
    )
    g_out_bias = jnp.sum(middle_residual_grad, axis=0)
    d_mid_b = middle_residual_grad.astype(jnp.bfloat16)
    g_w_attn_out = jnp.dot(attended_context.T, d_mid_b, preferred_element_type=jnp.float32)
    d_context = jnp.dot(d_mid_b, w_attn_out.T, preferred_element_type=jnp.float32).astype(
        jnp.bfloat16
    )
    query_heads = split_heads(query_block)
    key_heads = split_heads(key_block)
    scores = attn_scores(query_heads, key_heads)
    probab = jnp.exp(scores - log_normalizer)
    probab_b = probab.astype(jnp.bfloat16)
    ctx_heads = split_heads(d_context)
    d_value = merge_heads(
        jnp.einsum("bhqk,bqhd->bkhd", probab_b, ctx_heads, preferred_element_type=jnp.float32)
    )
    d_prob = jnp.einsum(
        "bqhd,bkhd->bhqk", ctx_heads, split_heads(value_block), preferred_element_type=jnp.float32
    )
    d_score = probab * (d_prob - jnp.sum(probab * d_prob, axis=-1, keepdims=True))
    d_score_b = d_score.astype(jnp.bfloat16)
    d_query = merge_heads(
        jnp.einsum("bhqk,bkhd->bqhd", d_score_b, key_heads, preferred_element_type=jnp.float32)
    ) * HEAD_DIM ** (-0.5)
    d_key = merge_heads(
        jnp.einsum("bhqk,bqhd->bkhd", d_score_b, query_heads, preferred_element_type=jnp.float32)
    ) * HEAD_DIM ** (-0.5)
    g_q_bias = jnp.sum(d_query, axis=0)
    g_v_bias = jnp.sum(d_value, axis=0)
    d_united = jnp.concatenate([d_query, d_key, d_value], axis=1).astype(jnp.bfloat16)
    g_w_qkv = jnp.dot(first_activation.T, d_united, preferred_element_type=jnp.float32)
    first_activation_grad = jnp.dot(d_united, w_qkv.T, preferred_element_type=jnp.float32)
    first_gain_grad = jnp.sum(first_activation_grad * first_centered_scaled, axis=0)
    g_bias_one = jnp.sum(first_activation_grad, axis=0)
    layer_input_grad = middle_residual_grad + layer_normalize_backward(
        first_activation_grad * first_norm_gain.astype(jnp.float32),
        first_centered_scaled,
        first_inverse_scale,
    )
    grads = (
        first_gain_grad,
        g_bias_one,
        g_w_qkv,
        g_q_bias,
        g_v_bias,
        g_w_attn_out,
        g_out_bias,
        second_gain_grad,
        g_bias_two,
        g_w_up,
        g_up_bias,
        g_w_down,
        g_down_bias,
    )
    return (layer_input_grad, grads)


MESH = pl.DeviceIdType.MESH
BF16 = jnp.bfloat16
F32 = jnp.float32


def place():
    rep = lax.axis_index("rep")
    shard = lax.axis_index("shard")
    x, lo, core = rep // 4, (rep // 2) % 2, rep % 2
    hi, z = shard // 4, shard % 4

    def dev(x_, lo_, core_, hi_, z_):
        return ((x_ * 2 + lo_) * 2 + core_, hi_ * 4 + z_)

    peers = dict(
        xr=dev((x + 1) % 4, lo, core, hi, z),
        xl=dev((x + 3) % 4, lo, core, hi, z),
        zr=dev(x, lo, core, hi, (z + 1) % 4),
        zl=dev(x, lo, core, hi, (z + 3) % 4),
        cross=dev(x, 1 - lo, core, 1 - hi, z),
        ylo=dev(x, 1 - lo, core, hi, z),
        core=dev(x, lo, 1 - core, hi, z),
    )
    return x, core, hi, z, peers


def greet(peers, names):
    barrier = pltpu.get_barrier_semaphore()
    for name in names:
        pl.semaphore_signal(barrier, inc=1, device_id=peers[name], device_id_type=MESH)
    pl.semaphore_wait(barrier, len(names))


GATHER_CHUNKS = (
    (4, 0, 128, 0, 128),
    (0, 0, 128, 0, 3072),
    (1, 0, 128, 0, 1024),
    (2, 0, 128, 0, 2048),
    (2, 0, 128, 2048, 2048),
    (3, 0, 256, 0, 1024),
    (3, 256, 256, 0, 1024),
)


def gather_kernel(*refs):
    ins, outs = refs[:5], refs[5:10]
    send_sem, recv_sem, own_sem = refs[10:]
    x, core, hi, z, peers = place()
    other = 1 - hi
    me = hi * 4 + z
    greet(peers, ("xr", "xl", "zr", "zl", "cross", "core"))
    own = []
    for a in range(5):
        cp = pltpu.make_async_copy(ins[a], outs[a].at[me], own_sem.at[a])
        cp.start()
        own.append(cp)

    started = []
    by_chunk = [dict() for _ in GATHER_CHUNKS]

    def send(k, name, src, dst, to):
        slot = len(by_chunk[k])
        cp = pltpu.make_async_remote_copy(
            src_ref=src,
            dst_ref=dst,
            send_sem=send_sem.at[k, slot],
            recv_sem=recv_sem.at[k, slot],
            device_id=peers[to],
            device_id_type=MESH,
        )
        cp.start()
        by_chunk[k][name] = cp
        started.append(cp)

    def part(k, which, first, count):
        a, r0, rows, c0, cols = GATHER_CHUNKS[k]
        start = pl.multiple_of(r0 + first, 16)
        return outs[a].at[which, pl.ds(start, count), pl.ds(c0, cols)]

    def stage0(k):
        a, r0, rows, c0, cols = GATHER_CHUNKS[k]
        half, sub = rows // 2, rows // 8
        mine = ins[a].at[pl.ds(pl.multiple_of(r0 + core * half, 16), half), pl.ds(c0, cols)]
        send(k, "z1r", mine, part(k, me, core * half, half), "zr")
        send(k, "z1l", mine, part(k, me, core * half, half), "zl")
        first = core * half + x * sub
        quarter = ins[a].at[pl.ds(pl.multiple_of(r0 + first, 16), sub), pl.ds(c0, cols)]
        send(k, "y0", quarter, part(k, me, first, sub), "cross")

    def stage1(k):
        rows = GATHER_CHUNKS[k][2]
        half, sub = rows // 2, rows // 8
        base = core * half
        left, right = hi * 4 + (z + 3) % 4, hi * 4 + (z + 1) % 4
        by_chunk[k]["z1r"].wait_recv()
        view = part(k, left, base, half // 2)
        send(k, "z2r", view, view, "zr")
        view = part(k, left, base + x * sub, sub)
        send(k, "y1", view, view, "cross")
        view = part(k, left, base, half)
        send(k, "c1", view, view, "core")
        by_chunk[k]["z1l"].wait_recv()
        view = part(k, right, base + half // 2, half // 2)
        send(k, "z2l", view, view, "zl")
        view = part(k, right, base + x * sub, sub)
        send(k, "y2", view, view, "cross")
        view = part(k, right, base, half)
        send(k, "c2", view, view, "core")

    def stage2(k):
        rows = GATHER_CHUNKS[k][2]
        half, sub = rows // 2, rows // 8
        base = core * half
        far = hi * 4 + (z + 2) % 4
        by_chunk[k]["z2r"].wait_recv()
        by_chunk[k]["z2l"].wait_recv()
        view = part(k, far, base + x * sub, sub)
        send(k, "y3", view, view, "cross")
        view = part(k, far, base, half)
        send(k, "c3", view, view, "core")

    def stage3(k):
        rows = GATHER_CHUNKS[k][2]
        half, sub = rows // 2, rows // 8
        for name in ("y0", "y1", "y2", "y3"):
            by_chunk[k][name].wait_recv()
        view = part(k, pl.ds(other * 4, 4), core * half + x * sub, sub)
        send(k, "x1r", view, view, "xr")
        send(k, "x1l", view, view, "xl")
        send(k, "c4", view, view, "core")

    def stage4(k):
        rows = GATHER_CHUNKS[k][2]
        half, sub = rows // 2, rows // 8
        for name, from_x, nxt, first, to in (
            ("x1r", (x + 3) % 4, "x2r", 0, "xr"),
            ("x1l", (x + 1) % 4, "x2l", 2, "xl"),
        ):
            by_chunk[k][name].wait_recv()
            view = part(k, pl.ds(other * 4 + first, 2), core * half + from_x * sub, sub)
            send(k, nxt, view, view, to)
            view = part(k, pl.ds(other * 4, 4), core * half + from_x * sub, sub)
            send(k, "c" + nxt, view, view, "core")

    def stage5(k):
        rows = GATHER_CHUNKS[k][2]
        half, sub = rows // 2, rows // 8
        by_chunk[k]["x2r"].wait_recv()
        by_chunk[k]["x2l"].wait_recv()
        view = part(k, pl.ds(other * 4, 4), core * half + ((x + 2) % 4) * sub, sub)
        send(k, "c7", view, view, "core")

    stages = (stage0, stage1, stage2, stage3, stage4, stage5)
    n = len(GATHER_CHUNKS)
    for k in range(n):
        stage0(k)
    for t in range(1, n + len(stages) - 1):
        for s in range(len(stages) - 1, 0, -1):
            if 0 <= t - s < n:
                stages[s](t - s)
    for k in range(n):
        for name, cp in by_chunk[k].items():
            if name[0] == "c":
                cp.wait_recv()
    for cp in started:
        cp.wait_send()
    for cp in own:
        cp.wait()


GATHER_COPIES = 20


def gather_all(small, w_qkv, w_attn_out, w_up, w_down):
    shards = (w_qkv, w_attn_out, w_up, w_down, small)
    n = len(GATHER_CHUNKS)
    outs = pl.pallas_call(
        gather_kernel,
        out_shape=[jax.ShapeDtypeStruct((8, *s.shape), s.dtype) for s in shards],
        in_specs=[pl.BlockSpec(memory_space=pl.ANY)] * 5,
        out_specs=[pl.BlockSpec(memory_space=pl.ANY)] * 5,
        scratch_shapes=[
            pltpu.SemaphoreType.DMA((n, GATHER_COPIES)),
            pltpu.SemaphoreType.DMA((n, GATHER_COPIES)),
            pltpu.SemaphoreType.DMA((5,)),
        ],
        compiler_params=pltpu.CompilerParams(collective_id=0, has_side_effects=True),
        name="gather_weights",
    )(*shards)
    wq, wo, wu, wd, sm = outs
    return (
        wq.reshape(-1, wq.shape[-1]),
        wo.reshape(-1, wo.shape[-1]),
        wu.reshape(-1, wu.shape[-1]),
        wd.reshape(-1, wd.shape[-1]),
        sm,
    )


NCH = 12
WIDE = 1024
SMALLW = 256
RCOPIES = 24


def reduce_kernel(*refs):
    g_qkv, g_o, g_up, g_down, g_small = refs[:5]
    fin_big, fin_small = refs[5:7]
    scr = refs[7:]
    nb = 9
    big, small = scr[:nb], scr[nb : 2 * nb]
    b_send, b_recv, b_own, s_send, s_recv, s_own = scr[2 * nb :]
    x, core, hi, z, peers = place()
    other = 1 - hi
    greet(peers, ("xr", "xl", "zr", "zl", "cross", "ylo", "core"))
    xp, xm, xo = (x + 1) % 4, (x + 3) % 4, (x + 2) % 4
    zp, zm, zo = (z + 1) % 4, (z + 3) % 4, (z + 2) % 4

    def sub(i):
        return pl.ds(pl.multiple_of(i * 16, 16), 16)

    def add(ref, idx, *others):
        total = ref[idx].astype(F32)
        for o_ref, o_idx in others:
            total = total + o_ref[o_idx].astype(F32)
        ref[idx] = total.astype(BF16)

    def build(bufs, fin, send_sem, recv_sem, own_sem, wide):
        acc, rc, rx1, rx2, ry, rz1, rz2, rf1, rf2 = bufs
        hw = wide // 2
        cols_a, cols_b = pl.ds(0, hw), pl.ds(hw, hw)

        def copy(k, slot, src, dst, to):
            return pltpu.make_async_remote_copy(
                src_ref=src,
                dst_ref=dst,
                send_sem=send_sem.at[k, slot],
                recv_sem=recv_sem.at[k, slot],
                device_id=peers[to],
                device_id_type=MESH,
            )

        def rows_of(i):
            return pl.ds(pl.multiple_of(core * 64 + i * 16, 16), 16)

        def x1(k):
            return (
                copy(k, 1, acc.at[k, pl.ds(other * 4, 2), sub(xo)], rx1.at[k, 0], "xr"),
                copy(k, 2, acc.at[k, pl.ds(other * 4 + 2, 2), sub(xo)], rx1.at[k, 1], "xl"),
            )

        def x2(k):
            return (
                copy(k, 3, acc.at[k, pl.ds(other * 4, 4), sub(xp)], rx2.at[k, 0], "xr"),
                copy(k, 4, acc.at[k, pl.ds(other * 4, 4), sub(xm)], rx2.at[k, 1], "xl"),
            )

        def y1(k):
            return (copy(k, 5, acc.at[k, pl.ds(other * 4, 4), sub(x)], ry.at[k], "cross"),)

        def z1(k):
            return (
                copy(k, 6, acc.at[k, hi * 4 + zo, pl.ds(0, 32)], rz1.at[k, 0], "zr"),
                copy(k, 7, acc.at[k, hi * 4 + zo, pl.ds(32, 32)], rz1.at[k, 1], "zl"),
            )

        def z2(k):
            return (
                copy(k, 8, acc.at[k, hi * 4 + zp], rz2.at[k, 0], "zr"),
                copy(k, 9, acc.at[k, hi * 4 + zm], rz2.at[k, 1], "zl"),
            )

        me = hi * 4 + z

        def f1(k):
            return (
                copy(k, 10, acc.at[k, me, sub(xo), cols_a], rf1.at[k, 0], "xr"),
                copy(k, 11, acc.at[k, me, sub(xo), cols_b], rf1.at[k, 1], "xl"),
            )

        def f2(k):
            return (
                copy(k, 12, acc.at[k, me, sub(xp)], rf2.at[k, 0], "xr"),
                copy(k, 13, acc.at[k, me, sub(xm)], rf2.at[k, 1], "xl"),
            )

        def fy(k):
            return (copy(k, 14, acc.at[k, me, sub(x)], rf2.at[k, 2], "ylo"),)

        def g1(k):
            view = fin.at[k, rows_of(x)]
            return (
                copy(k, 15, view, view, "xr"),
                copy(k, 16, view, view, "xl"),
                copy(k, 17, view, view, "core"),
            )

        def g2(k):
            va, vb = fin.at[k, rows_of(xm), cols_a], fin.at[k, rows_of(xp), cols_b]
            ca, cb = fin.at[k, rows_of(xm)], fin.at[k, rows_of(xp)]
            return (
                copy(k, 18, va, va, "xr"),
                copy(k, 19, vb, vb, "xl"),
                copy(k, 20, ca, ca, "core"),
                copy(k, 21, cb, cb, "core"),
            )

        def g3(k):
            view = fin.at[k, rows_of(xo)]
            return (copy(k, 22, view, view, "core"),)

        def go(copies):
            for cp in copies:
                cp.start()

        def got(copies):
            for cp in copies:
                cp.wait_recv()

        def s0(k):
            copy(k, 0, rc.at[k], rc.at[k], "core").wait_recv()
            pltpu.make_async_copy(acc.at[k], acc.at[k], own_sem.at[k]).wait()

            def body(i, carry):
                add(acc, (k, i), (rc, (k, i)))
                return carry

            lax.fori_loop(0, 8, body, 0)
            go(x1(k))

        def s1(k):
            got(x1(k))
            add(acc, (k, pl.ds(other * 4, 2), sub(xp)), (rx1, (k, 0)))
            add(acc, (k, pl.ds(other * 4 + 2, 2), sub(xm)), (rx1, (k, 1)))
            go(x2(k))

        def s2(k):
            got(x2(k))
            add(acc, (k, pl.ds(other * 4, 4), sub(x)), (rx2, (k, 0)), (rx2, (k, 1)))
            go(y1(k))

        def s3(k):
            got(y1(k))
            add(acc, (k, pl.ds(hi * 4, 4), sub(x)), (ry, (k,)))
            go(z1(k))

        def s4(k):
            got(z1(k))
            add(acc, (k, hi * 4 + zp, pl.ds(0, 32)), (rz1, (k, 0)))
            add(acc, (k, hi * 4 + zm, pl.ds(32, 32)), (rz1, (k, 1)))
            go(z2(k))

        def s5(k):
            got(z2(k))
            add(acc, (k, me), (rz2, (k, 0)), (rz2, (k, 1)))
            go(f1(k))

        def s6(k):
            got(f1(k))
            add(acc, (k, me, sub(xp), cols_a), (rf1, (k, 0)))
            add(acc, (k, me, sub(xm), cols_b), (rf1, (k, 1)))
            go(f2(k))

        def s7(k):
            got(f2(k))
            add(acc, (k, me, sub(x)), (rf2, (k, 0)), (rf2, (k, 1)))
            go(fy(k))

        def s8(k):
            got(fy(k))
            total = acc[k, me, sub(x)].astype(F32) + rf2[k, 2].astype(F32)
            fin[k, rows_of(x)] = total.astype(BF16)
            go(g1(k))

        def s9(k):
            a, b, c = g1(k)
            got((a, b))
            go(g2(k))

        def s10(k):
            got(g2(k)[:2])
            go(g3(k))

        def s11(k):
            got(g1(k)[2:])
            got(g2(k)[2:])
            got(g3(k))

        def done(k):
            copy(k, 0, rc.at[k], rc.at[k], "core").wait_send()
            for f in (x1, x2, y1, z1, z2, f1, f2, fy, g1, g2, g3):
                for cp in f(k):
                    cp.wait_send()

        return copy, (s0, s1, s2, s3, s4, s5, s6, s7, s8, s9, s10, s11), done

    b_copy, b_stages, b_done = build(big, fin_big, b_send, b_recv, b_own, WIDE)
    s_copy, s_stages, s_done = build(small, fin_small, s_send, s_recv, s_own, SMALLW)

    theirs = pl.ds(pl.multiple_of((1 - core) * 64, 16), 64)
    mine = pl.ds(pl.multiple_of(core * 64, 16), 64)

    def source(k, rows):
        if k < 4:
            return g_down.at[:, k, rows]
        if k < 8:
            return g_up.at[:, rows, pl.ds((k - 4) * WIDE, WIDE)]
        if k < 9:
            return g_o.at[:, rows]
        return g_qkv.at[:, rows, pl.ds((k - 9) * WIDE, WIDE)]

    for k in range(NCH):
        b_copy(k, 0, source(k, theirs), big[1].at[k], "core").start()
        pltpu.make_async_copy(source(k, mine), big[0].at[k], b_own.at[k]).start()
    s_copy(0, 0, g_small.at[:, theirs], small[1].at[0], "core").start()
    pltpu.make_async_copy(g_small.at[:, mine], small[0].at[0], s_own.at[0]).start()

    depth = len(b_stages)

    def step(t, carry):
        for s in range(depth - 1, -1, -1):
            k = t - s

            @pl.when((k >= 0) & (k < NCH))
            def _():
                b_stages[s](k)

        return carry

    lax.fori_loop(0, NCH + depth - 1, step, 0)
    for s in range(depth):
        s_stages[s](0)

    def finish(k, carry):
        b_done(k)
        return carry

    lax.fori_loop(0, NCH, finish, 0)
    s_done(0)


def reduce_all(g_qkv, g_o, g_up, g_down, g_small):
    def bufs(n, wide):
        return [
            pltpu.VMEM((n, 8, 64, wide), BF16),
            pltpu.VMEM((n, 8, 64, wide), BF16),
            pltpu.VMEM((n, 2, 2, 16, wide), BF16),
            pltpu.VMEM((n, 2, 4, 16, wide), BF16),
            pltpu.VMEM((n, 4, 16, wide), BF16),
            pltpu.VMEM((n, 2, 32, wide), BF16),
            pltpu.VMEM((n, 2, 64, wide), BF16),
            pltpu.VMEM((n, 2, 16, wide // 2), BF16),
            pltpu.VMEM((n, 3, 16, wide), BF16),
        ]

    def sems(n):
        return [
            pltpu.SemaphoreType.DMA((n, RCOPIES)),
            pltpu.SemaphoreType.DMA((n, RCOPIES)),
            pltpu.SemaphoreType.DMA((n,)),
        ]

    return pl.pallas_call(
        reduce_kernel,
        out_shape=[
            jax.ShapeDtypeStruct((NCH, 128, WIDE), BF16),
            jax.ShapeDtypeStruct((1, 128, SMALLW), BF16),
        ],
        in_specs=[pl.BlockSpec(memory_space=pl.ANY)] * 5,
        out_specs=[pl.BlockSpec(memory_space=pltpu.VMEM)] * 2,
        scratch_shapes=bufs(NCH, WIDE) + bufs(1, SMALLW) + sems(NCH) + sems(1),
        compiler_params=pltpu.CompilerParams(
            collective_id=1, has_side_effects=True, vmem_limit_bytes=60 * 1024 * 1024
        ),
        name="reduce_gradients",
    )(
        g_qkv.reshape(8, 128, 3 * WIDE),
        g_o.reshape(8, 128, WIDE),
        g_up.reshape(8, 128, 4 * WIDE),
        g_down.reshape(8, 4, 128, WIDE),
        g_small,
    )


def on_device(
    x_in,
    cotangent,
    ln1_gain,
    ln1_bias,
    w_qkv,
    q_bias,
    v_bias,
    w_attn_out,
    out_bias,
    ln2_gain,
    ln2_bias,
    w_up,
    up_bias,
    w_down,
    down_bias,
):
    small = jnp.concatenate(
        [ln1_gain, ln1_bias, q_bias, v_bias, out_bias, ln2_gain, ln2_bias, down_bias, up_bias]
    ).reshape(12, 128)
    small = jnp.pad(small, ((0, 116), (0, 0)))
    wq, wo, wu, wd, sm = gather_all(small, w_qkv, w_attn_out, w_up, w_down)
    vec = [sm[:, i, :].reshape(-1) for i in range(8)]
    params = (
        vec[0],
        vec[1],
        wq,
        vec[2],
        vec[3],
        wo,
        vec[4],
        vec[5],
        vec[6],
        wu,
        sm[:, 8:12, :].reshape(-1),
        wd,
        vec[7],
    )
    block_out, saved_state = layer_forward(x_in, params)
    layer_input_grad, grads = layer_backward(cotangent, saved_state, params)
    order = (0, 1, 3, 4, 6, 7, 8, 12)
    packed = jnp.concatenate(
        [grads[i].reshape(8, 1, 128) for i in order] + [grads[10].reshape(8, 4, 128)], axis=1
    ).astype(BF16)
    packed = jnp.pad(packed.reshape(8, 6, 256), ((0, 0), (0, 122), (0, 0)))
    big, sml = reduce_all(
        grads[2].astype(BF16), grads[5].astype(BF16), grads[9].astype(BF16), grads[11].astype(BF16), packed
    )
    big = big.astype(F32) / 128.0
    vals = sml[0, :6].reshape(12, 128).astype(F32) / 128.0
    return (
        block_out,
        layer_input_grad,
        vals[0],
        vals[1],
        jnp.concatenate([big[9], big[10], big[11]], axis=1),
        vals[2],
        vals[3],
        big[8],
        vals[4],
        vals[5],
        vals[6],
        jnp.concatenate([big[4], big[5], big[6], big[7]], axis=1),
        vals[8:12].reshape(-1),
        big[0:4].reshape(512, WIDE),
        vals[7],
    )


def solution(mesh):
    placed = (
        P(("rep", "shard"), None),
        P(("rep", "shard"), None),
        P("shard"),
        P("shard"),
        P("shard", None),
        P("shard"),
        P("shard"),
        P("shard", None),
        P("shard"),
        P("shard"),
        P("shard"),
        P("shard", None),
        P("shard"),
        P("shard", None),
        P("shard"),
    )
    return jax.shard_map(
        on_device,
        mesh=mesh,
        in_specs=placed,
        out_specs=(
            P(("rep", "shard"), None),
            P(("rep", "shard"), None),
            P("shard"),
            P("shard"),
            P("shard", None),
            P("shard"),
            P("shard"),
            P("shard", None),
            P("shard"),
            P("shard"),
            P("shard"),
            P("shard", None),
            P("shard"),
            P("shard", None),
            P("shard"),
        ),
        check_vma=False,
    )
```

```python
import math

import jax
import jax.numpy as jnp
from jax import lax
from jax.experimental import pallas as pl
from jax.experimental.pallas import tpu as pltpu
from jax.sharding import PartitionSpec as P

HEADS = 16
HEAD_DIM = 64
SEQ = 320
D = 1024
NCH = 12
MESH = pl.DeviceIdType.MESH
BF16 = jnp.bfloat16
F32 = jnp.float32
MIB = 1024 * 1024

eps_norm = 1e-05
sqrt_two_pi = math.sqrt(2.0 / math.pi)
cubic_coef = 0.044715

LN1G, LN1B, QB, VB, OB, LN2G, LN2B, DB, UB = 0, 1, 2, 3, 4, 5, 6, 7, 8
WQ, WK, WV, WO, WUP, WDN = 0, 1, 2, 3, 4, 8


def place():
    rep = lax.axis_index("rep")
    shard = lax.axis_index("shard")
    x, lo, core = rep // 4, (rep // 2) % 2, rep % 2
    hi, z = shard // 4, shard % 4

    def dev(x_, lo_, core_, hi_, z_):
        return ((x_ * 2 + lo_) * 2 + core_, hi_ * 4 + z_)

    peers = dict(
        xr=dev((x + 1) % 4, lo, core, hi, z),
        xl=dev((x + 3) % 4, lo, core, hi, z),
        xo=dev((x + 2) % 4, lo, core, hi, z),
        zr=dev(x, lo, core, hi, (z + 1) % 4),
        zl=dev(x, lo, core, hi, (z + 3) % 4),
        zo=dev(x, lo, core, hi, (z + 2) % 4),
        cross=dev(x, 1 - lo, core, 1 - hi, z),
        ylo=dev(x, 1 - lo, core, hi, z),
        yo=dev(x, lo, core, 1 - hi, z),
        core=dev(x, lo, 1 - core, hi, z),
    )
    return x, core, hi, z, peers


def greet(peers, names):
    barrier = pltpu.get_barrier_semaphore()
    for name in names:
        pl.semaphore_signal(barrier, inc=1, device_id=peers[name], device_id_type=MESH)
    pl.semaphore_wait(barrier, len(names))


def loop(n, body):
    def step(i, carry):
        body(i)
        return carry

    lax.fori_loop(0, n, step, 0)


def rows_of(i, n):
    return pl.ds(pl.multiple_of(i * n, n), n)


def nn(a, b):
    return jnp.dot(a, b, preferred_element_type=F32)


def nt(a, b):
    return lax.dot_general(a, b, (((1,), (1,)), ((), ())), preferred_element_type=F32)


def tn(a, b):
    return lax.dot_general(a, b, (((0,), (0,)), ((), ())), preferred_element_type=F32)


def slope_of(h):
    return 2.0 ** (-8.0 * (h + 1) / HEADS)


def gelu_both(u):
    tanh_val = jnp.tanh(sqrt_two_pi * (u + cubic_coef * u * u * u))
    value = 0.5 * u * (1.0 + tanh_val)
    slope = 0.5 * (1.0 + tanh_val) + 0.5 * u * (1.0 - tanh_val * tanh_val) * sqrt_two_pi * (
        1.0 + 3.0 * cubic_coef * u * u
    )
    return value, slope


def center_scale(rows):
    c = rows - jnp.mean(rows, axis=-1, keepdims=True)
    s = lax.rsqrt(jnp.mean(c * c, axis=-1, keepdims=True) + eps_norm)
    return c * s, s


def gelu_value(up_projected):
    inner = sqrt_two_pi * (up_projected + cubic_coef * up_projected * up_projected * up_projected)
    return 0.5 * up_projected * (1.0 + jnp.tanh(inner))


def gelu_slope(up_projected):
    tanh_val = jnp.tanh(
        sqrt_two_pi * (up_projected + cubic_coef * up_projected * up_projected * up_projected)
    )
    return 0.5 * (1.0 + tanh_val) + 0.5 * up_projected * (
        1.0 - tanh_val * tanh_val
    ) * sqrt_two_pi * (1.0 + 3.0 * cubic_coef * up_projected * up_projected)


def layer_normalize(rows_in, gain_vec, bias_vec):
    center = rows_in - jnp.mean(rows_in, axis=-1, keepdims=True)
    inv_std = lax.rsqrt(jnp.mean(center * center, axis=-1, keepdims=True) + eps_norm)
    x_hat = center * inv_std
    return (x_hat * gain_vec.astype(jnp.float32) + bias_vec.astype(jnp.float32), x_hat, inv_std)


def layer_normalize_backward(d_normed, x_hat, inv_std):
    return inv_std * (
        d_normed
        - jnp.mean(d_normed, axis=-1, keepdims=True)
        - x_hat * jnp.mean(d_normed * x_hat, axis=-1, keepdims=True)
    )


def split_heads(rows_in):
    return rows_in.reshape(rows_in.shape[0] // SEQ, SEQ, HEADS, HEAD_DIM)


def merge_heads(heads_in):
    return heads_in.reshape(-1, HEADS * HEAD_DIM)


def alibi_bias():
    positions = jnp.arange(SEQ)
    distance = (positions[:, None] - positions[None, :]).astype(jnp.float32)
    head_ids = jnp.arange(HEADS).astype(jnp.float32)
    slopes = jnp.exp2(-8.0 * (head_ids + 1.0) / HEADS)
    offsets = -slopes[:, None, None] * distance[None, :, :]
    return jnp.where(distance[None, :, :] >= 0.0, offsets, -jnp.inf)


def attn_scores(query_heads, key_heads):
    scores = jnp.einsum(
        "bqhd,bkhd->bhqk", query_heads, key_heads, preferred_element_type=jnp.float32
    )
    return scores * HEAD_DIM ** (-0.5) + alibi_bias()[None]


def layer_backward(cotangent, saved_state, params):
    (
        first_norm_gain,
        first_norm_bias,
        w_qkv,
        q_bias,
        v_bias,
        w_attn_out,
        out_bias,
        second_norm_gain,
        second_norm_bias,
        w_up,
        up_bias,
        w_down,
        down_bias,
    ) = params
    (
        first_centered_scaled,
        first_inverse_scale,
        first_activation,
        query_block,
        key_block,
        value_block,
        log_normalizer,
        attended_context,
        second_centered_scaled,
        second_inverse_scale,
        second_activation,
        up_projected,
        hidden_activations,
    ) = saved_state
    cot_b = cotangent.astype(jnp.bfloat16)
    g_down_bias = jnp.sum(cotangent, axis=0)
    g_w_down = jnp.dot(hidden_activations.T, cot_b, preferred_element_type=jnp.float32)
    d_up = jnp.dot(cot_b, w_down.T, preferred_element_type=jnp.float32) * up_projected
    g_up_bias = jnp.sum(d_up, axis=0)
    d_up_b = d_up.astype(jnp.bfloat16)
    g_w_up = jnp.dot(second_activation.T, d_up_b, preferred_element_type=jnp.float32)
    second_activation_grad = jnp.dot(d_up_b, w_up.T, preferred_element_type=jnp.float32)
    second_gain_grad = jnp.sum(second_activation_grad * second_centered_scaled, axis=0)
    g_bias_two = jnp.sum(second_activation_grad, axis=0)
    middle_residual_grad = cotangent + layer_normalize_backward(
        second_activation_grad * second_norm_gain.astype(jnp.float32),
        second_centered_scaled,
        second_inverse_scale,
    )
    g_out_bias = jnp.sum(middle_residual_grad, axis=0)
    d_mid_b = middle_residual_grad.astype(jnp.bfloat16)
    g_w_attn_out = jnp.dot(attended_context.T, d_mid_b, preferred_element_type=jnp.float32)
    d_context = jnp.dot(d_mid_b, w_attn_out.T, preferred_element_type=jnp.float32).astype(
        jnp.bfloat16
    )
    query_heads = split_heads(query_block)
    key_heads = split_heads(key_block)
    scores = attn_scores(query_heads, key_heads)
    probab = jnp.exp(scores - log_normalizer)
    probab_b = probab.astype(jnp.bfloat16)
    ctx_heads = split_heads(d_context)
    d_value = merge_heads(
        jnp.einsum("bhqk,bqhd->bkhd", probab_b, ctx_heads, preferred_element_type=jnp.float32)
    )
    d_prob = jnp.einsum(
        "bqhd,bkhd->bhqk", ctx_heads, split_heads(value_block), preferred_element_type=jnp.float32
    )
    d_score = probab * (d_prob - jnp.sum(probab * d_prob, axis=-1, keepdims=True))
    d_score_b = d_score.astype(jnp.bfloat16)
    d_query = merge_heads(
        jnp.einsum("bhqk,bkhd->bqhd", d_score_b, key_heads, preferred_element_type=jnp.float32)
    ) * HEAD_DIM ** (-0.5)
    d_key = merge_heads(
        jnp.einsum("bhqk,bqhd->bkhd", d_score_b, query_heads, preferred_element_type=jnp.float32)
    ) * HEAD_DIM ** (-0.5)
    g_q_bias = jnp.sum(d_query, axis=0)
    g_v_bias = jnp.sum(d_value, axis=0)
    d_united = jnp.concatenate([d_query, d_key, d_value], axis=1).astype(jnp.bfloat16)
    g_w_qkv = jnp.dot(first_activation.T, d_united, preferred_element_type=jnp.float32)
    first_activation_grad = jnp.dot(d_united, w_qkv.T, preferred_element_type=jnp.float32)
    first_gain_grad = jnp.sum(first_activation_grad * first_centered_scaled, axis=0)
    g_bias_one = jnp.sum(first_activation_grad, axis=0)
    layer_input_grad = middle_residual_grad + layer_normalize_backward(
        first_activation_grad * first_norm_gain.astype(jnp.float32),
        first_centered_scaled,
        first_inverse_scale,
    )
    grads = (
        first_gain_grad,
        g_bias_one,
        g_w_qkv,
        g_q_bias,
        g_v_bias,
        g_w_attn_out,
        g_out_bias,
        second_gain_grad,
        g_bias_two,
        g_w_up,
        g_up_bias,
        g_w_down,
        g_down_bias,
    )
    return (layer_input_grad, grads)


GCOPIES = 20


def forward_kernel(*refs):
    w_qkv, w_o, w_up, w_down, small, x_in = refs[:6]
    full_out, sm_all, block_out, act1, q, k_, v, lse, ctx, act2, n2, hid, slope = refs[6:19]
    full, mid, dist, vecs, tmp = refs[19:24]
    send_sem, recv_sem, own_sem, out_sem, sm_send, sm_recv = refs[24:]
    x, core, hi, z, peers = place()
    other = 1 - hi
    me = hi * 4 + z
    left, right, far = hi * 4 + (z + 3) % 4, hi * 4 + (z + 1) % 4, hi * 4 + (z + 2) % 4
    qkv_out = (q, k_, v)

    for c in range(3):
        pltpu.make_async_copy(
            w_qkv.at[:, pl.ds(c * D, D)], full.at[WQ + c, me], own_sem.at[WQ + c]
        ).start()
    pltpu.make_async_copy(w_o, full.at[WO, me], own_sem.at[WO]).start()
    sm_all[me] = small[...]
    greet(peers, ("xr", "xl", "zr", "zl", "cross", "core"))

    started = []

    def push(src, dst, ss, rs, to):
        cp = pltpu.make_async_remote_copy(
            src_ref=src,
            dst_ref=dst,
            send_sem=ss,
            recv_sem=rs,
            device_id=peers[to],
            device_id_type=MESH,
        )
        cp.start()
        started.append(cp)
        return cp

    by_chunk = [dict() for _ in range(NCH)]

    def send(k, name, view, to):
        slot = len(by_chunk[k])
        by_chunk[k][name] = push(view, view, send_sem.at[k, slot], recv_sem.at[k, slot], to)

    def part(k, which, first, count):
        return full.at[k, which, pl.ds(pl.multiple_of(first, 16), count)]

    base, quarter = core * 64, core * 64 + x * 16
    others = pl.ds(other * 4, 4)

    def stage0(k):
        pltpu.make_async_copy(full.at[k, me], full.at[k, me], own_sem.at[k]).wait()
        send(k, "z1r", part(k, me, base, 64), "zr")
        send(k, "z1l", part(k, me, base, 64), "zl")
        send(k, "y0", part(k, me, quarter, 16), "cross")

    def stage1(k):
        by_chunk[k]["z1r"].wait_recv()
        send(k, "z2r", part(k, left, base, 32), "zr")
        send(k, "y1", part(k, left, quarter, 16), "cross")
        send(k, "c1", part(k, left, base, 64), "core")
        by_chunk[k]["z1l"].wait_recv()
        send(k, "z2l", part(k, right, base + 32, 32), "zl")
        send(k, "y2", part(k, right, quarter, 16), "cross")
        send(k, "c2", part(k, right, base, 64), "core")

    def stage2(k):
        by_chunk[k]["z2r"].wait_recv()
        by_chunk[k]["z2l"].wait_recv()
        send(k, "y3", part(k, far, quarter, 16), "cross")
        send(k, "c3", part(k, far, base, 64), "core")

    def stage3(k):
        for name in ("y0", "y1", "y2", "y3"):
            by_chunk[k][name].wait_recv()
        view = part(k, others, quarter, 16)
        send(k, "x1r", view, "xr")
        send(k, "x1l", view, "xl")
        send(k, "c4", view, "core")

    def stage4(k):
        for name, from_x, nxt, first, to in (
            ("x1r", (x + 3) % 4, "x2r", 0, "xr"),
            ("x1l", (x + 1) % 4, "x2l", 2, "xl"),
        ):
            by_chunk[k][name].wait_recv()
            send(k, nxt, part(k, pl.ds(other * 4 + first, 2), base + from_x * 16, 16), to)
            send(k, "c" + nxt, part(k, others, base + from_x * 16, 16), "core")

    def stage5(k):
        by_chunk[k]["x2r"].wait_recv()
        by_chunk[k]["x2l"].wait_recv()
        send(k, "c7", part(k, others, base + ((x + 2) % 4) * 16, 16), "core")

    def keep(k):
        return pltpu.make_async_copy(full.at[k], full_out.at[k], out_sem.at[k])

    def stage6(k):
        for name, cp in by_chunk[k].items():
            if name[0] == "c":
                cp.wait_recv()
        keep(k).start()

    stages = (None, stage1, stage2, stage3, stage4, stage5, stage6)

    sm_copies = []

    def sm_step(i):
        def sm(name_slot, view, to):
            sm_copies.append(push(view, view, sm_send.at[name_slot], sm_recv.at[name_slot], to))

        if i == 0:
            sm(0, sm_all.at[me], "zr")
            sm(1, sm_all.at[me], "zl")
        elif i == 1:
            sm_copies[0].wait_recv()
            sm_copies[1].wait_recv()
            sm(2, sm_all.at[left], "zr")
        elif i == 2:
            sm_copies[2].wait_recv()
            sm(3, sm_all.at[pl.ds(hi * 4, 4)], "cross")
        else:
            sm_copies[3].wait_recv()
            for s in range(8):
                vecs[:, pl.ds(s * 128, 128)] = sm_all[s].astype(F32)

    def comm(t):
        for s in range(6, 0, -1):
            if 0 <= t - s < NCH:
                stages[s](t - s)
        if t + 2 < NCH:
            stage0(t + 2)

    def vec(i):
        return vecs[i : i + 1, :]

    def norm_one():
        def body(i):
            r = rows_of(i, 32)
            n, s = center_scale(x_in[r, :].astype(F32))
            act1[r, :] = (n * vec(LN1G) + vec(LN1B)).astype(BF16)

        loop(10, body)
        row = lax.broadcasted_iota(jnp.int32, (SEQ, SEQ), 0)
        col = lax.broadcasted_iota(jnp.int32, (SEQ, SEQ), 1)
        dist[...] = (row - col).astype(F32)

    def matmul(a_ref, k, write):
        def body(i):
            cols = rows_of(i, 256)
            w = full[k, :, :, cols].reshape(D, 256)
            write(i, cols, nn(a_ref[...], w))

        loop(4, body)

    def project(c):
        def write(i, cols, res):
            if c == 0:
                res = res + vecs[QB : QB + 1, cols]
            if c == 2:
                res = res + vecs[VB : VB + 1, cols]
            qkv_out[c][:, cols] = res.astype(BF16)

        matmul(act1, WQ + c, write)

    def attend(p):
        cols = pl.ds(p * 128, 128)
        lane = lax.broadcasted_iota(jnp.int32, (SEQ, 128), 1)
        q_pair, k_pair, v_pair = q[:, cols], k_[:, cols], v[:, cols]
        out = []
        lse_all = lse[...] if p else jnp.zeros((SEQ, 128), F32)
        for e in range(2):
            h = 2 * p + e
            mine = (lane < 64) if e == 0 else (lane >= 64)
            s = nt(jnp.where(mine, q_pair, jnp.zeros_like(q_pair)), k_pair)
            d = dist[...]
            s = jnp.where(d >= 0.0, s * HEAD_DIM**-0.5 - slope_of(h) * d, -jnp.inf)
            top = jnp.max(s, axis=-1, keepdims=True)
            s = jnp.exp(s - top)
            total = jnp.sum(s, axis=-1, keepdims=True)
            lse_all = jnp.where(lane == h, top + jnp.log(total), lse_all)
            out.append(nn((s / total).astype(BF16), v_pair))
        lse[...] = lse_all
        ctx[:, cols] = jnp.where(lane < 64, out[0], out[1]).astype(BF16)

    def out_proj():
        def write(i, cols, res):
            mid[:, cols] = res + vecs[OB : OB + 1, cols] + x_in[:, cols].astype(F32)

        matmul(ctx, WO, write)

        def body(i):
            r = rows_of(i, 32)
            n, s = center_scale(mid[r, :])
            n2[r, pl.ds(0, D)] = n
            n2[r, pl.ds(D, 128)] = jnp.broadcast_to(s, (32, 128))
            act2[r, :] = (n * vec(LN2G) + vec(LN2B)).astype(BF16)

        loop(10, body)

    def up(j):
        def write(i, cols, res):
            tmp[:, cols] = res + vecs[UB + j : UB + j + 1, cols]

        matmul(act2, WUP + j, write)

        def body(i):
            r = rows_of(i, 16)
            value, grad = gelu_both(tmp[r, :])
            hid[j, r, :] = value.astype(BF16)
            slope[j, r, :] = grad

        loop(20, body)

    def down(j):
        def write(i, cols, res):
            base_val = mid[:, cols]
            if j == 0:
                base_val = base_val + vecs[DB : DB + 1, cols]
            res = res + base_val
            if j < 3:
                mid[:, cols] = res
            else:
                block_out[:, cols] = res.astype(BF16)

        matmul(hid.at[j], WDN + j, write)

    plan = {t: [] for t in range(40)}
    plan[4].append(norm_one)
    for c in range(3):
        plan[6 + c].append(lambda c=c: project(c))
    for p in range(8):
        plan[8 + (p + 1) // 3].append(lambda p=p: attend(p))
    plan[11].append(out_proj)
    for j in range(4):
        plan[max(11, 10 + j)].append(lambda j=j: up(j))
        plan[14 + j].append(lambda j=j: down(j))

    sm_step(0)
    stage0(0)
    stage0(1)
    for j in range(4):
        for s in range(8):
            pltpu.make_async_copy(
                w_up.at[:, pl.ds(s * 512 + j * 128, 128)],
                full.at[WUP + j, me, :, pl.ds(s * 128, 128)],
                own_sem.at[WUP + j],
            ).start()
        pltpu.make_async_copy(
            w_down.at[pl.ds(j * 128, 128)], full.at[WDN + j, me], own_sem.at[WDN + j]
        ).start()
    stage0(2)
    for t in range(1, 18):
        if t < 4:
            sm_step(t)
        comm(t)
        for piece in plan[t]:
            piece()
    for cp in started:
        cp.wait_send()
    for k in range(NCH):
        keep(k).wait()


def gather_forward(w_qkv, w_attn_out, w_up, w_down, small, x_in):
    vm = pl.BlockSpec(memory_space=pltpu.VMEM)
    hbm = pl.BlockSpec(memory_space=pl.ANY)
    S = jax.ShapeDtypeStruct
    act = S((SEQ, D), BF16)
    return pl.pallas_call(
        forward_kernel,
        out_shape=[
            S((NCH, 8, 128, D), BF16),
            S((8, 16, 128), BF16),
            act,
            act,
            act,
            act,
            act,
            S((SEQ, 128), F32),
            act,
            act,
            S((SEQ, D + 128), F32),
            S((4, SEQ, D), BF16),
            S((4, SEQ, D), F32),
        ],
        in_specs=[hbm] * 4 + [vm] * 2,
        out_specs=[hbm] + [vm] * 12,
        scratch_shapes=[
            pltpu.VMEM((NCH, 8, 128, D), BF16),
            pltpu.VMEM((SEQ, D), F32),
            pltpu.VMEM((SEQ, SEQ), F32),
            pltpu.VMEM((16, D), F32),
            pltpu.VMEM((SEQ, D), F32),
            pltpu.SemaphoreType.DMA((NCH, GCOPIES)),
            pltpu.SemaphoreType.DMA((NCH, GCOPIES)),
            pltpu.SemaphoreType.DMA((NCH,)),
            pltpu.SemaphoreType.DMA((NCH,)),
            pltpu.SemaphoreType.DMA((4,)),
            pltpu.SemaphoreType.DMA((4,)),
        ],
        compiler_params=pltpu.CompilerParams(
            collective_id=0, has_side_effects=True, vmem_limit_bytes=56 * MIB
        ),
        name="gather_forward",
    )(w_qkv, w_attn_out, w_up, w_down, small, x_in)


WIDE = 1024
SMALLW = 256
RCOPIES = 24


def reduce_kernel(*refs):
    g_qkv, g_o, g_up, g_down, g_small = refs[:5]
    fin_big, fin_small = refs[5:7]
    scr = refs[7:]
    nb = 9
    big, small = scr[:nb], scr[nb : 2 * nb]
    b_send, b_recv, b_own, s_send, s_recv, s_own = scr[2 * nb :]
    x, core, hi, z, peers = place()
    other = 1 - hi
    greet(peers, ("xr", "xl", "zr", "zl", "cross", "ylo", "core"))
    xp, xm, xo = (x + 1) % 4, (x + 3) % 4, (x + 2) % 4
    zp, zm, zo = (z + 1) % 4, (z + 3) % 4, (z + 2) % 4

    def sub(i):
        return pl.ds(pl.multiple_of(i * 16, 16), 16)

    def add(ref, idx, *others):
        total = ref[idx].astype(F32)
        for o_ref, o_idx in others:
            total = total + o_ref[o_idx].astype(F32)
        ref[idx] = total.astype(BF16)

    def build(bufs, fin, send_sem, recv_sem, own_sem, wide):
        acc, rc, rx1, rx2, ry, rz1, rz2, rf1, rf2 = bufs
        hw = wide // 2
        cols_a, cols_b = pl.ds(0, hw), pl.ds(hw, hw)

        def copy(k, slot, src, dst, to):
            return pltpu.make_async_remote_copy(
                src_ref=src,
                dst_ref=dst,
                send_sem=send_sem.at[k, slot],
                recv_sem=recv_sem.at[k, slot],
                device_id=peers[to],
                device_id_type=MESH,
            )

        def rows_of(i):
            return pl.ds(pl.multiple_of(core * 64 + i * 16, 16), 16)

        def x1(k):
            return (
                copy(k, 1, acc.at[k, pl.ds(other * 4, 2), sub(xo)], rx1.at[k, 0], "xr"),
                copy(k, 2, acc.at[k, pl.ds(other * 4 + 2, 2), sub(xo)], rx1.at[k, 1], "xl"),
            )

        def x2(k):
            return (
                copy(k, 3, acc.at[k, pl.ds(other * 4, 4), sub(xp)], rx2.at[k, 0], "xr"),
                copy(k, 4, acc.at[k, pl.ds(other * 4, 4), sub(xm)], rx2.at[k, 1], "xl"),
            )

        def y1(k):
            return (copy(k, 5, acc.at[k, pl.ds(other * 4, 4), sub(x)], ry.at[k], "cross"),)

        def z1(k):
            return (
                copy(k, 6, acc.at[k, hi * 4 + zo, pl.ds(0, 32)], rz1.at[k, 0], "zr"),
                copy(k, 7, acc.at[k, hi * 4 + zo, pl.ds(32, 32)], rz1.at[k, 1], "zl"),
            )

        def z2(k):
            return (
                copy(k, 8, acc.at[k, hi * 4 + zp], rz2.at[k, 0], "zr"),
                copy(k, 9, acc.at[k, hi * 4 + zm], rz2.at[k, 1], "zl"),
            )

        me = hi * 4 + z

        def f1(k):
            return (
                copy(k, 10, acc.at[k, me, sub(xo), cols_a], rf1.at[k, 0], "xr"),
                copy(k, 11, acc.at[k, me, sub(xo), cols_b], rf1.at[k, 1], "xl"),
            )

        def f2(k):
            return (
                copy(k, 12, acc.at[k, me, sub(xp)], rf2.at[k, 0], "xr"),
                copy(k, 13, acc.at[k, me, sub(xm)], rf2.at[k, 1], "xl"),
            )

        def fy(k):
            return (copy(k, 14, acc.at[k, me, sub(x)], rf2.at[k, 2], "ylo"),)

        def g1(k):
            view = fin.at[k, rows_of(x)]
            return (
                copy(k, 15, view, view, "xr"),
                copy(k, 16, view, view, "xl"),
                copy(k, 17, view, view, "core"),
            )

        def g2(k):
            va, vb = fin.at[k, rows_of(xm), cols_a], fin.at[k, rows_of(xp), cols_b]
            ca, cb = fin.at[k, rows_of(xm)], fin.at[k, rows_of(xp)]
            return (
                copy(k, 18, va, va, "xr"),
                copy(k, 19, vb, vb, "xl"),
                copy(k, 20, ca, ca, "core"),
                copy(k, 21, cb, cb, "core"),
            )

        def g3(k):
            view = fin.at[k, rows_of(xo)]
            return (copy(k, 22, view, view, "core"),)

        def go(copies):
            for cp in copies:
                cp.start()

        def got(copies):
            for cp in copies:
                cp.wait_recv()

        def s0(k):
            copy(k, 0, rc.at[k], rc.at[k], "core").wait_recv()
            pltpu.make_async_copy(acc.at[k], acc.at[k], own_sem.at[k]).wait()

            def body(i, carry):
                add(acc, (k, i), (rc, (k, i)))
                return carry

            lax.fori_loop(0, 8, body, 0)
            go(x1(k))

        def s1(k):
            got(x1(k))
            add(acc, (k, pl.ds(other * 4, 2), sub(xp)), (rx1, (k, 0)))
            add(acc, (k, pl.ds(other * 4 + 2, 2), sub(xm)), (rx1, (k, 1)))
            go(x2(k))

        def s2(k):
            got(x2(k))
            add(acc, (k, pl.ds(other * 4, 4), sub(x)), (rx2, (k, 0)), (rx2, (k, 1)))
            go(y1(k))

        def s3(k):
            got(y1(k))
            add(acc, (k, pl.ds(hi * 4, 4), sub(x)), (ry, (k,)))
            go(z1(k))

        def s4(k):
            got(z1(k))
            add(acc, (k, hi * 4 + zp, pl.ds(0, 32)), (rz1, (k, 0)))
            add(acc, (k, hi * 4 + zm, pl.ds(32, 32)), (rz1, (k, 1)))
            go(z2(k))

        def s5(k):
            got(z2(k))
            add(acc, (k, me), (rz2, (k, 0)), (rz2, (k, 1)))
            go(f1(k))

        def s6(k):
            got(f1(k))
            add(acc, (k, me, sub(xp), cols_a), (rf1, (k, 0)))
            add(acc, (k, me, sub(xm), cols_b), (rf1, (k, 1)))
            go(f2(k))

        def s7(k):
            got(f2(k))
            add(acc, (k, me, sub(x)), (rf2, (k, 0)), (rf2, (k, 1)))
            go(fy(k))

        def s8(k):
            got(fy(k))
            total = acc[k, me, sub(x)].astype(F32) + rf2[k, 2].astype(F32)
            fin[k, rows_of(x)] = total.astype(BF16)
            go(g1(k))

        def s9(k):
            a, b, c = g1(k)
            got((a, b))
            go(g2(k))

        def s10(k):
            got(g2(k)[:2])
            go(g3(k))

        def s11(k):
            got(g1(k)[2:])
            got(g2(k)[2:])
            got(g3(k))

        def done(k):
            copy(k, 0, rc.at[k], rc.at[k], "core").wait_send()
            for f in (x1, x2, y1, z1, z2, f1, f2, fy, g1, g2, g3):
                for cp in f(k):
                    cp.wait_send()

        return copy, (s0, s1, s2, s3, s4, s5, s6, s7, s8, s9, s10, s11), done

    b_copy, b_stages, b_done = build(big, fin_big, b_send, b_recv, b_own, WIDE)
    s_copy, s_stages, s_done = build(small, fin_small, s_send, s_recv, s_own, SMALLW)

    theirs = pl.ds(pl.multiple_of((1 - core) * 64, 16), 64)
    mine = pl.ds(pl.multiple_of(core * 64, 16), 64)

    def source(k, rows):
        if k < 4:
            return g_down.at[:, k, rows]
        if k < 8:
            return g_up.at[:, rows, pl.ds((k - 4) * WIDE, WIDE)]
        if k < 9:
            return g_o.at[:, rows]
        return g_qkv.at[:, rows, pl.ds((k - 9) * WIDE, WIDE)]

    for k in range(NCH):
        b_copy(k, 0, source(k, theirs), big[1].at[k], "core").start()
        pltpu.make_async_copy(source(k, mine), big[0].at[k], b_own.at[k]).start()
    s_copy(0, 0, g_small.at[:, theirs], small[1].at[0], "core").start()
    pltpu.make_async_copy(g_small.at[:, mine], small[0].at[0], s_own.at[0]).start()

    depth = len(b_stages)

    def step(t, carry):
        for s in range(depth - 1, -1, -1):
            k = t - s

            @pl.when((k >= 0) & (k < NCH))
            def _():
                b_stages[s](k)

        return carry

    lax.fori_loop(0, NCH + depth - 1, step, 0)
    for s in range(depth):
        s_stages[s](0)

    def finish(k, carry):
        b_done(k)
        return carry

    lax.fori_loop(0, NCH, finish, 0)
    s_done(0)


def reduce_all(g_qkv, g_o, g_up, g_down, g_small):
    def bufs(n, wide):
        return [
            pltpu.VMEM((n, 8, 64, wide), BF16),
            pltpu.VMEM((n, 8, 64, wide), BF16),
            pltpu.VMEM((n, 2, 2, 16, wide), BF16),
            pltpu.VMEM((n, 2, 4, 16, wide), BF16),
            pltpu.VMEM((n, 4, 16, wide), BF16),
            pltpu.VMEM((n, 2, 32, wide), BF16),
            pltpu.VMEM((n, 2, 64, wide), BF16),
            pltpu.VMEM((n, 2, 16, wide // 2), BF16),
            pltpu.VMEM((n, 3, 16, wide), BF16),
        ]

    def sems(n):
        return [
            pltpu.SemaphoreType.DMA((n, RCOPIES)),
            pltpu.SemaphoreType.DMA((n, RCOPIES)),
            pltpu.SemaphoreType.DMA((n,)),
        ]

    return pl.pallas_call(
        reduce_kernel,
        out_shape=[
            jax.ShapeDtypeStruct((NCH, 128, WIDE), BF16),
            jax.ShapeDtypeStruct((1, 128, SMALLW), BF16),
        ],
        in_specs=[pl.BlockSpec(memory_space=pl.ANY)] * 5,
        out_specs=[pl.BlockSpec(memory_space=pltpu.VMEM)] * 2,
        scratch_shapes=bufs(NCH, WIDE) + bufs(1, SMALLW) + sems(NCH) + sems(1),
        compiler_params=pltpu.CompilerParams(
            collective_id=1, has_side_effects=True, vmem_limit_bytes=60 * 1024 * 1024
        ),
        name="reduce_gradients",
    )(
        g_qkv.reshape(8, 128, 3 * WIDE),
        g_o.reshape(8, 128, WIDE),
        g_up.reshape(8, 128, 4 * WIDE),
        g_down.reshape(8, 4, 128, WIDE),
        g_small,
    )


def on_device(
    x_in,
    cotangent,
    ln1_gain,
    ln1_bias,
    w_qkv,
    q_bias,
    v_bias,
    w_attn_out,
    out_bias,
    ln2_gain,
    ln2_bias,
    w_up,
    up_bias,
    w_down,
    down_bias,
):
    small = jnp.concatenate(
        [ln1_gain, ln1_bias, q_bias, v_bias, out_bias, ln2_gain, ln2_bias, down_bias, up_bias]
    ).reshape(12, 128)
    small = jnp.pad(small, ((0, 4), (0, 0)))
    full, sm, block_out, act1, q, k, v, lse, ctx, act2, n2, hid, slope = gather_forward(
        w_qkv, w_attn_out, w_up, w_down, small, x_in
    )
    full = full.reshape(12, 1024, 1024)
    vec = [sm[:, i, :].reshape(-1) for i in range(8)]
    wqkv = jnp.concatenate([full[0], full[1], full[2]], axis=1)
    wup = full[4:8].reshape(4, 1024, 8, 128).transpose(1, 2, 0, 3).reshape(1024, 4096)
    wdn = full[8:12].reshape(4, 8, 128, 1024).transpose(1, 0, 2, 3).reshape(4096, 1024)
    params = (vec[0], vec[1], wqkv, vec[2], vec[3], full[3], vec[4], vec[5], vec[6], wup,
              sm[:, 8:12, :].reshape(-1), wdn, vec[7])
    _, n1, s1 = layer_normalize(x_in.astype(F32), vec[0], vec[1])
    unj = lambda a: a.reshape(4, 320, 8, 128).transpose(1, 2, 0, 3).reshape(320, 4096)
    saved = (n1, s1, act1, q, k, v, lse[:, :16].T[None, :, :, None], ctx, n2[:, :1024], n2[:, 1024:1025], act2, unj(slope), unj(hid))
    layer_input_grad, grads = layer_backward(cotangent, saved, params)
    order = (0, 1, 3, 4, 6, 7, 8, 12)
    packed = jnp.concatenate(
        [grads[i].reshape(8, 1, 128) for i in order] + [grads[10].reshape(8, 4, 128)], axis=1
    ).astype(BF16)
    packed = jnp.pad(packed.reshape(8, 6, 256), ((0, 0), (0, 122), (0, 0)))
    big, sml = reduce_all(
        grads[2].astype(BF16), grads[5].astype(BF16), grads[9].astype(BF16), grads[11].astype(BF16), packed
    )
    big = big.astype(F32) / 128.0
    vals = sml[0, :6].reshape(12, 128).astype(F32) / 128.0
    return (
        block_out,
        layer_input_grad,
        vals[0],
        vals[1],
        jnp.concatenate([big[9], big[10], big[11]], axis=1),
        vals[2],
        vals[3],
        big[8],
        vals[4],
        vals[5],
        vals[6],
        jnp.concatenate([big[4], big[5], big[6], big[7]], axis=1),
        vals[8:12].reshape(-1),
        big[0:4].reshape(512, WIDE),
        vals[7],
    )


def solution(mesh):
    placed = (
        P(("rep", "shard"), None),
        P(("rep", "shard"), None),
        P("shard"),
        P("shard"),
        P("shard", None),
        P("shard"),
        P("shard"),
        P("shard", None),
        P("shard"),
        P("shard"),
        P("shard"),
        P("shard", None),
        P("shard"),
        P("shard", None),
        P("shard"),
    )
    return jax.shard_map(
        on_device,
        mesh=mesh,
        in_specs=placed,
        out_specs=(
            P(("rep", "shard"), None),
            P(("rep", "shard"), None),
            P("shard"),
            P("shard"),
            P("shard", None),
            P("shard"),
            P("shard"),
            P("shard", None),
            P("shard"),
            P("shard"),
            P("shard"),
            P("shard", None),
            P("shard"),
            P("shard", None),
            P("shard"),
        ),
        check_vma=False,
    )
```

```python
import math

import jax
import jax.numpy as jnp
from jax import lax
from jax.experimental import pallas as pl
from jax.experimental.pallas import tpu as pltpu
from jax.sharding import PartitionSpec as P

HEADS = 16
HEAD_DIM = 64
SEQ = 320
D = 1024
NCH = 12
MESH = pl.DeviceIdType.MESH
BF16 = jnp.bfloat16
F32 = jnp.float32
MIB = 1024 * 1024

eps_norm = 1e-05
sqrt_two_pi = math.sqrt(2.0 / math.pi)
cubic_coef = 0.044715

LN1G, LN1B, QB, VB, OB, LN2G, LN2B, DB, UB = 0, 1, 2, 3, 4, 5, 6, 7, 8
WQ, WK, WV, WO, WUP, WDN = 0, 1, 2, 3, 4, 8


def place():
    rep = lax.axis_index("rep")
    shard = lax.axis_index("shard")
    x, lo, core = rep // 4, (rep // 2) % 2, rep % 2
    hi, z = shard // 4, shard % 4

    def dev(x_, lo_, core_, hi_, z_):
        return ((x_ * 2 + lo_) * 2 + core_, hi_ * 4 + z_)

    peers = dict(
        xr=dev((x + 1) % 4, lo, core, hi, z),
        xl=dev((x + 3) % 4, lo, core, hi, z),
        xo=dev((x + 2) % 4, lo, core, hi, z),
        zr=dev(x, lo, core, hi, (z + 1) % 4),
        zl=dev(x, lo, core, hi, (z + 3) % 4),
        zo=dev(x, lo, core, hi, (z + 2) % 4),
        cross=dev(x, 1 - lo, core, 1 - hi, z),
        ylo=dev(x, 1 - lo, core, hi, z),
        yo=dev(x, lo, core, 1 - hi, z),
        core=dev(x, lo, 1 - core, hi, z),
    )
    return x, core, hi, z, peers


def greet(peers, names):
    barrier = pltpu.get_barrier_semaphore()
    for name in names:
        pl.semaphore_signal(barrier, inc=1, device_id=peers[name], device_id_type=MESH)
    pl.semaphore_wait(barrier, len(names))


def loop(n, body):
    def step(i, carry):
        body(i)
        return carry

    lax.fori_loop(0, n, step, 0)


def rows_of(i, n):
    return pl.ds(pl.multiple_of(i * n, n), n)


def nn(a, b):
    return jnp.dot(a, b, preferred_element_type=F32)


def nt(a, b):
    return lax.dot_general(a, b, (((1,), (1,)), ((), ())), preferred_element_type=F32)


def tn(a, b):
    return lax.dot_general(a, b, (((0,), (0,)), ((), ())), preferred_element_type=F32)


def slope_of(h):
    return 2.0 ** (-8.0 * (h + 1) / HEADS)


def gelu_both(u):
    tanh_val = jnp.tanh(sqrt_two_pi * (u + cubic_coef * u * u * u))
    value = 0.5 * u * (1.0 + tanh_val)
    slope = 0.5 * (1.0 + tanh_val) + 0.5 * u * (1.0 - tanh_val * tanh_val) * sqrt_two_pi * (
        1.0 + 3.0 * cubic_coef * u * u
    )
    return value, slope


def center_scale(rows):
    c = rows - jnp.mean(rows, axis=-1, keepdims=True)
    s = lax.rsqrt(jnp.mean(c * c, axis=-1, keepdims=True) + eps_norm)
    return c * s, s


GCOPIES = 20


def forward_kernel(*refs):
    w_qkv, w_o, w_up, w_down, small, x_in = refs[:6]
    full_out, sm_all, block_out, act1, q, k_, v, lse, ctx, act2, n2, hid, slope = refs[6:19]
    full, mid, dist, vecs, tmp = refs[19:24]
    send_sem, recv_sem, own_sem, out_sem, sm_send, sm_recv = refs[24:]
    x, core, hi, z, peers = place()
    other = 1 - hi
    me = hi * 4 + z
    left, right, far = hi * 4 + (z + 3) % 4, hi * 4 + (z + 1) % 4, hi * 4 + (z + 2) % 4
    qkv_out = (q, k_, v)

    for c in range(3):
        pltpu.make_async_copy(
            w_qkv.at[:, pl.ds(c * D, D)], full.at[WQ + c, me], own_sem.at[WQ + c]
        ).start()
    pltpu.make_async_copy(w_o, full.at[WO, me], own_sem.at[WO]).start()
    sm_all[me] = small[...]
    greet(peers, ("xr", "xl", "zr", "zl", "cross", "core"))

    started = []

    def push(src, dst, ss, rs, to):
        cp = pltpu.make_async_remote_copy(
            src_ref=src,
            dst_ref=dst,
            send_sem=ss,
            recv_sem=rs,
            device_id=peers[to],
            device_id_type=MESH,
        )
        cp.start()
        started.append(cp)
        return cp

    by_chunk = [dict() for _ in range(NCH)]

    def send(k, name, view, to):
        slot = len(by_chunk[k])
        by_chunk[k][name] = push(view, view, send_sem.at[k, slot], recv_sem.at[k, slot], to)

    def part(k, which, first, count):
        return full.at[k, which, pl.ds(pl.multiple_of(first, 16), count)]

    base, quarter = core * 64, core * 64 + x * 16
    others = pl.ds(other * 4, 4)

    def stage0(k):
        pltpu.make_async_copy(full.at[k, me], full.at[k, me], own_sem.at[k]).wait()
        send(k, "z1r", part(k, me, base, 64), "zr")
        send(k, "z1l", part(k, me, base, 64), "zl")
        send(k, "y0", part(k, me, quarter, 16), "cross")

    def stage1(k):
        by_chunk[k]["z1r"].wait_recv()
        send(k, "z2r", part(k, left, base, 32), "zr")
        send(k, "y1", part(k, left, quarter, 16), "cross")
        send(k, "c1", part(k, left, base, 64), "core")
        by_chunk[k]["z1l"].wait_recv()
        send(k, "z2l", part(k, right, base + 32, 32), "zl")
        send(k, "y2", part(k, right, quarter, 16), "cross")
        send(k, "c2", part(k, right, base, 64), "core")

    def stage2(k):
        by_chunk[k]["z2r"].wait_recv()
        by_chunk[k]["z2l"].wait_recv()
        send(k, "y3", part(k, far, quarter, 16), "cross")
        send(k, "c3", part(k, far, base, 64), "core")

    def stage3(k):
        for name in ("y0", "y1", "y2", "y3"):
            by_chunk[k][name].wait_recv()
        view = part(k, others, quarter, 16)
        send(k, "x1r", view, "xr")
        send(k, "x1l", view, "xl")
        send(k, "c4", view, "core")

    def stage4(k):
        for name, from_x, nxt, first, to in (
            ("x1r", (x + 3) % 4, "x2r", 0, "xr"),
            ("x1l", (x + 1) % 4, "x2l", 2, "xl"),
        ):
            by_chunk[k][name].wait_recv()
            send(k, nxt, part(k, pl.ds(other * 4 + first, 2), base + from_x * 16, 16), to)
            send(k, "c" + nxt, part(k, others, base + from_x * 16, 16), "core")

    def stage5(k):
        by_chunk[k]["x2r"].wait_recv()
        by_chunk[k]["x2l"].wait_recv()
        send(k, "c7", part(k, others, base + ((x + 2) % 4) * 16, 16), "core")

    def keep(k):
        return pltpu.make_async_copy(full.at[k], full_out.at[k], out_sem.at[k])

    def stage6(k):
        for name, cp in by_chunk[k].items():
            if name[0] == "c":
                cp.wait_recv()
        keep(k).start()

    stages = (None, stage1, stage2, stage3, stage4, stage5, stage6)

    sm_copies = []

    def sm_step(i):
        def sm(name_slot, view, to):
            sm_copies.append(push(view, view, sm_send.at[name_slot], sm_recv.at[name_slot], to))

        if i == 0:
            sm(0, sm_all.at[me], "zr")
            sm(1, sm_all.at[me], "zl")
        elif i == 1:
            sm_copies[0].wait_recv()
            sm_copies[1].wait_recv()
            sm(2, sm_all.at[left], "zr")
        elif i == 2:
            sm_copies[2].wait_recv()
            sm(3, sm_all.at[pl.ds(hi * 4, 4)], "cross")
        else:
            sm_copies[3].wait_recv()
            for s in range(8):
                vecs[:, pl.ds(s * 128, 128)] = sm_all[s].astype(F32)

    def comm(t):
        for s in range(6, 0, -1):
            if 0 <= t - s < NCH:
                stages[s](t - s)
        if t + 2 < NCH:
            stage0(t + 2)

    def vec(i):
        return vecs[i : i + 1, :]

    def norm_one():
        def body(i):
            r = rows_of(i, 32)
            n, s = center_scale(x_in[r, :].astype(F32))
            act1[r, :] = (n * vec(LN1G) + vec(LN1B)).astype(BF16)

        loop(10, body)
        row = lax.broadcasted_iota(jnp.int32, (SEQ, SEQ), 0)
        col = lax.broadcasted_iota(jnp.int32, (SEQ, SEQ), 1)
        dist[...] = (row - col).astype(F32)

    def matmul(a_ref, k, write):
        def body(i):
            cols = rows_of(i, 256)
            w = full[k, :, :, cols].reshape(D, 256)
            write(i, cols, nn(a_ref[...], w))

        loop(4, body)

    def project(c):
        def write(i, cols, res):
            if c == 0:
                res = res + vecs[QB : QB + 1, cols]
            if c == 2:
                res = res + vecs[VB : VB + 1, cols]
            qkv_out[c][:, cols] = res.astype(BF16)

        matmul(act1, WQ + c, write)

    def attend(p):
        cols = pl.ds(p * 128, 128)
        lane = lax.broadcasted_iota(jnp.int32, (SEQ, 128), 1)
        q_pair, k_pair, v_pair = q[:, cols], k_[:, cols], v[:, cols]
        out = []
        lse_all = lse[...] if p else jnp.zeros((SEQ, 128), F32)
        for e in range(2):
            h = 2 * p + e
            mine = (lane < 64) if e == 0 else (lane >= 64)
            s = nt(jnp.where(mine, q_pair, jnp.zeros_like(q_pair)), k_pair)
            d = dist[...]
            s = jnp.where(d >= 0.0, s * HEAD_DIM**-0.5 - slope_of(h) * d, -jnp.inf)
            top = jnp.max(s, axis=-1, keepdims=True)
            s = jnp.exp(s - top)
            total = jnp.sum(s, axis=-1, keepdims=True)
            lse_all = jnp.where(lane == h, top + jnp.log(total), lse_all)
            out.append(nn((s / total).astype(BF16), v_pair))
        lse[...] = lse_all
        ctx[:, cols] = jnp.where(lane < 64, out[0], out[1]).astype(BF16)

    def out_proj():
        def write(i, cols, res):
            mid[:, cols] = res + vecs[OB : OB + 1, cols] + x_in[:, cols].astype(F32)

        matmul(ctx, WO, write)

        def body(i):
            r = rows_of(i, 32)
            n, s = center_scale(mid[r, :])
            n2[r, pl.ds(0, D)] = n
            n2[r, pl.ds(D, 128)] = jnp.broadcast_to(s, (32, 128))
            act2[r, :] = (n * vec(LN2G) + vec(LN2B)).astype(BF16)

        loop(10, body)

    def up(j):
        def write(i, cols, res):
            tmp[:, cols] = res + vecs[UB + j : UB + j + 1, cols]

        matmul(act2, WUP + j, write)

        def body(i):
            r = rows_of(i, 16)
            value, grad = gelu_both(tmp[r, :])
            hid[j, r, :] = value.astype(BF16)
            slope[j, r, :] = grad

        loop(20, body)

    def down(j):
        def write(i, cols, res):
            base_val = mid[:, cols]
            if j == 0:
                base_val = base_val + vecs[DB : DB + 1, cols]
            res = res + base_val
            if j < 3:
                mid[:, cols] = res
            else:
                block_out[:, cols] = res.astype(BF16)

        matmul(hid.at[j], WDN + j, write)

    plan = {t: [] for t in range(40)}
    plan[4].append(norm_one)
    for c in range(3):
        plan[6 + c].append(lambda c=c: project(c))
    for p in range(8):
        plan[8 + (p + 1) // 3].append(lambda p=p: attend(p))
    plan[11].append(out_proj)
    for j in range(4):
        plan[max(11, 10 + j)].append(lambda j=j: up(j))
        plan[14 + j].append(lambda j=j: down(j))

    sm_step(0)
    stage0(0)
    stage0(1)
    for j in range(4):
        for s in range(8):
            pltpu.make_async_copy(
                w_up.at[:, pl.ds(s * 512 + j * 128, 128)],
                full.at[WUP + j, me, :, pl.ds(s * 128, 128)],
                own_sem.at[WUP + j],
            ).start()
        pltpu.make_async_copy(
            w_down.at[pl.ds(j * 128, 128)], full.at[WDN + j, me], own_sem.at[WDN + j]
        ).start()
    stage0(2)
    for t in range(1, 18):
        if t < 4:
            sm_step(t)
        comm(t)
        for piece in plan[t]:
            piece()
    for cp in started:
        cp.wait_send()
    for k in range(NCH):
        keep(k).wait()


def gather_forward(w_qkv, w_attn_out, w_up, w_down, small, x_in):
    vm = pl.BlockSpec(memory_space=pltpu.VMEM)
    hbm = pl.BlockSpec(memory_space=pl.ANY)
    S = jax.ShapeDtypeStruct
    act = S((SEQ, D), BF16)
    return pl.pallas_call(
        forward_kernel,
        out_shape=[
            S((NCH, 8, 128, D), BF16),
            S((8, 16, 128), BF16),
            act,
            act,
            act,
            act,
            act,
            S((SEQ, 128), F32),
            act,
            act,
            S((SEQ, D + 128), F32),
            S((4, SEQ, D), BF16),
            S((4, SEQ, D), F32),
        ],
        in_specs=[hbm] * 4 + [vm] * 2,
        out_specs=[hbm] + [vm] * 12,
        scratch_shapes=[
            pltpu.VMEM((NCH, 8, 128, D), BF16),
            pltpu.VMEM((SEQ, D), F32),
            pltpu.VMEM((SEQ, SEQ), F32),
            pltpu.VMEM((16, D), F32),
            pltpu.VMEM((SEQ, D), F32),
            pltpu.SemaphoreType.DMA((NCH, GCOPIES)),
            pltpu.SemaphoreType.DMA((NCH, GCOPIES)),
            pltpu.SemaphoreType.DMA((NCH,)),
            pltpu.SemaphoreType.DMA((NCH,)),
            pltpu.SemaphoreType.DMA((4,)),
            pltpu.SemaphoreType.DMA((4,)),
        ],
        compiler_params=pltpu.CompilerParams(
            collective_id=0, has_side_effects=True, vmem_limit_bytes=56 * MIB
        ),
        name="gather_forward",
    )(w_qkv, w_attn_out, w_up, w_down, small, x_in)


RCOPIES = 20
STAGED = 3
WSLOTS = 3
MADE = (WDN, WUP, WDN + 1, WUP + 1, WDN + 2, WUP + 2, WDN + 3, WUP + 3, WO, WV, WK, WQ)


def backward_kernel(*refs):
    full, hid_hbm, slope_hbm, sm_all, x_in, cot, act1, q, k_, v, lse, ctx, act2, n2 = refs[:14]
    input_grad, fin, fin_small = refs[14:17]
    acc, staged, rx1, rx2, ry, rz1, rz2, rp1, rp2 = refs[17:26]
    wbuf, hid_buf, slope_buf, cot_b, dub, dact, dmid, dmid_b, dctx, dq, dk, dv, dist, vecs = refs[26:40]
    sums, small_in = refs[40:42]
    send_sem, recv_sem, load_sem, hid_sem, sm_send, sm_recv = refs[42:]
    x, core, hi, z, peers = place()
    lo = (lax.axis_index("rep") // 2) % 2
    other = 1 - hi
    me = hi * 4 + z
    xp, xm, xo = (x + 1) % 4, (x + 3) % 4, (x + 2) % 4
    zp, zm, zo = (z + 1) % 4, (z + 3) % 4, (z + 2) % 4
    others = pl.ds(other * 4, 4)

    started = []

    def push(src, dst, ss, rs, to):
        cp = pltpu.make_async_remote_copy(
            src_ref=src,
            dst_ref=dst,
            send_sem=ss,
            recv_sem=rs,
            device_id=peers[to],
            device_id_type=MESH,
        )
        cp.start()
        started.append(cp)
        return cp

    by_chunk = [dict() for _ in range(NCH)]

    def send(k, name, src, dst, to):
        slot = len(by_chunk[k])
        by_chunk[k][name] = push(src, dst, send_sem.at[k, slot], recv_sem.at[k, slot], to)

    def got(k, *names):
        for name in names:
            by_chunk[k][name].wait_recv()

    def add(idx, *terms):
        total = acc[idx].astype(F32)
        for ref, i in terms:
            total = total + ref[i].astype(F32)
        acc[idx] = total.astype(BF16)

    def sub(i):
        return pl.ds(pl.multiple_of(i * 16, 16), 16)

    def s0(k):
        got(k, "c")

        def body(i):
            add((k, i), (staged, (k % STAGED, core, i)))

        loop(8, body)
        send(k, "x1r", acc.at[k, pl.ds(other * 4, 2), sub(xo)], rx1.at[k, 0], "xr")
        send(k, "x1l", acc.at[k, pl.ds(other * 4 + 2, 2), sub(xo)], rx1.at[k, 1], "xl")

    def s1(k):
        got(k, "x1r", "x1l")
        add((k, pl.ds(other * 4, 2), sub(xp)), (rx1, (k, 0)))
        send(k, "x2r", acc.at[k, others, sub(xp)], rx2.at[k, 0], "xr")
        add((k, pl.ds(other * 4 + 2, 2), sub(xm)), (rx1, (k, 1)))
        send(k, "x2l", acc.at[k, others, sub(xm)], rx2.at[k, 1], "xl")

    def s2(k):
        got(k, "x2r", "x2l")
        add((k, others, sub(x)), (rx2, (k, 0)), (rx2, (k, 1)))
        send(k, "y", acc.at[k, others, sub(x)], ry.at[k], "cross")

    def s3(k):
        got(k, "y")
        add((k, pl.ds(hi * 4, 4), sub(x)), (ry, (k,)))
        send(k, "z1r", acc.at[k, hi * 4 + zo, pl.ds(0, 32)], rz1.at[k, 0], "zr")
        send(k, "z1l", acc.at[k, hi * 4 + zo, pl.ds(32, 32)], rz1.at[k, 1], "zl")

    def s4(k):
        got(k, "z1r", "z1l")
        add((k, hi * 4 + zp, pl.ds(0, 32)), (rz1, (k, 0)))
        send(k, "z2r", acc.at[k, hi * 4 + zp], rz2.at[k, 0], "zr")
        add((k, hi * 4 + zm, pl.ds(32, 32)), (rz1, (k, 1)))
        send(k, "z2l", acc.at[k, hi * 4 + zm], rz2.at[k, 1], "zl")

    def s5(k):
        got(k, "z2r", "z2l")
        add((k, me), (rz2, (k, 0)), (rz2, (k, 1)))
        theirs = pl.ds(pl.multiple_of((1 - lo) * 32, 32), 32)
        send(k, "p1", acc.at[k, me, theirs], rp1.at[k], "ylo")

    mine32 = pl.ds(pl.multiple_of(lo * 32, 32), 32)

    def block(i):
        return pl.ds(pl.multiple_of(i * 256, 256), 256)

    def s6(k):
        got(k, "p1")
        add((k, me, mine32), (rp1, (k,)))
        send(k, "p2r", acc.at[k, me, mine32, block(xp)], rp2.at[k, 0], "xr")
        send(k, "p2l", acc.at[k, me, mine32, block(xm)], rp2.at[k, 1], "xl")
        send(k, "p2o", acc.at[k, me, mine32, block(xo)], rp2.at[k, 2], "xo")

    def fin_rows(lo_):
        return pl.ds(pl.multiple_of(core * 64 + lo_ * 32, 32), 32)

    def s7(k):
        got(k, "p2r", "p2l", "p2o")
        total = acc[k, me, mine32, block(x)].astype(F32)
        for i in range(3):
            total = total + rp2[k, i].astype(F32)
        m = MADE[k]
        fin[m, fin_rows(lo), block(x)] = (total * (1.0 / 128.0)).astype(BF16)
        view = fin.at[m, fin_rows(lo), block(x)]
        for to in ("xr", "xl", "xo"):
            send(k, "p3" + to, view, view, to)

    def s8(k):
        got(k, "p3xr", "p3xl", "p3xo")
        view = fin.at[MADE[k], fin_rows(lo)]
        send(k, "p4y", view, view, "ylo")
        send(k, "p4c", view, view, "core")

    def s9(k):
        got(k, "p4y")
        view = fin.at[MADE[k], fin_rows(1 - lo)]
        send(k, "p5", view, view, "core")

    def s10(k):
        got(k, "p4c", "p5")

    stages = (s0, s1, s2, s3, s4, s5, s6, s7, s8, s9, s10)
    at = {}

    def comm():
        for k in sorted(at):
            stages[at[k]](k)
            at[k] += 1
            if at[k] == len(stages):
                del at[k]

    def produce(k, a_ref, b_ref):
        if k >= STAGED:
            sent = by_chunk[k - STAGED]["c"]
            sent.wait_send()
            started[:] = [cp for cp in started if cp is not sent]
        slot = k % STAGED

        def body(i):
            res = tn(a_ref[:, rows_of(i, 256)], b_ref[...]).astype(BF16)
            for e in range(2):
                for h in range(2):
                    first = e * 128 + h * 64
                    staged[slot, h, 2 * i + e] = res[first : first + 64]

        loop(4, body)
        send(k, "c", staged.at[slot, 1 - core], acc.at[k], "core")
        at[k] = 0

    uses = (WDN, WUP, WDN + 1, WUP + 1, WDN + 2, WUP + 2, WDN + 3, WUP + 3, WO, WV, WK, WQ)

    def load(u):
        return pltpu.make_async_copy(
            full.at[uses[u]], wbuf.at[u % WSLOTS], load_sem.at[u % WSLOTS]
        )

    def need(u):
        load(u).wait()

    def done_with(u):
        if u + WSLOTS < len(uses):
            load(u + WSLOTS).start()

    def bring(j):
        return (
            pltpu.make_async_copy(hid_hbm.at[j], hid_buf.at[j % 2], hid_sem.at[j % 2, 0]),
            pltpu.make_async_copy(slope_hbm.at[j], slope_buf.at[j % 2], hid_sem.at[j % 2, 1]),
        )

    def times_t(a_ref, u, write):
        def body(i):
            w = wbuf[u % WSLOTS, pl.ds(2 * i, 2)].reshape(256, D)
            cols = rows_of(i, 256)
            write(cols, nt(a_ref[...], w))

        loop(4, body)

    def bump(row, cols, rows):
        sums[row : row + 1, cols] += jnp.sum(rows, axis=0, keepdims=True)

    everything = pl.ds(0, D)
    for u in range(WSLOTS):
        load(u).start()
    for cp in bring(0):
        cp.start()
    sums[...] = jnp.zeros_like(sums)
    for s in range(8):
        vecs[:, pl.ds(s * 128, 128)] = sm_all[s].astype(F32)

    def prepare(i):
        r = rows_of(i, 32)
        rows = cot[r, :]
        cot_b[r, :] = rows.astype(BF16)
        bump(DB, everything, rows)

    loop(10, prepare)
    row = lax.broadcasted_iota(jnp.int32, (SEQ, SEQ), 0)
    col = lax.broadcasted_iota(jnp.int32, (SEQ, SEQ), 1)
    dist[...] = (row - col).astype(F32)
    greet(peers, ("xr", "xl", "xo", "zr", "zl", "zo", "cross", "ylo", "yo", "core"))

    for j in range(4):
        for cp in bring(j):
            cp.wait()
        if j < 3:
            for cp in bring(j + 1):
                cp.start()
        need(2 * j)

        def to_dup(cols, res):
            res = res * slope_buf[j % 2, :, cols]
            dub[:, cols] = res.astype(BF16)
            bump(UB + j, cols, res)

        times_t(cot_b, 2 * j, to_dup)
        done_with(2 * j)
        produce(2 * j, hid_buf.at[j % 2], cot_b)
        comm()
        produce(2 * j + 1, act2, dub)
        need(2 * j + 1)

        def to_dact(cols, res):
            dact[:, cols] = res if j == 0 else dact[:, cols] + res

        times_t(dub, 2 * j + 1, to_dact)
        done_with(2 * j + 1)
        comm()

    def norm_two(i):
        r = rows_of(i, 32)
        e, n, s = dact[r, :], n2[r, pl.ds(0, D)], n2[r, pl.ds(D, 128)][:, 0:1]
        bump(LN2G, everything, e * n)
        bump(LN2B, everything, e)
        e = e * vecs[LN2G : LN2G + 1, :]
        e = e - jnp.mean(e, axis=-1, keepdims=True) - n * jnp.mean(e * n, axis=-1, keepdims=True)
        m = cot[r, :] + s * e
        dmid[r, :] = m
        dmid_b[r, :] = m.astype(BF16)
        bump(OB, everything, m)

    loop(10, norm_two)
    produce(8, ctx, dmid_b)
    need(8)

    def to_dctx(cols, res):
        dctx[:, cols] = res.astype(BF16)

    times_t(dmid_b, 8, to_dctx)
    done_with(8)
    comm()

    lane = lax.broadcasted_iota(jnp.int32, (SEQ, 128), 1)
    scale = HEAD_DIM**-0.5

    def attend_back(p):
        cols = pl.ds(p * 128, 128)
        q_pair, k_pair, v_pair, c_pair = q[:, cols], k_[:, cols], v[:, cols], dctx[:, cols]
        out = []
        for e in range(2):
            h = 2 * p + e
            mine = (lane < 64) if e == 0 else (lane >= 64)
            zero = jnp.zeros_like(q_pair)
            s = nt(jnp.where(mine, q_pair, zero), k_pair)
            d = dist[...]
            s = jnp.where(d >= 0.0, s * scale - slope_of(h) * d, -jnp.inf)
            prob = jnp.exp(s - lse[:, h : h + 1])
            d_prob = nt(jnp.where(mine, c_pair, zero), v_pair)
            d_score = prob * (d_prob - jnp.sum(prob * d_prob, axis=-1, keepdims=True))
            d_score = d_score.astype(BF16)
            out.append((nn(d_score, k_pair), tn(d_score, q_pair), tn(prob.astype(BF16), c_pair)))
        low = lane < 64
        g_q = jnp.where(low, out[0][0], out[1][0]) * scale
        g_k = jnp.where(low, out[0][1], out[1][1]) * scale
        g_v = jnp.where(low, out[0][2], out[1][2])
        dq[:, cols], dk[:, cols], dv[:, cols] = g_q.astype(BF16), g_k.astype(BF16), g_v.astype(BF16)
        bump(QB, cols, g_q)
        bump(VB, cols, g_v)

    for p in range(8):
        attend_back(p)
        comm()

    for i, grad in enumerate((dv, dk, dq)):
        produce(9 + i, act1, grad)
        comm()
    for i, grad in enumerate((dv, dk, dq)):
        need(9 + i)

        def to_e1(cols, res):
            dact[:, cols] = res if i == 0 else dact[:, cols] + res

        times_t(grad, 9 + i, to_e1)
        comm()

    def norm_one(i):
        r = rows_of(i, 32)
        n, s = center_scale(x_in[r, :].astype(F32))
        e = dact[r, :]
        bump(LN1G, everything, e * n)
        bump(LN1B, everything, e)
        e = e * vecs[LN1G : LN1G + 1, :]
        e = e - jnp.mean(e, axis=-1, keepdims=True) - n * jnp.mean(e * n, axis=-1, keepdims=True)
        input_grad[r, :] = dmid[r, :] + s * e

    loop(10, norm_one)

    y = hi * 2 + lo
    small_in[0, core] = sums[...].astype(BF16)
    rounds = (
        (core, 2, ("core",)),
        (x, 4, ("xr", "xl", "xo")),
        (y, 4, ("ylo", "cross", "yo")),
        (z, 4, ("zr", "zl", "zo")),
    )
    for i, (mine, n, to) in enumerate(rounds):
        copies = [
            push(
                small_in.at[i, mine],
                small_in.at[i, mine],
                sm_send.at[i, m],
                sm_recv.at[i, m],
                name,
            )
            for m, name in enumerate(to)
        ]
        comm()
        for cp in copies:
            cp.wait_recv()
        total = small_in[i, 0].astype(F32)
        for m in range(1, n):
            total = total + small_in[i, m].astype(F32)
        if i < 3:
            small_in[i + 1, rounds[i + 1][0]] = total.astype(BF16)
        else:
            sums[...] = total * (1.0 / 128.0)
    fin_small[...] = sums[:, pl.ds(pl.multiple_of(me * 128, 128), 128)]
    while at:
        comm()
    for cp in started:
        cp.wait_send()


def backward_reduce(full, hid, slope, sm, x_in, cot, act1, q, k, v, lse, ctx, act2, n2):
    vm = pl.BlockSpec(memory_space=pltpu.VMEM)
    hbm = pl.BlockSpec(memory_space=pl.ANY)
    S = jax.ShapeDtypeStruct
    V = pltpu.VMEM
    dma = pltpu.SemaphoreType.DMA
    return pl.pallas_call(
        backward_kernel,
        out_shape=[
            S((SEQ, D), F32),
            S((NCH, 128, D), BF16),
            S((16, 128), F32),
        ],
        in_specs=[hbm] * 3 + [vm] * 11,
        out_specs=[vm] * 3,
        scratch_shapes=[
            V((NCH, 8, 64, D), BF16),
            V((STAGED, 2, 8, 64, D), BF16),
            V((NCH, 2, 2, 16, D), BF16),
            V((NCH, 2, 4, 16, D), BF16),
            V((NCH, 4, 16, D), BF16),
            V((NCH, 2, 32, D), BF16),
            V((NCH, 2, 64, D), BF16),
            V((NCH, 32, D), BF16),
            V((NCH, 3, 32, 256), BF16),
            V((WSLOTS, 8, 128, D), BF16),
            V((2, SEQ, D), BF16),
            V((2, SEQ, D), F32),
            V((SEQ, D), BF16),
            V((SEQ, D), BF16),
            V((SEQ, D), F32),
            V((SEQ, D), F32),
            V((SEQ, D), BF16),
            V((SEQ, D), BF16),
            V((SEQ, D), BF16),
            V((SEQ, D), BF16),
            V((SEQ, D), BF16),
            V((SEQ, SEQ), F32),
            V((16, D), F32),
            V((16, D), F32),
            V((4, 4, 16, D), BF16),
            dma((NCH, RCOPIES)),
            dma((NCH, RCOPIES)),
            dma((WSLOTS,)),
            dma((2, 2)),
            dma((4, 3)),
            dma((4, 3)),
        ],
        compiler_params=pltpu.CompilerParams(
            collective_id=1, has_side_effects=True, vmem_limit_bytes=63 * MIB
        ),
        name="backward_reduce",
    )(full, hid, slope, sm, x_in, cot, act1, q, k, v, lse, ctx, act2, n2)


def on_device(
    x_in,
    cotangent,
    ln1_gain,
    ln1_bias,
    w_qkv,
    q_bias,
    v_bias,
    w_attn_out,
    out_bias,
    ln2_gain,
    ln2_bias,
    w_up,
    up_bias,
    w_down,
    down_bias,
):
    small = jnp.concatenate(
        [ln1_gain, ln1_bias, q_bias, v_bias, out_bias, ln2_gain, ln2_bias, down_bias, up_bias]
        + [jnp.zeros((512,), BF16)]
    ).reshape(16, 128)
    full, sm, block_out, act1, q, k, v, lse, ctx, act2, n2, hid, slope = gather_forward(
        w_qkv, w_attn_out, w_up, w_down, small, x_in
    )
    input_grad, big, vals = backward_reduce(
        full, hid, slope, sm, x_in, cotangent, act1, q, k, v, lse, ctx, act2, n2
    )
    big = big.astype(F32)
    return (
        block_out,
        input_grad,
        vals[LN1G],
        vals[LN1B],
        jnp.concatenate([big[WQ], big[WK], big[WV]], axis=1),
        vals[QB],
        vals[VB],
        big[WO],
        vals[OB],
        vals[LN2G],
        vals[LN2B],
        big[WUP : WUP + 4].reshape(4, 128, 8, 128).transpose(1, 2, 0, 3).reshape(128, 4 * D),
        vals[UB : UB + 4].reshape(-1),
        big[WDN : WDN + 4].reshape(512, D),
        vals[DB],
    )


def solution(mesh):
    placed = (
        P(("rep", "shard"), None),
        P(("rep", "shard"), None),
        P("shard"),
        P("shard"),
        P("shard", None),
        P("shard"),
        P("shard"),
        P("shard", None),
        P("shard"),
        P("shard"),
        P("shard"),
        P("shard", None),
        P("shard"),
        P("shard", None),
        P("shard"),
    )
    return jax.shard_map(
        on_device,
        mesh=mesh,
        in_specs=placed,
        out_specs=(
            P(("rep", "shard"), None),
            P(("rep", "shard"), None),
            P("shard"),
            P("shard"),
            P("shard", None),
            P("shard"),
            P("shard"),
            P("shard", None),
            P("shard"),
            P("shard"),
            P("shard"),
            P("shard", None),
            P("shard"),
            P("shard", None),
            P("shard"),
        ),
        check_vma=False,
    )
```

```python
import math

import jax
import jax.numpy as jnp
from jax import lax
from jax.experimental import pallas as pl
from jax.experimental.pallas import tpu as pltpu
from jax.sharding import PartitionSpec as P

HEADS = 16
HEAD_DIM = 64
SEQ = 320
D = 1024
NCH = 12
MESH = pl.DeviceIdType.MESH
BF16 = jnp.bfloat16
F32 = jnp.float32
MIB = 1024 * 1024

eps_norm = 1e-05
sqrt_two_pi = math.sqrt(2.0 / math.pi)
cubic_coef = 0.044715

LN1G, LN1B, QB, VB, OB, LN2G, LN2B, DB, UB = 0, 1, 2, 3, 4, 5, 6, 7, 8
WQ, WK, WV, WO, WUP, WDN = 0, 1, 2, 3, 4, 8


def place():
    rep = lax.axis_index("rep")
    shard = lax.axis_index("shard")
    x, lo, core = rep // 4, (rep // 2) % 2, rep % 2
    hi, z = shard // 4, shard % 4

    def dev(x_, lo_, core_, hi_, z_):
        return ((x_ * 2 + lo_) * 2 + core_, hi_ * 4 + z_)

    peers = dict(
        xr=dev((x + 1) % 4, lo, core, hi, z),
        xl=dev((x + 3) % 4, lo, core, hi, z),
        xo=dev((x + 2) % 4, lo, core, hi, z),
        zr=dev(x, lo, core, hi, (z + 1) % 4),
        zl=dev(x, lo, core, hi, (z + 3) % 4),
        zo=dev(x, lo, core, hi, (z + 2) % 4),
        cross=dev(x, 1 - lo, core, 1 - hi, z),
        ylo=dev(x, 1 - lo, core, hi, z),
        yo=dev(x, lo, core, 1 - hi, z),
        core=dev(x, lo, 1 - core, hi, z),
    )
    return x, core, hi, z, peers


def greet(peers, names):
    barrier = pltpu.get_barrier_semaphore()
    for name in names:
        pl.semaphore_signal(barrier, inc=1, device_id=peers[name], device_id_type=MESH)
    pl.semaphore_wait(barrier, len(names))


def loop(n, body):
    def step(i, carry):
        body(i)
        return carry

    lax.fori_loop(0, n, step, 0)


def rows_of(i, n):
    return pl.ds(pl.multiple_of(i * n, n), n)


def nn(a, b):
    return jnp.dot(a, b, preferred_element_type=F32)


def nt(a, b):
    return lax.dot_general(a, b, (((1,), (1,)), ((), ())), preferred_element_type=F32)


def tn(a, b):
    return lax.dot_general(a, b, (((0,), (0,)), ((), ())), preferred_element_type=F32)


def slope_of(h):
    return 2.0 ** (-8.0 * (h + 1) / HEADS)


def gelu_both(u):
    tanh_val = jnp.tanh(sqrt_two_pi * (u + cubic_coef * u * u * u))
    value = 0.5 * u * (1.0 + tanh_val)
    slope = 0.5 * (1.0 + tanh_val) + 0.5 * u * (1.0 - tanh_val * tanh_val) * sqrt_two_pi * (
        1.0 + 3.0 * cubic_coef * u * u
    )
    return value, slope


def center_scale(rows):
    c = rows - jnp.mean(rows, axis=-1, keepdims=True)
    s = lax.rsqrt(jnp.mean(c * c, axis=-1, keepdims=True) + eps_norm)
    return c * s, s


HALF = 512
NH = 24
GCOPIES = 20
GAP = 3


def forward_kernel(*refs):
    w_qkv, w_o, w_up, w_down, small, x_in = refs[:6]
    full_out, sm_all, block_out, act1_o, qkv_o, lse, ctx_o, act2_o, n2_o, hid_o, slope_o = refs[6:17]
    full, act1, qkv, ctx, act2, n2, hid, slope, mid, dist, vecs, qkv_bias = refs[17:29]
    send_sem, recv_sem, own_sem, out_sem, sm_send, sm_recv, save_sem = refs[29:]
    x, core, hi, z, peers = place()
    other = 1 - hi
    me = hi * 4 + z
    left, right, far = hi * 4 + (z + 3) % 4, hi * 4 + (z + 1) % 4, hi * 4 + (z + 2) % 4

    def own(src, m, cols):
        pltpu.make_async_copy(src, full.at[m, me, :, cols], own_sem.at[m]).start()

    wide = pl.ds(0, D)
    for c in range(3):
        own(w_qkv.at[:, pl.ds(c * D, D)], WQ + c, wide)
    own(w_o, WO, wide)
    for j in range(4):
        for s in range(8):
            own(w_up.at[:, pl.ds(s * 512 + j * 128, 128)], WUP + j, pl.ds(s * 128, 128))
    for j in range(4):
        own(w_down.at[pl.ds(j * 128, 128)], WDN + j, wide)
    sm_all[me] = small[...]
    greet(peers, ("xr", "xl", "zr", "zl", "cross", "core"))

    def remote(src, dst, ss, rs, to):
        return pltpu.make_async_remote_copy(
            src_ref=src,
            dst_ref=dst,
            send_sem=ss,
            recv_sem=rs,
            device_id=peers[to],
            device_id_type=MESH,
        )

    base, quarter = core * 64, core * 64 + x * 16
    others = pl.ds(other * 4, 4)
    sx = lambda i: base + ((x + i) % 4) * 16

    def copies(k):
        cols = pl.ds(pl.multiple_of((k % 2) * HALF, HALF), HALF)

        def view(which, first, count):
            return full.at[k // 2, which, pl.ds(pl.multiple_of(first, 16), count), cols]

        table = (
            ("z1r", view(me, base, 64), "zr"),
            ("z1l", view(me, base, 64), "zl"),
            ("y0", view(me, quarter, 16), "cross"),
            ("z2r", view(left, base, 32), "zr"),
            ("y1", view(left, quarter, 16), "cross"),
            ("c1", view(left, base, 64), "core"),
            ("z2l", view(right, base + 32, 32), "zl"),
            ("y2", view(right, quarter, 16), "cross"),
            ("c2", view(right, base, 64), "core"),
            ("y3", view(far, quarter, 16), "cross"),
            ("c3", view(far, base, 64), "core"),
            ("x1r", view(others, quarter, 16), "xr"),
            ("x1l", view(others, quarter, 16), "xl"),
            ("c4", view(others, quarter, 16), "core"),
            ("x2r", view(pl.ds(other * 4, 2), sx(3), 16), "xr"),
            ("c5", view(others, sx(3), 16), "core"),
            ("x2l", view(pl.ds(other * 4 + 2, 2), sx(1), 16), "xl"),
            ("c6", view(others, sx(1), 16), "core"),
            ("c7", view(others, sx(2), 16), "core"),
        )
        return {
            name: remote(v, v, send_sem.at[k, i], recv_sem.at[k, i], to)
            for i, (name, v, to) in enumerate(table)
        }

    def stage(waits, sends):
        def run(k):
            c = copies(k)
            for name in waits:
                c[name].wait_recv()
            for name in sends:
                c[name].start()

        return run

    def stage0(k):
        @pl.when(k % 2 == 0)
        def _():
            mine = full.at[k // 2, me]
            pltpu.make_async_copy(mine, mine, own_sem.at[k // 2]).wait()

        stage((), ("z1r", "z1l", "y0"))(k)

    def stage1(k):
        stage(("z1r",), ("z2r", "y1", "c1"))(k)
        stage(("z1l",), ("z2l", "y2", "c2"))(k)

    def stage4(k):
        stage(("x1r",), ("x2r", "c5"))(k)
        stage(("x1l",), ("x2l", "c6"))(k)

    def keep(m):
        return pltpu.make_async_copy(full.at[m], full_out.at[m], out_sem.at[m])

    def stage6(k):
        stage(("c1", "c2", "c3", "c4", "c5", "c6", "c7"), ())(k)

        @pl.when(k % 2 == 1)
        def _():
            keep(k // 2).start()

    stages = (
        stage0,
        stage1,
        stage(("z2r", "z2l"), ("y3", "c3")),
        stage(("y0", "y1", "y2", "y3"), ("x1r", "x1l", "c4")),
        stage4,
        stage(("x2r", "x2l"), ("c7",)),
        stage6,
    )

    def comm(t):
        for s in range(6, -1, -1):
            k = t - GAP * s

            @pl.when((k >= 0) & (k < NH))
            def _():
                stages[s](k)

    sm_copy = [
        remote(sm_all.at[me], sm_all.at[me], sm_send.at[0], sm_recv.at[0], "zr"),
        remote(sm_all.at[me], sm_all.at[me], sm_send.at[1], sm_recv.at[1], "zl"),
        remote(sm_all.at[left], sm_all.at[left], sm_send.at[2], sm_recv.at[2], "zr"),
        remote(sm_all.at[pl.ds(hi * 4, 4)], sm_all.at[pl.ds(hi * 4, 4)], sm_send.at[3], sm_recv.at[3], "cross"),
    ]

    def vec(i):
        return vecs[i : i + 1, :]

    def save(i, src, dst):
        return pltpu.make_async_copy(src, dst, save_sem.at[i])

    saves = [
        save(0, act1, act1_o),
        save(1, qkv, qkv_o),
        save(2, ctx, ctx_o),
        save(3, act2, act2_o),
        save(4, n2, n2_o),
    ]

    def norm_one():
        for s in range(8):
            vecs[:, pl.ds(s * 128, 128)] = sm_all[s].astype(F32)
        qkv_bias[0:1, :] = vec(QB)
        qkv_bias[1:2, :] = jnp.zeros((1, D), F32)
        qkv_bias[2:3, :] = vec(VB)

        def body(i):
            r = rows_of(i, 32)
            n, s = center_scale(x_in[r, :].astype(F32))
            act1[r, :] = (n * vec(LN1G) + vec(LN1B)).astype(BF16)

        loop(10, body)
        row = lax.broadcasted_iota(jnp.int32, (SEQ, SEQ), 0)
        col = lax.broadcasted_iota(jnp.int32, (SEQ, SEQ), 1)
        dist[...] = (row - col).astype(F32)
        saves[0].start()

    def matmul(a_ref, k, write):
        def body(i):
            cols = pl.ds(pl.multiple_of((k % 2) * HALF + i * 256, 256), 256)
            write(cols, nn(a_ref[...], full[k // 2, :, :, cols].reshape(D, 256)))

        loop(2, body)

    def project(k):
        def write(cols, res):
            qkv[k // 2, :, cols] = (res + qkv_bias[pl.ds(k // 2, 1), cols]).astype(BF16)

        matmul(act1, k, write)

    def attend(p, factor):
        cols = pl.ds(pl.multiple_of(p * 128, 128), 128)
        lane = lax.broadcasted_iota(jnp.int32, (SEQ, 128), 1)
        q_pair, k_pair, v_pair = qkv[0, :, cols], qkv[1, :, cols], qkv[2, :, cols]
        out = []
        lse_all = lse[...]
        for e in range(2):
            mine = (lane < 64) if e == 0 else (lane >= 64)
            s = nt(jnp.where(mine, q_pair, jnp.zeros_like(q_pair)), k_pair)
            d = dist[...]
            s = jnp.where(d >= 0.0, s * HEAD_DIM**-0.5 - (factor * slope_of(e)) * d, -jnp.inf)
            top = jnp.max(s, axis=-1, keepdims=True)
            s = jnp.exp(s - top)
            total = jnp.sum(s, axis=-1, keepdims=True)
            lse_all = jnp.where(lane == 2 * p + e, top + jnp.log(total), lse_all)
            out.append(nn((s / total).astype(BF16), v_pair))
        lse[...] = lse_all
        ctx[:, cols] = jnp.where(lane < 64, out[0], out[1]).astype(BF16)
        return factor * 0.5

    def attend_half(i):
        @pl.when(i == 0)
        def _():
            lse[...] = jnp.zeros_like(lse)
            saves[1].start()

        first = jnp.where(i == 0, 1.0, 0.0625).astype(F32)
        lax.fori_loop(0, 4, lambda p, f: attend(i * 4 + p, f), first)

    def out_proj():
        saves[2].start()

        def body(k):
            def write(cols, res):
                mid[:, cols] = res + vecs[OB : OB + 1, cols] + x_in[:, cols].astype(F32)

            matmul(ctx, 2 * WO + k, write)

        loop(2, body)

        def norm(i):
            r = rows_of(i, 32)
            n, s = center_scale(mid[r, :])
            n2[r, pl.ds(0, D)] = n
            n2[r, pl.ds(D, 128)] = jnp.broadcast_to(s, (32, 128))
            act2[r, :] = (n * vec(LN2G) + vec(LN2B)).astype(BF16)

        loop(10, norm)
        saves[3].start()
        saves[4].start()

    def save_up(j):
        return (
            pltpu.make_async_copy(hid.at[j], hid_o.at[j], save_sem.at[5 + j]),
            pltpu.make_async_copy(slope.at[j], slope_o.at[j], save_sem.at[9 + j]),
        )

    def up(k):
        j = k // 2 - WUP

        def write(cols, res):
            value, grad = gelu_both(res + vecs[pl.ds(UB + j, 1), cols])
            hid[j, :, cols] = value.astype(BF16)
            slope[j, :, cols] = grad

        matmul(act2, k, write)

        @pl.when(k % 2 == 1)
        def _():
            for cp in save_up(j):
                cp.start()

    def down(k):
        j = k // 2 - WDN

        def write(cols, res):
            res = res + mid[:, cols]

            @pl.when(j < 3)
            def _():
                mid[:, cols] = res

            @pl.when(j == 3)
            def _():
                block_out[:, cols] = (res + vecs[DB : DB + 1, cols]).astype(BF16)

        matmul(hid.at[j], k, write)

    sm_copy[0].start()
    sm_copy[1].start()

    def slot(t):
        comm(t)

        @pl.when(t == 2)
        def _():
            sm_copy[0].wait_recv()
            sm_copy[1].wait_recv()
            sm_copy[2].start()

        @pl.when(t == 4)
        def _():
            sm_copy[2].wait_recv()
            sm_copy[3].start()

        @pl.when(t == 6)
        def _():
            sm_copy[3].wait_recv()
            norm_one()

        k = t - 6 * GAP

        @pl.when((k >= 0) & (k < 6))
        def _():
            project(k)

        @pl.when((k >= 6) & (k < 8))
        def _():
            attend_half(k - 6)

        @pl.when(k == 7)
        def _():
            out_proj()

        @pl.when((k >= 8) & (k < 16))
        def _():
            up(k)

        @pl.when(k >= 16)
        def _():
            down(k)

    loop(NH + 6 * GAP, slot)

    def sent(k):
        for cp in copies(k).values():
            cp.wait_send()

    loop(NH, sent)
    for cp in sm_copy:
        cp.wait_send()
    for m in range(NCH):
        keep(m).wait()
    for cp in saves:
        cp.wait()
    for j in range(4):
        for cp in save_up(j):
            cp.wait()


def gather_forward(w_qkv, w_attn_out, w_up, w_down, small, x_in):
    vm = pl.BlockSpec(memory_space=pltpu.VMEM)
    hbm = pl.BlockSpec(memory_space=pl.ANY)
    S = jax.ShapeDtypeStruct
    V = pltpu.VMEM
    dma = pltpu.SemaphoreType.DMA
    act = S((SEQ, D), BF16)
    return pl.pallas_call(
        forward_kernel,
        out_shape=[
            S((NCH, 8, 128, D), BF16),
            S((8, 16, 128), BF16),
            act,
            act,
            S((3, SEQ, D), BF16),
            S((SEQ, 128), F32),
            act,
            act,
            S((SEQ, D + 128), F32),
            S((4, SEQ, D), BF16),
            S((4, SEQ, D), F32),
        ],
        in_specs=[hbm] * 4 + [vm] * 2,
        out_specs=[hbm, vm, vm, hbm, hbm, vm, hbm, hbm, hbm, hbm, hbm],
        scratch_shapes=[
            V((NCH, 8, 128, D), BF16),
            V((SEQ, D), BF16),
            V((3, SEQ, D), BF16),
            V((SEQ, D), BF16),
            V((SEQ, D), BF16),
            V((SEQ, D + 128), F32),
            V((4, SEQ, D), BF16),
            V((4, SEQ, D), F32),
            V((SEQ, D), F32),
            V((SEQ, SEQ), F32),
            V((16, D), F32),
            V((8, D), F32),
            dma((NH, GCOPIES)),
            dma((NH, GCOPIES)),
            dma((NCH,)),
            dma((NCH,)),
            dma((4,)),
            dma((4,)),
            dma((13,)),
        ],
        compiler_params=pltpu.CompilerParams(
            collective_id=0, has_side_effects=True, vmem_limit_bytes=60 * MIB
        ),
        name="gather_forward",
    )(w_qkv, w_attn_out, w_up, w_down, small, x_in)


RCOPIES = 20
STAGED = 4
WSLOTS = 3
RGAP = 2
MADE = (
    [(m + j, h) for j in range(4) for m in (WDN, WUP) for h in range(2)]
    + [(WO, 0), (WO, 1)]
    + [(m, h) for h in range(2) for m in (WV, WK, WQ)]
)


def backward_kernel(*refs):
    full, hid_hbm, slope_hbm, sm_all, x_in, cot, act1, qkv, lse, ctx, act2, n2 = refs[:12]
    input_grad, out_qkv, out_o, out_up, out_down, fin_small = refs[12:18]
    acc, staged, rx1, rx2, ry, rz1, rz2, rp1, rp2, fin = refs[18:28]
    wbuf, hid_buf, slope_buf, cot_b, dub, dact, dmid, dmid_b, dctx, dqkv, dist, vecs = refs[28:40]
    sums, small_in = refs[40:42]
    send_sem, recv_sem, load_sem, hid_sem, sm_send, sm_recv = refs[42:]
    x, core, hi, z, peers = place()
    lo = (lax.axis_index("rep") // 2) % 2
    other = 1 - hi
    me = hi * 4 + z
    xp, xm, xo = (x + 1) % 4, (x + 3) % 4, (x + 2) % 4
    zp, zm, zo = (z + 1) % 4, (z + 3) % 4, (z + 2) % 4
    others = pl.ds(other * 4, 4)

    def remote(src, dst, ss, rs, to):
        return pltpu.make_async_remote_copy(
            src_ref=src,
            dst_ref=dst,
            send_sem=ss,
            recv_sem=rs,
            device_id=peers[to],
            device_id_type=MESH,
        )

    def sub(i):
        return pl.ds(pl.multiple_of(i * 16, 16), 16)

    def block(i):
        return pl.ds(pl.multiple_of(i * 128, 128), 128)

    def fin_rows(lo_):
        return pl.ds(pl.multiple_of(core * 64 + lo_ * 32, 32), 32)

    mine32 = pl.ds(pl.multiple_of(lo * 32, 32), 32)
    theirs32 = pl.ds(pl.multiple_of((1 - lo) * 32, 32), 32)

    def copies(k):
        piece = fin.at[k, fin_rows(lo), block(x)]
        whole = fin.at[k, fin_rows(lo)]
        theirs = fin.at[k, fin_rows(1 - lo)]
        table = (
            ("c", staged.at[k % STAGED, 1 - core], acc.at[k], "core"),
            ("x1r", acc.at[k, pl.ds(other * 4, 2), sub(xo)], rx1.at[k, 0], "xr"),
            ("x1l", acc.at[k, pl.ds(other * 4 + 2, 2), sub(xo)], rx1.at[k, 1], "xl"),
            ("x2r", acc.at[k, others, sub(xp)], rx2.at[k, 0], "xr"),
            ("x2l", acc.at[k, others, sub(xm)], rx2.at[k, 1], "xl"),
            ("y", acc.at[k, others, sub(x)], ry.at[k], "cross"),
            ("z1r", acc.at[k, hi * 4 + zo, pl.ds(0, 32)], rz1.at[k, 0], "zr"),
            ("z1l", acc.at[k, hi * 4 + zo, pl.ds(32, 32)], rz1.at[k, 1], "zl"),
            ("z2r", acc.at[k, hi * 4 + zp], rz2.at[k, 0], "zr"),
            ("z2l", acc.at[k, hi * 4 + zm], rz2.at[k, 1], "zl"),
            ("p1", acc.at[k, me, theirs32], rp1.at[k], "ylo"),
            ("p2r", acc.at[k, me, mine32, block(xp)], rp2.at[k, 0], "xr"),
            ("p2l", acc.at[k, me, mine32, block(xm)], rp2.at[k, 1], "xl"),
            ("p2o", acc.at[k, me, mine32, block(xo)], rp2.at[k, 2], "xo"),
            ("p3r", piece, piece, "xr"),
            ("p3l", piece, piece, "xl"),
            ("p3o", piece, piece, "xo"),
            ("p4y", whole, whole, "ylo"),
            ("p4c", whole, whole, "core"),
            ("p5", theirs, theirs, "core"),
        )
        return {
            name: remote(src, dst, send_sem.at[k, i], recv_sem.at[k, i], to)
            for i, (name, src, dst, to) in enumerate(table)
        }

    def got(c, *names):
        for name in names:
            c[name].wait_recv()

    def go(c, *names):
        for name in names:
            c[name].start()

    def add(idx, *terms):
        total = acc[idx].astype(F32)
        for ref, i in terms:
            total = total + ref[i].astype(F32)
        acc[idx] = total.astype(BF16)

    def s0(k):
        c = copies(k)
        got(c, "c")

        def body(i):
            add((k, i), (staged, (k % STAGED, core, i)))

        loop(8, body)
        go(c, "x1r", "x1l")

    def s1(k):
        c = copies(k)
        got(c, "x1r", "x1l")
        add((k, pl.ds(other * 4, 2), sub(xp)), (rx1, (k, 0)))
        go(c, "x2r")
        add((k, pl.ds(other * 4 + 2, 2), sub(xm)), (rx1, (k, 1)))
        go(c, "x2l")

    def s2(k):
        c = copies(k)
        got(c, "x2r", "x2l")
        add((k, others, sub(x)), (rx2, (k, 0)), (rx2, (k, 1)))
        go(c, "y")

    def s3(k):
        c = copies(k)
        got(c, "y")
        add((k, pl.ds(hi * 4, 4), sub(x)), (ry, (k,)))
        go(c, "z1r", "z1l")

    def s4(k):
        c = copies(k)
        got(c, "z1r", "z1l")
        add((k, hi * 4 + zp, pl.ds(0, 32)), (rz1, (k, 0)))
        go(c, "z2r")
        add((k, hi * 4 + zm, pl.ds(32, 32)), (rz1, (k, 1)))
        go(c, "z2l")

    def s5(k):
        c = copies(k)
        got(c, "z2r", "z2l")
        add((k, me), (rz2, (k, 0)), (rz2, (k, 1)))
        go(c, "p1")

    def s6(k):
        c = copies(k)
        got(c, "p1")
        add((k, me, mine32), (rp1, (k,)))
        go(c, "p2r", "p2l", "p2o")

    def s7(k):
        c = copies(k)
        got(c, "p2r", "p2l", "p2o")
        total = acc[k, me, mine32, block(x)].astype(F32)
        for i in range(3):
            total = total + rp2[k, i].astype(F32)
        fin[k, fin_rows(lo), block(x)] = (total * (1.0 / 128.0)).astype(BF16)
        go(c, "p3r", "p3l", "p3o")

    def s8(k):
        c = copies(k)
        got(c, "p3r", "p3l", "p3o")
        go(c, "p4y", "p4c")

    def s9(k):
        c = copies(k)
        got(c, "p4y")
        go(c, "p5")

    def s10(k):
        got(copies(k), "p4c", "p5")

    stages = (s0, s1, s2, s3, s4, s5, s6, s7, s8, s9, s10)

    def comm(t):
        for s in range(10, -1, -1):
            k = t - RGAP * (s + 1)

            @pl.when((k >= 0) & (k < NH))
            def _():
                stages[s](k)

    def produce(k, half, a_ref, b_ref):
        slot = k % STAGED

        @pl.when(k >= STAGED)
        def _():
            copies(k - STAGED)["c"].wait_send()

        cols = pl.ds(pl.multiple_of(half * HALF, HALF), HALF)

        def body(i):
            res = tn(a_ref[:, rows_of(i, 256)], b_ref[:, cols]).astype(BF16)
            for e in range(2):
                for h in range(2):
                    first = e * 128 + h * 64
                    staged[slot, h, 2 * i + e] = res[first : first + 64]

        loop(4, body)
        copies(k)["c"].start()

    def load(m, u):
        return pltpu.make_async_copy(full.at[m], wbuf.at[u % WSLOTS], load_sem.at[u % WSLOTS])

    def bring(j):
        return (
            pltpu.make_async_copy(hid_hbm.at[j], hid_buf.at[j % 2], hid_sem.at[j % 2, 0]),
            pltpu.make_async_copy(slope_hbm.at[j], slope_buf.at[j % 2], hid_sem.at[j % 2, 1]),
        )

    def times_t(a_ref, u, write):
        def body(i):
            w = wbuf[u % WSLOTS, pl.ds(2 * i, 2)].reshape(256, D)
            write(rows_of(i, 256), nt(a_ref[...], w))

        loop(4, body)

    def bump(row, cols, rows):
        sums[row, cols] += jnp.sum(rows, axis=0, keepdims=True)

    def one(i):
        return pl.ds(i, 1)

    wide = pl.ds(0, D)
    load(WDN, 0).start()
    load(WUP, 1).start()
    load(WDN + 1, 2).start()
    for cp in bring(0):
        cp.start()
    sums[...] = jnp.zeros_like(sums)
    for s in range(8):
        vecs[:, pl.ds(s * 128, 128)] = sm_all[s].astype(F32)

    def prepare(i):
        r = rows_of(i, 32)
        rows = cot[r, :]
        cot_b[r, :] = rows.astype(BF16)
        bump(one(DB), wide, rows)

    loop(10, prepare)
    dact[...] = jnp.zeros_like(dact)
    iota_row = lax.broadcasted_iota(jnp.int32, (SEQ, SEQ), 0)
    iota_col = lax.broadcasted_iota(jnp.int32, (SEQ, SEQ), 1)
    dist[...] = (iota_row - iota_col).astype(F32)
    greet(peers, ("xr", "xl", "xo", "zr", "zl", "zo", "cross", "ylo", "yo", "core"))

    def ffn_first(j):
        for cp in bring(j):
            cp.wait()

        @pl.when(j < 3)
        def _():
            for cp in bring(j + 1):
                cp.start()

        load(WDN, 2 * j).wait()

        def write(cols, res):
            res = res * slope_buf[j % 2, :, cols]
            dub[:, cols] = res.astype(BF16)
            bump(one(UB + j), cols, res)

        times_t(cot_b, 2 * j, write)

        @pl.when(j < 3)
        def _():
            load(WUP + j + 1, 2 * j + 3).start()

        @pl.when(j == 3)
        def _():
            load(WV, 9).start()

    def ffn_second(j):
        load(WUP, 2 * j + 1).wait()

        def write(cols, res):
            dact[:, cols] += res

        times_t(dub, 2 * j + 1, write)

        @pl.when(j < 2)
        def _():
            load(WDN + j + 2, 2 * j + 4).start()

        @pl.when(j == 2)
        def _():
            load(WO, 8).start()

        @pl.when(j == 3)
        def _():
            load(WK, 10).start()

    def back(e, n):
        return e - jnp.mean(e, axis=-1, keepdims=True) - n * jnp.mean(e * n, axis=-1, keepdims=True)

    def norm_two(i):
        r = rows_of(i, 32)
        e, n, s = dact[r, :], n2[r, pl.ds(0, D)], n2[r, pl.ds(D, 128)][:, 0:1]
        bump(one(LN2G), wide, e * n)
        bump(one(LN2B), wide, e)
        m = cot[r, :] + s * back(e * vecs[LN2G : LN2G + 1, :], n)
        dmid[r, :] = m
        dmid_b[r, :] = m.astype(BF16)
        bump(one(OB), wide, m)

    def context():
        load(WO, 8).wait()

        def write(cols, res):
            dctx[:, cols] = res.astype(BF16)

        times_t(dmid_b, 8, write)
        load(WQ, 11).start()

    scale = HEAD_DIM**-0.5

    def attend_back(p, factor):
        lane = lax.broadcasted_iota(jnp.int32, (SEQ, 128), 1)
        lane_row = lax.broadcasted_iota(jnp.int32, (SEQ, 128), 1)
        cols = pl.ds(pl.multiple_of(p * 128, 128), 128)
        q_pair, k_pair, v_pair = qkv[0, :, cols], qkv[1, :, cols], qkv[2, :, cols]
        c_pair = dctx[:, cols]
        out = []
        for e in range(2):
            mine = (lane < 64) if e == 0 else (lane >= 64)
            zero = jnp.zeros_like(q_pair)
            s = nt(jnp.where(mine, q_pair, zero), k_pair)
            d = dist[...]
            s = jnp.where(d >= 0.0, s * scale - (factor * slope_of(e)) * d, -jnp.inf)
            total = jnp.sum(
                jnp.where(lane_row == 2 * p + e, lse[...], 0.0), axis=-1, keepdims=True
            )
            prob = jnp.exp(s - total)
            d_prob = nt(jnp.where(mine, c_pair, zero), v_pair)
            d_score = prob * (d_prob - jnp.sum(prob * d_prob, axis=-1, keepdims=True))
            d_score = d_score.astype(BF16)
            out.append((nn(d_score, k_pair), tn(d_score, q_pair), tn(prob.astype(BF16), c_pair)))
        low = lane < 64
        g_q = jnp.where(low, out[0][0], out[1][0]) * scale
        g_k = jnp.where(low, out[0][1], out[1][1]) * scale
        g_v = jnp.where(low, out[0][2], out[1][2])
        dqkv[2, :, cols], dqkv[1, :, cols], dqkv[0, :, cols] = (
            g_q.astype(BF16),
            g_k.astype(BF16),
            g_v.astype(BF16),
        )
        bump(one(QB), cols, g_q)
        bump(one(VB), cols, g_v)
        return factor * 0.5

    def first_grad(i):
        load(WV, 9 + i).wait()

        def write(cols, res):
            @pl.when(i == 0)
            def _():
                dact[:, cols] = res

            @pl.when(i > 0)
            def _():
                dact[:, cols] += res

        times_t(dqkv.at[i], 9 + i, write)

    def norm_one(i):
        r = rows_of(i, 32)
        n, s = center_scale(x_in[r, :].astype(F32))
        e = dact[r, :]
        bump(one(LN1G), wide, e * n)
        bump(one(LN1B), wide, e)
        input_grad[r, :] = dmid[r, :] + s * back(e * vecs[LN1G : LN1G + 1, :], n)

    rounds = (
        (core, 2, ("core",)),
        (x, 4, ("xr", "xl", "xo")),
        (hi * 2 + lo, 4, ("ylo", "cross", "yo")),
        (z, 4, ("zr", "zl", "zo")),
    )

    def small_copies(i):
        mine, n, to = rounds[i]
        view = small_in.at[i, mine]
        return [
            remote(view, view, sm_send.at[i, m], sm_recv.at[i, m], name)
            for m, name in enumerate(to)
        ]

    def small_round(i):
        if i == 0:
            small_in[0, core] = sums[...].astype(BF16)
        else:
            for cp in small_copies(i - 1):
                cp.wait_recv()
            total = small_in[i - 1, 0].astype(F32)
            for m in range(1, rounds[i - 1][1]):
                total = total + small_in[i - 1, m].astype(F32)
            if i < 4:
                small_in[i, rounds[i][0]] = total.astype(BF16)
            else:
                sums[...] = total * (1.0 / 128.0)
        if i < 4:
            for cp in small_copies(i):
                cp.start()

    def slot(t):
        comm(t)
        j, w, half = t // 4, (t // 2) % 2, t % 2

        @pl.when((t < 16) & (t % 4 == 0))
        def _():
            ffn_first(j)

        @pl.when((t < 16) & (w == 0))
        def _():
            produce(t, half, hid_buf.at[j % 2], cot_b)

        @pl.when((t < 16) & (w == 1))
        def _():
            produce(t, half, act2, dub)

        @pl.when((t < 16) & (t % 4 == 3))
        def _():
            ffn_second(j)

        @pl.when(t == 16)
        def _():
            loop(10, norm_two)

        @pl.when((t >= 16) & (t < 18))
        def _():
            produce(t, half, ctx, dmid_b)

        @pl.when(t == 17)
        def _():
            context()

        @pl.when((t >= 18) & (t < 20))
        def _():
            first = jnp.where(t == 18, 1.0, 0.0625).astype(F32)
            lax.fori_loop(0, 4, lambda p, f: attend_back((t - 18) * 4 + p, f), first)

        @pl.when((t >= 18) & (t < 24))
        def _():
            produce(t, (t - 18) // 3, act1, dqkv.at[(t - 18) % 3])

        @pl.when((t >= 24) & (t < 27))
        def _():
            first_grad(t - 24)

        @pl.when(t == 27)
        def _():
            loop(10, norm_one)

        for i in range(5):

            @pl.when(t == 28 + RGAP * i)
            def _():
                small_round(i)

    loop(NH + RGAP * 11, slot)
    fin_small[...] = sums[:, pl.ds(pl.multiple_of(me * 128, 128), 128)]
    for k in range(NH):
        m, half = MADE[k]
        cols = pl.ds(half * HALF, HALF)
        if m < WO:
            out_qkv[:, pl.ds(m * D + half * HALF, HALF)] = fin[k]
        elif m == WO:
            out_o[:, cols] = fin[k]
        elif m < WDN:
            for s in range(4):
                first = (half * 4 + s) * 512 + (m - WUP) * 128
                out_up[:, pl.ds(first, 128)] = fin[k, :, pl.ds(s * 128, 128)]
        else:
            out_down[pl.ds((m - WDN) * 128, 128), cols] = fin[k]

    def sent(k):
        c = copies(k)
        for name in c:
            if name != "c":
                c[name].wait_send()

        @pl.when(k >= NH - STAGED)
        def _():
            c["c"].wait_send()

    loop(NH, sent)
    for i in range(4):
        for cp in small_copies(i):
            cp.wait_send()


def backward_reduce(full, hid, slope, sm, x_in, cot, act1, qkv, lse, ctx, act2, n2):
    vm = pl.BlockSpec(memory_space=pltpu.VMEM)
    hbm = pl.BlockSpec(memory_space=pl.ANY)
    S = jax.ShapeDtypeStruct
    V = pltpu.VMEM
    dma = pltpu.SemaphoreType.DMA
    return pl.pallas_call(
        backward_kernel,
        out_shape=[
            S((SEQ, D), F32),
            S((128, 3 * D), BF16),
            S((128, D), BF16),
            S((128, 4 * D), BF16),
            S((512, D), BF16),
            S((16, 128), F32),
        ],
        in_specs=[hbm] * 3 + [vm] * 9,
        out_specs=[vm] * 6,
        scratch_shapes=[
            V((NH, 8, 64, HALF), BF16),
            V((STAGED, 2, 8, 64, HALF), BF16),
            V((NH, 2, 2, 16, HALF), BF16),
            V((NH, 2, 4, 16, HALF), BF16),
            V((NH, 4, 16, HALF), BF16),
            V((NH, 2, 32, HALF), BF16),
            V((NH, 2, 64, HALF), BF16),
            V((NH, 32, HALF), BF16),
            V((NH, 3, 32, 128), BF16),
            V((NH, 128, HALF), BF16),
            V((WSLOTS, 8, 128, D), BF16),
            V((2, SEQ, D), BF16),
            V((2, SEQ, D), F32),
            V((SEQ, D), BF16),
            V((SEQ, D), BF16),
            V((SEQ, D), F32),
            V((SEQ, D), F32),
            V((SEQ, D), BF16),
            V((SEQ, D), BF16),
            V((3, SEQ, D), BF16),
            V((SEQ, SEQ), F32),
            V((16, D), F32),
            V((16, D), F32),
            V((4, 4, 16, D), BF16),
            dma((NH, RCOPIES)),
            dma((NH, RCOPIES)),
            dma((WSLOTS,)),
            dma((2, 2)),
            dma((4, 3)),
            dma((4, 3)),
        ],
        compiler_params=pltpu.CompilerParams(
            collective_id=1, has_side_effects=True, vmem_limit_bytes=63 * MIB
        ),
        name="backward_reduce",
    )(full, hid, slope, sm, x_in, cot, act1, qkv, lse, ctx, act2, n2)


def on_device(
    x_in,
    cotangent,
    ln1_gain,
    ln1_bias,
    w_qkv,
    q_bias,
    v_bias,
    w_attn_out,
    out_bias,
    ln2_gain,
    ln2_bias,
    w_up,
    up_bias,
    w_down,
    down_bias,
):
    rows = (ln1_gain, ln1_bias, q_bias, v_bias, out_bias, ln2_gain, ln2_bias, down_bias)
    small = jnp.pad(up_bias.reshape(4, 128), ((UB, 4), (0, 0)))
    for i, row in enumerate(rows):
        small = small + jnp.pad(row.reshape(1, 128), ((i, 15 - i), (0, 0)))
    full, sm, block_out, act1, qkv, lse, ctx, act2, n2, hid, slope = gather_forward(
        w_qkv, w_attn_out, w_up, w_down, small, x_in
    )
    input_grad, g_qkv, g_o, g_up, g_down, vals = backward_reduce(
        full, hid, slope, sm, x_in, cotangent, act1, qkv, lse, ctx, act2, n2
    )
    return (
        block_out,
        input_grad,
        vals[LN1G],
        vals[LN1B],
        g_qkv.astype(F32),
        vals[QB],
        vals[VB],
        g_o.astype(F32),
        vals[OB],
        vals[LN2G],
        vals[LN2B],
        g_up.astype(F32),
        vals[UB : UB + 4].reshape(-1),
        g_down.astype(F32),
        vals[DB],
    )


def solution(mesh):
    placed = (
        P(("rep", "shard"), None),
        P(("rep", "shard"), None),
        P("shard"),
        P("shard"),
        P("shard", None),
        P("shard"),
        P("shard"),
        P("shard", None),
        P("shard"),
        P("shard"),
        P("shard"),
        P("shard", None),
        P("shard"),
        P("shard", None),
        P("shard"),
    )
    return jax.shard_map(
        on_device,
        mesh=mesh,
        in_specs=placed,
        out_specs=(
            P(("rep", "shard"), None),
            P(("rep", "shard"), None),
            P("shard"),
            P("shard"),
            P("shard", None),
            P("shard"),
            P("shard"),
            P("shard", None),
            P("shard"),
            P("shard"),
            P("shard"),
            P("shard", None),
            P("shard"),
            P("shard", None),
            P("shard"),
        ),
        check_vma=False,
    )
```

```python
import math

import jax
import jax.numpy as jnp
from jax import lax
from jax.experimental import pallas as pl
from jax.experimental.pallas import tpu as pltpu
from jax.sharding import PartitionSpec as P

HEADS = 16
HEAD_DIM = 64
SEQ = 320
D = 1024
NCH = 12
MESH = pl.DeviceIdType.MESH
BF16 = jnp.bfloat16
F32 = jnp.float32
MIB = 1024 * 1024

eps_norm = 1e-05
sqrt_two_pi = math.sqrt(2.0 / math.pi)
cubic_coef = 0.044715

LN1G, LN1B, QB, VB, OB, LN2G, LN2B, DB, UB = 0, 1, 2, 3, 4, 5, 6, 7, 8
WQ, WK, WV, WO, WUP, WDN = 0, 1, 2, 3, 4, 8


def place():
    rep = lax.axis_index("rep")
    shard = lax.axis_index("shard")
    x, lo, core = rep // 4, (rep // 2) % 2, rep % 2
    hi, z = shard // 4, shard % 4

    def dev(x_, lo_, core_, hi_, z_):
        return ((x_ * 2 + lo_) * 2 + core_, hi_ * 4 + z_)

    peers = dict(
        xr=dev((x + 1) % 4, lo, core, hi, z),
        xl=dev((x + 3) % 4, lo, core, hi, z),
        xo=dev((x + 2) % 4, lo, core, hi, z),
        zr=dev(x, lo, core, hi, (z + 1) % 4),
        zl=dev(x, lo, core, hi, (z + 3) % 4),
        zo=dev(x, lo, core, hi, (z + 2) % 4),
        cross=dev(x, 1 - lo, core, 1 - hi, z),
        ylo=dev(x, 1 - lo, core, hi, z),
        yo=dev(x, lo, core, 1 - hi, z),
        core=dev(x, lo, 1 - core, hi, z),
    )
    return x, core, hi, z, peers


def greet(peers, names):
    barrier = pltpu.get_barrier_semaphore()
    for name in names:
        pl.semaphore_signal(barrier, inc=1, device_id=peers[name], device_id_type=MESH)
    pl.semaphore_wait(barrier, len(names))


def loop(n, body):
    def step(i, carry):
        body(i)
        return carry

    lax.fori_loop(0, n, step, 0)


def rows_of(i, n):
    return pl.ds(pl.multiple_of(i * n, n), n)


def nn(a, b):
    return jnp.dot(a, b, preferred_element_type=F32)


def nt(a, b):
    return lax.dot_general(a, b, (((1,), (1,)), ((), ())), preferred_element_type=F32)


def tn(a, b):
    return lax.dot_general(a, b, (((0,), (0,)), ((), ())), preferred_element_type=F32)


def slope_of(h):
    return 2.0 ** (-8.0 * (h + 1) / HEADS)


def gelu_both(u):
    tanh_val = jnp.tanh(sqrt_two_pi * (u + cubic_coef * u * u * u))
    value = 0.5 * u * (1.0 + tanh_val)
    slope = 0.5 * (1.0 + tanh_val) + 0.5 * u * (1.0 - tanh_val * tanh_val) * sqrt_two_pi * (
        1.0 + 3.0 * cubic_coef * u * u
    )
    return value, slope


def center_scale(rows):
    c = rows - jnp.mean(rows, axis=-1, keepdims=True)
    s = lax.rsqrt(jnp.mean(c * c, axis=-1, keepdims=True) + eps_norm)
    return c * s, s


HALF = 512
NH = 24
GCOPIES = 20
GAP = 3


def forward_kernel(*refs):
    w_qkv, w_o, w_up, w_down, small, x_in = refs[:6]
    full_out, sm_all, block_out, act1_o, qkv_o, lse, ctx_o, act2_o, n2_o, hid_o, slope_o = refs[6:17]
    full, act1, qkv, ctx, act2, n2, hid, slope, mid, dist, vecs, qkv_bias = refs[17:29]
    act1_t, ctx_t, act2_t, hid_t = refs[29:33]
    send_sem, recv_sem, own_sem, out_sem, sm_send, sm_recv, save_sem = refs[33:]
    x, core, hi, z, peers = place()
    other = 1 - hi
    me = hi * 4 + z
    left, right, far = hi * 4 + (z + 3) % 4, hi * 4 + (z + 1) % 4, hi * 4 + (z + 2) % 4

    def own(src, m, cols):
        pltpu.make_async_copy(src, full.at[m, me, :, cols], own_sem.at[m]).start()

    wide = pl.ds(0, D)
    for c in range(3):
        own(w_qkv.at[:, pl.ds(c * D, D)], WQ + c, wide)
    own(w_o, WO, wide)
    for j in range(4):
        for s in range(8):
            own(w_up.at[:, pl.ds(s * 512 + j * 128, 128)], WUP + j, pl.ds(s * 128, 128))
    for j in range(4):
        own(w_down.at[pl.ds(j * 128, 128)], WDN + j, wide)
    sm_all[me] = small[...]
    greet(peers, ("xr", "xl", "zr", "zl", "cross", "core"))

    def remote(src, dst, ss, rs, to):
        return pltpu.make_async_remote_copy(
            src_ref=src,
            dst_ref=dst,
            send_sem=ss,
            recv_sem=rs,
            device_id=peers[to],
            device_id_type=MESH,
        )

    base, quarter = core * 64, core * 64 + x * 16
    others = pl.ds(other * 4, 4)
    sx = lambda i: base + ((x + i) % 4) * 16

    def table(m, cols):
        def view(which, first, count):
            return full.at[m, which, pl.ds(pl.multiple_of(first, 16), count), cols]

        return (
            ("z1r", view(me, base, 64), "zr", 0),
            ("z1l", view(me, base, 64), "zl", 1),
            ("y0", view(me, quarter, 16), "cross", 2),
            ("z2r", view(left, base, 32), "zr", 3),
            ("y1", view(left, quarter, 16), "cross", 2),
            ("c1", view(left, base, 64), "core", 8),
            ("z2l", view(right, base + 32, 32), "zl", 4),
            ("y2", view(right, quarter, 16), "cross", 2),
            ("c2", view(right, base, 64), "core", 8),
            ("y3", view(far, quarter, 16), "cross", 2),
            ("c3", view(far, base, 64), "core", 8),
            ("x1r", view(others, quarter, 16), "xr", 5),
            ("x1l", view(others, quarter, 16), "xl", 6),
            ("c4", view(others, quarter, 16), "core", 8),
            ("x2r", view(pl.ds(other * 4, 2), sx(3), 16), "xr", 7),
            ("c5", view(others, sx(3), 16), "core", 8),
            ("x2l", view(pl.ds(other * 4 + 2, 2), sx(1), 16), "xl", 9),
            ("c6", view(others, sx(1), 16), "core", 8),
            ("c7", view(others, sx(2), 16), "core", 8),
        )

    def copies(k):
        cols = pl.ds(pl.multiple_of((k % 2) * HALF, HALF), HALF)
        made = {
            name: remote(v, v, send_sem.at[i], recv_sem.at[k, r], to)
            for i, (name, v, to, r) in enumerate(table(k // 2, cols))
        }
        quarters = full.at[k // 2, others, pl.ds(pl.multiple_of(quarter, 16), 16), cols]
        made["y"] = remote(quarters, quarters, send_sem.at[2], recv_sem.at[k, 2], "cross")
        seven = full.at[k // 2, pl.ds(0, 7), pl.ds(pl.multiple_of(base, 64), 64), cols]
        made["c"] = remote(seven, seven, send_sem.at[5], recv_sem.at[k, 8], "core")
        return made

    def stage(waits, sends):
        def run(k):
            c = copies(k)
            for name in waits:
                c[name].wait_recv()
            for name in sends:
                c[name].start()

        return run

    def stage0(k):
        @pl.when(k % 2 == 0)
        def _():
            mine = full.at[k // 2, me]
            pltpu.make_async_copy(mine, mine, own_sem.at[k // 2]).wait()

        stage((), ("z1r", "z1l", "y0"))(k)

    def stage1(k):
        stage(("z1r",), ("z2r", "y1", "c1"))(k)
        stage(("z1l",), ("z2l", "y2", "c2"))(k)

    def stage4(k):
        stage(("x1r",), ("x2r", "c5"))(k)
        stage(("x1l",), ("x2l", "c6"))(k)

    def keep(m):
        return pltpu.make_async_copy(full.at[m], full_out.at[m], out_sem.at[m])

    def stage6(k):
        stage(("c",), ())(k)

        @pl.when(k % 2 == 1)
        def _():
            keep(k // 2).start()

    stages = (
        stage0,
        stage1,
        stage(("z2r", "z2l"), ("y3", "c3")),
        stage(("y",), ("x1r", "x1l", "c4")),
        stage4,
        stage(("x2r", "x2l"), ("c7",)),
        stage6,
    )

    def comm(t):
        for s in range(6, -1, -1):
            k = t - GAP * s

            @pl.when((k >= 0) & (k < NH))
            def _():
                stages[s](k)

    sm_copy = [
        remote(sm_all.at[me], sm_all.at[me], sm_send.at[0], sm_recv.at[0], "zr"),
        remote(sm_all.at[me], sm_all.at[me], sm_send.at[1], sm_recv.at[1], "zl"),
        remote(sm_all.at[left], sm_all.at[left], sm_send.at[2], sm_recv.at[2], "zr"),
        remote(sm_all.at[pl.ds(hi * 4, 4)], sm_all.at[pl.ds(hi * 4, 4)], sm_send.at[3], sm_recv.at[3], "cross"),
    ]

    def vec(i):
        return vecs[i : i + 1, :]

    def save(i, src, dst):
        return pltpu.make_async_copy(src, dst, save_sem.at[i])

    saves = [
        save(0, act1_t, act1_o),
        save(1, qkv, qkv_o),
        save(2, ctx_t, ctx_o),
        save(3, act2_t, act2_o),
        save(4, n2, n2_o),
    ]

    def turn(src, dst):
        def body(i):
            dst[rows_of(i, 256), :] = src[:, rows_of(i, 256)].T

        loop(4, body)

    def norm_one():
        for s in range(8):
            vecs[:, pl.ds(s * 128, 128)] = sm_all[s].astype(F32)
        qkv_bias[0:1, :] = vec(QB)
        qkv_bias[1:2, :] = jnp.zeros((1, D), F32)
        qkv_bias[2:3, :] = vec(VB)

        def body(i):
            r = rows_of(i, 32)
            n, s = center_scale(x_in[r, :].astype(F32))
            act1[r, :] = (n * vec(LN1G) + vec(LN1B)).astype(BF16)

        loop(10, body)
        row = lax.broadcasted_iota(jnp.int32, (SEQ, SEQ), 0)
        col = lax.broadcasted_iota(jnp.int32, (SEQ, SEQ), 1)
        dist[...] = (row - col).astype(F32)
        turn(act1, act1_t)
        saves[0].start()

    def matmul(a_ref, k, write):
        def body(i):
            cols = pl.ds(pl.multiple_of((k % 2) * HALF + i * 256, 256), 256)
            write(cols, nn(a_ref[...], full[k // 2, :, :, cols].reshape(D, 256)))

        loop(2, body)

    def project(k):
        def write(cols, res):
            qkv[k // 2, :, cols] = (res + qkv_bias[pl.ds(k // 2, 1), cols]).astype(BF16)

        matmul(act1, k, write)

    def attend(p, factor):
        cols = pl.ds(pl.multiple_of(p * 128, 128), 128)
        lane = lax.broadcasted_iota(jnp.int32, (SEQ, 128), 1)
        q_pair, k_pair, v_pair = qkv[0, :, cols], qkv[1, :, cols], qkv[2, :, cols]
        out = []
        lse_all = lse[...]
        for e in range(2):
            mine = (lane < 64) if e == 0 else (lane >= 64)
            s = nt(jnp.where(mine, q_pair, jnp.zeros_like(q_pair)), k_pair)
            d = dist[...]
            s = jnp.where(d >= 0.0, s * HEAD_DIM**-0.5 - (factor * slope_of(e)) * d, -jnp.inf)
            top = jnp.max(s, axis=-1, keepdims=True)
            s = jnp.exp(s - top)
            total = jnp.sum(s, axis=-1, keepdims=True)
            lse_all = jnp.where(lane == 2 * p + e, top + jnp.log(total), lse_all)
            out.append(nn((s / total).astype(BF16), v_pair))
        lse[...] = lse_all
        ctx[:, cols] = jnp.where(lane < 64, out[0], out[1]).astype(BF16)
        return factor * 0.5

    def attend_half(i):
        @pl.when(i == 0)
        def _():
            lse[...] = jnp.zeros_like(lse)
            saves[1].start()

        first = jnp.where(i == 0, 1.0, 0.0625).astype(F32)
        lax.fori_loop(0, 4, lambda p, f: attend(i * 4 + p, f), first)

    def out_proj():
        turn(ctx, ctx_t)
        saves[2].start()

        def body(k):
            def write(cols, res):
                mid[:, cols] = res + vecs[OB : OB + 1, cols] + x_in[:, cols].astype(F32)

            matmul(ctx, 2 * WO + k, write)

        loop(2, body)

        def norm(i):
            r = rows_of(i, 32)
            n, s = center_scale(mid[r, :])
            n2[r, pl.ds(0, D)] = n
            n2[r, pl.ds(D, 128)] = jnp.broadcast_to(s, (32, 128))
            act2[r, :] = (n * vec(LN2G) + vec(LN2B)).astype(BF16)

        loop(10, norm)
        turn(act2, act2_t)
        saves[3].start()
        saves[4].start()

    def save_up(j):
        return (
            pltpu.make_async_copy(hid_t.at[j], hid_o.at[j], save_sem.at[5 + j]),
            pltpu.make_async_copy(slope.at[j], slope_o.at[j], save_sem.at[9 + j]),
        )

    def up(k):
        j = k // 2 - WUP

        def write(cols, res):
            value, grad = gelu_both(res + vecs[pl.ds(UB + j, 1), cols])
            value = value.astype(BF16)
            hid[j, :, cols] = value
            hid_t[j, cols, :] = value.T
            slope[j, :, cols] = grad

        matmul(act2, k, write)

        @pl.when(k % 2 == 1)
        def _():
            for cp in save_up(j):
                cp.start()

    def down(k):
        j = k // 2 - WDN

        def write(cols, res):
            res = res + mid[:, cols]

            @pl.when(j < 3)
            def _():
                mid[:, cols] = res

            @pl.when(j == 3)
            def _():
                block_out[:, cols] = (res + vecs[DB : DB + 1, cols]).astype(BF16)

        matmul(hid.at[j], k, write)

    sm_copy[0].start()
    sm_copy[1].start()

    def slot(t):
        comm(t)

        @pl.when(t == 2)
        def _():
            sm_copy[0].wait_recv()
            sm_copy[1].wait_recv()
            sm_copy[2].start()

        @pl.when(t == 4)
        def _():
            sm_copy[2].wait_recv()
            sm_copy[3].start()

        @pl.when(t == 6)
        def _():
            sm_copy[3].wait_recv()
            norm_one()

        k = t - 6 * GAP

        @pl.when((k >= 0) & (k < 6))
        def _():
            project(k)

        @pl.when((k >= 6) & (k < 8))
        def _():
            attend_half(k - 6)

        @pl.when(k == 7)
        def _():
            out_proj()

        @pl.when((k >= 8) & (k < 16))
        def _():
            up(k)

        @pl.when(k >= 16)
        def _():
            down(k)

    loop(NH + 6 * GAP, slot)

    for i, (name, v, to, r) in enumerate(table(pl.ds(0, NCH), wide)):
        remote(v, v, send_sem.at[i], recv_sem.at[0, r], to).wait_send()
    for cp in sm_copy:
        cp.wait_send()
    for m in range(NCH):
        keep(m).wait()
    for cp in saves:
        cp.wait()
    for j in range(4):
        for cp in save_up(j):
            cp.wait()


def gather_forward(w_qkv, w_attn_out, w_up, w_down, small, x_in):
    vm = pl.BlockSpec(memory_space=pltpu.VMEM)
    hbm = pl.BlockSpec(memory_space=pl.ANY)
    S = jax.ShapeDtypeStruct
    V = pltpu.VMEM
    dma = pltpu.SemaphoreType.DMA
    act, turned = S((SEQ, D), BF16), S((D, SEQ), BF16)
    return pl.pallas_call(
        forward_kernel,
        out_shape=[
            S((NCH, 8, 128, D), BF16),
            S((8, 16, 128), BF16),
            act,
            turned,
            S((3, SEQ, D), BF16),
            S((SEQ, 128), F32),
            turned,
            turned,
            S((SEQ, D + 128), F32),
            S((4, D, SEQ), BF16),
            S((4, SEQ, D), F32),
        ],
        in_specs=[hbm] * 4 + [vm] * 2,
        out_specs=[hbm, vm, vm, hbm, hbm, vm, hbm, hbm, hbm, hbm, hbm],
        scratch_shapes=[
            V((NCH, 8, 128, D), BF16),
            V((SEQ, D), BF16),
            V((3, SEQ, D), BF16),
            V((SEQ, D), BF16),
            V((SEQ, D), BF16),
            V((SEQ, D + 128), F32),
            V((4, SEQ, D), BF16),
            V((4, SEQ, D), F32),
            V((SEQ, D), F32),
            V((SEQ, SEQ), F32),
            V((16, D), F32),
            V((8, D), F32),
            V((D, SEQ), BF16),
            V((D, SEQ), BF16),
            V((D, SEQ), BF16),
            V((4, D, SEQ), BF16),
            dma((GCOPIES,)),
            dma((NH, 10)),
            dma((NCH,)),
            dma((NCH,)),
            dma((4,)),
            dma((4,)),
            dma((13,)),
        ],
        compiler_params=pltpu.CompilerParams(
            collective_id=0, has_side_effects=True, vmem_limit_bytes=60 * MIB
        ),
        name="gather_forward",
    )(w_qkv, w_attn_out, w_up, w_down, small, x_in)


RCOPIES = 20
STAGED = 4
WSLOTS = 3
RGAP = 2
MADE = (
    [(m + j, h) for j in range(4) for m in (WDN, WUP) for h in range(2)]
    + [(WO, 0), (WO, 1)]
    + [(m, h) for h in range(2) for m in (WV, WK, WQ)]
)


def backward_kernel(*refs):
    full, hid_hbm, slope_hbm, sm_all, x_in, cot, act1, qkv, lse, ctx, act2, n2 = refs[:12]
    input_grad, out_qkv, out_o, out_up, out_down, fin_small = refs[12:18]
    acc, staged, rx1, rx2, ry, rz1, rz2, rp1, rp2, fin = refs[18:28]
    wbuf, hid_buf, slope_buf, cot_b, dub, dact, dmid, dmid_b, dctx, dqkv, dist, vecs = refs[28:40]
    sums, small_in = refs[40:42]
    send_sem, send_c, recv_sem, load_sem, hid_sem, sm_send, sm_recv = refs[42:]
    x, core, hi, z, peers = place()
    lo = (lax.axis_index("rep") // 2) % 2
    other = 1 - hi
    me = hi * 4 + z
    xp, xm, xo = (x + 1) % 4, (x + 3) % 4, (x + 2) % 4
    zp, zm, zo = (z + 1) % 4, (z + 3) % 4, (z + 2) % 4
    others = pl.ds(other * 4, 4)

    def remote(src, dst, ss, rs, to):
        return pltpu.make_async_remote_copy(
            src_ref=src,
            dst_ref=dst,
            send_sem=ss,
            recv_sem=rs,
            device_id=peers[to],
            device_id_type=MESH,
        )

    def sub(i):
        return pl.ds(pl.multiple_of(i * 16, 16), 16)

    def block(i):
        return pl.ds(pl.multiple_of(i * 128, 128), 128)

    def fin_rows(lo_):
        return pl.ds(pl.multiple_of(core * 64 + lo_ * 32, 32), 32)

    mine32 = pl.ds(pl.multiple_of(lo * 32, 32), 32)
    theirs32 = pl.ds(pl.multiple_of((1 - lo) * 32, 32), 32)

    def table(k):
        piece = fin.at[k, fin_rows(lo), block(x)]
        whole = fin.at[k, fin_rows(lo)]
        theirs = fin.at[k, fin_rows(1 - lo)]
        slot = k % STAGED if not isinstance(k, pl.Slice) else 0
        return (
            ("c", staged.at[slot, 1 - core], acc.at[k], "core"),
            ("x1r", acc.at[k, pl.ds(other * 4, 2), sub(xo)], rx1.at[k, 0], "xr"),
            ("x1l", acc.at[k, pl.ds(other * 4 + 2, 2), sub(xo)], rx1.at[k, 1], "xl"),
            ("x2r", acc.at[k, others, sub(xp)], rx2.at[k, 0], "xr"),
            ("x2l", acc.at[k, others, sub(xm)], rx2.at[k, 1], "xl"),
            ("y", acc.at[k, others, sub(x)], ry.at[k], "cross"),
            ("z1r", acc.at[k, hi * 4 + zo, pl.ds(0, 32)], rz1.at[k, 0], "zr"),
            ("z1l", acc.at[k, hi * 4 + zo, pl.ds(32, 32)], rz1.at[k, 1], "zl"),
            ("z2r", acc.at[k, hi * 4 + zp], rz2.at[k, 0], "zr"),
            ("z2l", acc.at[k, hi * 4 + zm], rz2.at[k, 1], "zl"),
            ("p1", acc.at[k, me, theirs32], rp1.at[k], "ylo"),
            ("p2r", acc.at[k, me, mine32, block(xp)], rp2.at[k, 0], "xr"),
            ("p2l", acc.at[k, me, mine32, block(xm)], rp2.at[k, 1], "xl"),
            ("p2o", acc.at[k, me, mine32, block(xo)], rp2.at[k, 2], "xo"),
            ("p3r", piece, piece, "xr"),
            ("p3l", piece, piece, "xl"),
            ("p3o", piece, piece, "xo"),
            ("p4y", whole, whole, "ylo"),
            ("p4c", whole, whole, "core"),
            ("p5", theirs, theirs, "core"),
        )

    def copies(k):
        return {
            name: remote(
                src, dst, send_c.at[k % STAGED] if name == "c" else send_sem.at[i], recv_sem.at[k, i], to
            )
            for i, (name, src, dst, to) in enumerate(table(k))
        }

    def got(c, *names):
        for name in names:
            c[name].wait_recv()

    def go(c, *names):
        for name in names:
            c[name].start()

    def add(idx, *terms):
        total = acc[idx].astype(F32)
        for ref, i in terms:
            total = total + ref[i].astype(F32)
        acc[idx] = total.astype(BF16)

    def s0(k):
        c = copies(k)
        got(c, "c")

        def body(i):
            add((k, i), (staged, (k % STAGED, core, i)))

        loop(8, body)
        go(c, "x1r", "x1l")

    def s1(k):
        c = copies(k)
        got(c, "x1r", "x1l")
        add((k, pl.ds(other * 4, 2), sub(xp)), (rx1, (k, 0)))
        go(c, "x2r")
        add((k, pl.ds(other * 4 + 2, 2), sub(xm)), (rx1, (k, 1)))
        go(c, "x2l")

    def s2(k):
        c = copies(k)
        got(c, "x2r", "x2l")
        add((k, others, sub(x)), (rx2, (k, 0)), (rx2, (k, 1)))
        go(c, "y")

    def s3(k):
        c = copies(k)
        got(c, "y")
        add((k, pl.ds(hi * 4, 4), sub(x)), (ry, (k,)))
        go(c, "z1r", "z1l")

    def s4(k):
        c = copies(k)
        got(c, "z1r", "z1l")
        add((k, hi * 4 + zp, pl.ds(0, 32)), (rz1, (k, 0)))
        go(c, "z2r")
        add((k, hi * 4 + zm, pl.ds(32, 32)), (rz1, (k, 1)))
        go(c, "z2l")

    def s5(k):
        c = copies(k)
        got(c, "z2r", "z2l")
        add((k, me), (rz2, (k, 0)), (rz2, (k, 1)))
        go(c, "p1")

    def s6(k):
        c = copies(k)
        got(c, "p1")
        add((k, me, mine32), (rp1, (k,)))
        go(c, "p2r", "p2l", "p2o")

    def s7(k):
        c = copies(k)
        got(c, "p2r", "p2l", "p2o")
        total = acc[k, me, mine32, block(x)].astype(F32)
        for i in range(3):
            total = total + rp2[k, i].astype(F32)
        fin[k, fin_rows(lo), block(x)] = (total * (1.0 / 128.0)).astype(BF16)
        go(c, "p3r", "p3l", "p3o")

    def s8(k):
        c = copies(k)
        got(c, "p3r", "p3l", "p3o")
        go(c, "p4y", "p4c")

    def s9(k):
        c = copies(k)
        got(c, "p4y")
        go(c, "p5")

    def s10(k):
        got(copies(k), "p4c", "p5")

    stages = (s0, s1, s2, s3, s4, s5, s6, s7, s8, s9, s10)

    def comm(t):
        for s in range(10, -1, -1):
            k = t - RGAP * (s + 1)

            @pl.when((k >= 0) & (k < NH))
            def _():
                stages[s](k)

    def produce(k, half, a_ref, b_ref):
        slot = k % STAGED

        @pl.when(k >= STAGED)
        def _():
            copies(k - STAGED)["c"].wait_send()

        cols = pl.ds(pl.multiple_of(half * HALF, HALF), HALF)

        def body(i):
            res = nn(a_ref[rows_of(i, 256), :], b_ref[:, cols]).astype(BF16)
            for e in range(2):
                for h in range(2):
                    first = e * 128 + h * 64
                    staged[slot, h, 2 * i + e] = res[first : first + 64]

        loop(4, body)
        copies(k)["c"].start()

    def load(m, u):
        return pltpu.make_async_copy(full.at[m], wbuf.at[u % WSLOTS], load_sem.at[u % WSLOTS])

    def bring(j):
        return (
            pltpu.make_async_copy(hid_hbm.at[j], hid_buf.at[j % 2], hid_sem.at[j % 2, 0]),
            pltpu.make_async_copy(slope_hbm.at[j], slope_buf.at[j % 2], hid_sem.at[j % 2, 1]),
        )

    def times_t(a_ref, u, write):
        def body(i):
            w = wbuf[u % WSLOTS, pl.ds(2 * i, 2)].reshape(256, D)
            write(rows_of(i, 256), nt(a_ref[...], w))

        loop(4, body)

    def bump(row, cols, rows):
        sums[row, cols] += jnp.sum(rows, axis=0, keepdims=True)

    def one(i):
        return pl.ds(i, 1)

    wide = pl.ds(0, D)
    load(WDN, 0).start()
    load(WUP, 1).start()
    load(WDN + 1, 2).start()
    for cp in bring(0):
        cp.start()
    sums[...] = jnp.zeros_like(sums)
    for s in range(8):
        vecs[:, pl.ds(s * 128, 128)] = sm_all[s].astype(F32)

    def prepare(i):
        r = rows_of(i, 32)
        rows = cot[r, :]
        cot_b[r, :] = rows.astype(BF16)
        bump(one(DB), wide, rows)

    loop(10, prepare)
    dact[...] = jnp.zeros_like(dact)
    iota_row = lax.broadcasted_iota(jnp.int32, (SEQ, SEQ), 0)
    iota_col = lax.broadcasted_iota(jnp.int32, (SEQ, SEQ), 1)
    dist[...] = (iota_row - iota_col).astype(F32)
    greet(peers, ("xr", "xl", "xo", "zr", "zl", "zo", "cross", "ylo", "yo", "core"))

    def ffn_first(j):
        for cp in bring(j):
            cp.wait()

        @pl.when(j < 3)
        def _():
            for cp in bring(j + 1):
                cp.start()

        load(WDN, 2 * j).wait()

        def write(cols, res):
            res = res * slope_buf[j % 2, :, cols]
            dub[:, cols] = res.astype(BF16)
            bump(one(UB + j), cols, res)

        times_t(cot_b, 2 * j, write)

        @pl.when(j < 3)
        def _():
            load(WUP + j + 1, 2 * j + 3).start()

        @pl.when(j == 3)
        def _():
            load(WV, 9).start()

    def ffn_second(j):
        load(WUP, 2 * j + 1).wait()

        def write(cols, res):
            dact[:, cols] += res

        times_t(dub, 2 * j + 1, write)

        @pl.when(j < 2)
        def _():
            load(WDN + j + 2, 2 * j + 4).start()

        @pl.when(j == 2)
        def _():
            load(WO, 8).start()

        @pl.when(j == 3)
        def _():
            load(WK, 10).start()

    def back(e, n):
        return e - jnp.mean(e, axis=-1, keepdims=True) - n * jnp.mean(e * n, axis=-1, keepdims=True)

    def norm_two(i):
        r = rows_of(i, 32)
        e, n, s = dact[r, :], n2[r, pl.ds(0, D)], n2[r, pl.ds(D, 128)][:, 0:1]
        bump(one(LN2G), wide, e * n)
        bump(one(LN2B), wide, e)
        m = cot[r, :] + s * back(e * vecs[LN2G : LN2G + 1, :], n)
        dmid[r, :] = m
        dmid_b[r, :] = m.astype(BF16)
        bump(one(OB), wide, m)

    def context():
        load(WO, 8).wait()

        def write(cols, res):
            dctx[:, cols] = res.astype(BF16)

        times_t(dmid_b, 8, write)
        load(WQ, 11).start()

    scale = HEAD_DIM**-0.5

    def attend_back(p, factor):
        lane = lax.broadcasted_iota(jnp.int32, (SEQ, 128), 1)
        lane_row = lax.broadcasted_iota(jnp.int32, (SEQ, 128), 1)
        cols = pl.ds(pl.multiple_of(p * 128, 128), 128)
        q_pair, k_pair, v_pair = qkv[0, :, cols], qkv[1, :, cols], qkv[2, :, cols]
        c_pair = dctx[:, cols]
        out = []
        for e in range(2):
            mine = (lane < 64) if e == 0 else (lane >= 64)
            zero = jnp.zeros_like(q_pair)
            s = nt(jnp.where(mine, q_pair, zero), k_pair)
            d = dist[...]
            s = jnp.where(d >= 0.0, s * scale - (factor * slope_of(e)) * d, -jnp.inf)
            total = jnp.sum(
                jnp.where(lane_row == 2 * p + e, lse[...], 0.0), axis=-1, keepdims=True
            )
            prob = jnp.exp(s - total)
            d_prob = nt(jnp.where(mine, c_pair, zero), v_pair)
            d_score = prob * (d_prob - jnp.sum(prob * d_prob, axis=-1, keepdims=True))
            d_score = d_score.astype(BF16)
            out.append((nn(d_score, k_pair), tn(d_score, q_pair), tn(prob.astype(BF16), c_pair)))
        low = lane < 64
        g_q = jnp.where(low, out[0][0], out[1][0]) * scale
        g_k = jnp.where(low, out[0][1], out[1][1]) * scale
        g_v = jnp.where(low, out[0][2], out[1][2])
        dqkv[2, :, cols], dqkv[1, :, cols], dqkv[0, :, cols] = (
            g_q.astype(BF16),
            g_k.astype(BF16),
            g_v.astype(BF16),
        )
        bump(one(QB), cols, g_q)
        bump(one(VB), cols, g_v)
        return factor * 0.5

    def first_grad(i):
        load(WV, 9 + i).wait()

        def write(cols, res):
            @pl.when(i == 0)
            def _():
                dact[:, cols] = res

            @pl.when(i > 0)
            def _():
                dact[:, cols] += res

        times_t(dqkv.at[i], 9 + i, write)

    def norm_one(i):
        r = rows_of(i, 32)
        n, s = center_scale(x_in[r, :].astype(F32))
        e = dact[r, :]
        bump(one(LN1G), wide, e * n)
        bump(one(LN1B), wide, e)
        input_grad[r, :] = dmid[r, :] + s * back(e * vecs[LN1G : LN1G + 1, :], n)

    rounds = (
        (core, 2, ("core",)),
        (x, 4, ("xr", "xl", "xo")),
        (hi * 2 + lo, 4, ("ylo", "cross", "yo")),
        (z, 4, ("zr", "zl", "zo")),
    )

    def small_copies(i):
        mine, n, to = rounds[i]
        view = small_in.at[i, mine]
        return [
            remote(view, view, sm_send.at[i, m], sm_recv.at[i, m], name)
            for m, name in enumerate(to)
        ]

    def small_round(i):
        if i == 0:
            small_in[0, core] = sums[...].astype(BF16)
        else:
            for cp in small_copies(i - 1):
                cp.wait_recv()
            total = small_in[i - 1, 0].astype(F32)
            for m in range(1, rounds[i - 1][1]):
                total = total + small_in[i - 1, m].astype(F32)
            if i < 4:
                small_in[i, rounds[i][0]] = total.astype(BF16)
            else:
                sums[...] = total * (1.0 / 128.0)
        if i < 4:
            for cp in small_copies(i):
                cp.start()

    def slot(t):
        comm(t)
        j, w, half = t // 4, (t // 2) % 2, t % 2

        @pl.when((t < 16) & (t % 4 == 0))
        def _():
            ffn_first(j)

        @pl.when((t < 16) & (w == 0))
        def _():
            produce(t, half, hid_buf.at[j % 2], cot_b)

        @pl.when((t < 16) & (w == 1))
        def _():
            produce(t, half, act2, dub)

        @pl.when((t < 16) & (t % 4 == 3))
        def _():
            ffn_second(j)

        @pl.when(t == 16)
        def _():
            loop(10, norm_two)

        @pl.when((t >= 16) & (t < 18))
        def _():
            produce(t, half, ctx, dmid_b)

        @pl.when(t == 17)
        def _():
            context()

        @pl.when((t >= 18) & (t < 20))
        def _():
            first = jnp.where(t == 18, 1.0, 0.0625).astype(F32)
            lax.fori_loop(0, 4, lambda p, f: attend_back((t - 18) * 4 + p, f), first)

        @pl.when((t >= 18) & (t < 24))
        def _():
            produce(t, (t - 18) // 3, act1, dqkv.at[(t - 18) % 3])

        @pl.when((t >= 24) & (t < 27))
        def _():
            first_grad(t - 24)

        @pl.when(t == 27)
        def _():
            loop(10, norm_one)

        for i in range(5):

            @pl.when(t == 28 + RGAP * i)
            def _():
                small_round(i)

    loop(NH + RGAP * 11, slot)
    fin_small[...] = sums[:, pl.ds(pl.multiple_of(me * 128, 128), 128)]
    for k in range(NH):
        m, half = MADE[k]
        cols = pl.ds(half * HALF, HALF)
        if m < WO:
            out_qkv[:, pl.ds(m * D + half * HALF, HALF)] = fin[k]
        elif m == WO:
            out_o[:, cols] = fin[k]
        elif m < WDN:
            for s in range(4):
                first = (half * 4 + s) * 512 + (m - WUP) * 128
                out_up[:, pl.ds(first, 128)] = fin[k, :, pl.ds(s * 128, 128)]
        else:
            out_down[pl.ds((m - WDN) * 128, 128), cols] = fin[k]

    for i, (name, src, dst, to) in enumerate(table(pl.ds(0, NH))):
        if name != "c":
            remote(src, dst, send_sem.at[i], recv_sem.at[0, i], to).wait_send()
    for k in range(NH - STAGED, NH):
        copies(k)["c"].wait_send()
    for i in range(4):
        for cp in small_copies(i):
            cp.wait_send()


def backward_reduce(full, hid, slope, sm, x_in, cot, act1, qkv, lse, ctx, act2, n2):
    vm = pl.BlockSpec(memory_space=pltpu.VMEM)
    hbm = pl.BlockSpec(memory_space=pl.ANY)
    S = jax.ShapeDtypeStruct
    V = pltpu.VMEM
    dma = pltpu.SemaphoreType.DMA
    return pl.pallas_call(
        backward_kernel,
        out_shape=[
            S((SEQ, D), F32),
            S((128, 3 * D), BF16),
            S((128, D), BF16),
            S((128, 4 * D), BF16),
            S((512, D), BF16),
            S((16, 128), F32),
        ],
        in_specs=[hbm] * 3 + [vm] * 9,
        out_specs=[vm] * 6,
        scratch_shapes=[
            V((NH, 8, 64, HALF), BF16),
            V((STAGED, 2, 8, 64, HALF), BF16),
            V((NH, 2, 2, 16, HALF), BF16),
            V((NH, 2, 4, 16, HALF), BF16),
            V((NH, 4, 16, HALF), BF16),
            V((NH, 2, 32, HALF), BF16),
            V((NH, 2, 64, HALF), BF16),
            V((NH, 32, HALF), BF16),
            V((NH, 3, 32, 128), BF16),
            V((NH, 128, HALF), BF16),
            V((WSLOTS, 8, 128, D), BF16),
            V((2, D, SEQ), BF16),
            V((2, SEQ, D), F32),
            V((SEQ, D), BF16),
            V((SEQ, D), BF16),
            V((SEQ, D), F32),
            V((SEQ, D), F32),
            V((SEQ, D), BF16),
            V((SEQ, D), BF16),
            V((3, SEQ, D), BF16),
            V((SEQ, SEQ), F32),
            V((16, D), F32),
            V((16, D), F32),
            V((4, 4, 16, D), BF16),
            dma((RCOPIES,)),
            dma((STAGED,)),
            dma((NH, RCOPIES)),
            dma((WSLOTS,)),
            dma((2, 2)),
            dma((4, 3)),
            dma((4, 3)),
        ],
        compiler_params=pltpu.CompilerParams(
            collective_id=1, has_side_effects=True, vmem_limit_bytes=63 * MIB
        ),
        name="backward_reduce",
    )(full, hid, slope, sm, x_in, cot, act1, qkv, lse, ctx, act2, n2)


def on_device(
    x_in,
    cotangent,
    ln1_gain,
    ln1_bias,
    w_qkv,
    q_bias,
    v_bias,
    w_attn_out,
    out_bias,
    ln2_gain,
    ln2_bias,
    w_up,
    up_bias,
    w_down,
    down_bias,
):
    rows = (ln1_gain, ln1_bias, q_bias, v_bias, out_bias, ln2_gain, ln2_bias, down_bias)
    small = jnp.pad(up_bias.reshape(4, 128), ((UB, 4), (0, 0)))
    for i, row in enumerate(rows):
        small = small + jnp.pad(row.reshape(1, 128), ((i, 15 - i), (0, 0)))
    full, sm, block_out, act1, qkv, lse, ctx, act2, n2, hid, slope = gather_forward(
        w_qkv, w_attn_out, w_up, w_down, small, x_in
    )
    input_grad, g_qkv, g_o, g_up, g_down, vals = backward_reduce(
        full, hid, slope, sm, x_in, cotangent, act1, qkv, lse, ctx, act2, n2
    )
    return (
        block_out,
        input_grad,
        vals[LN1G],
        vals[LN1B],
        g_qkv.astype(F32),
        vals[QB],
        vals[VB],
        g_o.astype(F32),
        vals[OB],
        vals[LN2G],
        vals[LN2B],
        g_up.astype(F32),
        vals[UB : UB + 4].reshape(-1),
        g_down.astype(F32),
        vals[DB],
    )


def solution(mesh):
    placed = (
        P(("rep", "shard"), None),
        P(("rep", "shard"), None),
        P("shard"),
        P("shard"),
        P("shard", None),
        P("shard"),
        P("shard"),
        P("shard", None),
        P("shard"),
        P("shard"),
        P("shard"),
        P("shard", None),
        P("shard"),
        P("shard", None),
        P("shard"),
    )
    return jax.shard_map(
        on_device,
        mesh=mesh,
        in_specs=placed,
        out_specs=(
            P(("rep", "shard"), None),
            P(("rep", "shard"), None),
            P("shard"),
            P("shard"),
            P("shard", None),
            P("shard"),
            P("shard"),
            P("shard", None),
            P("shard"),
            P("shard"),
            P("shard"),
            P("shard", None),
            P("shard"),
            P("shard", None),
            P("shard"),
        ),
        check_vma=False,
    )
```

```python
import math

import jax
import jax.numpy as jnp
from jax import lax
from jax.experimental import pallas as pl
from jax.experimental.pallas import tpu as pltpu
from jax.sharding import PartitionSpec as P

HEADS = 16
HEAD_DIM = 64
SEQ = 320
D = 1024
NCH = 12
MESH = pl.DeviceIdType.MESH
BF16 = jnp.bfloat16
F32 = jnp.float32
MIB = 1024 * 1024

eps_norm = 1e-05
sqrt_two_pi = math.sqrt(2.0 / math.pi)
cubic_coef = 0.044715

LN1G, LN1B, QB, VB, OB, LN2G, LN2B, DB, UB = 0, 1, 2, 3, 4, 5, 6, 7, 8
WQ, WK, WV, WO, WUP, WDN = 0, 1, 2, 3, 4, 8


def place():
    rep = lax.axis_index("rep")
    shard = lax.axis_index("shard")
    x, lo, core = rep // 4, (rep // 2) % 2, rep % 2
    hi, z = shard // 4, shard % 4

    def dev(x_, lo_, core_, hi_, z_):
        return ((x_ * 2 + lo_) * 2 + core_, hi_ * 4 + z_)

    peers = dict(
        xr=dev((x + 1) % 4, lo, core, hi, z),
        xl=dev((x + 3) % 4, lo, core, hi, z),
        xo=dev((x + 2) % 4, lo, core, hi, z),
        zr=dev(x, lo, core, hi, (z + 1) % 4),
        zl=dev(x, lo, core, hi, (z + 3) % 4),
        zo=dev(x, lo, core, hi, (z + 2) % 4),
        cross=dev(x, 1 - lo, core, 1 - hi, z),
        ylo=dev(x, 1 - lo, core, hi, z),
        yo=dev(x, lo, core, 1 - hi, z),
        core=dev(x, lo, 1 - core, hi, z),
    )
    return x, core, hi, z, peers


def greet(peers, names):
    barrier = pltpu.get_barrier_semaphore()
    for name in names:
        pl.semaphore_signal(barrier, inc=1, device_id=peers[name], device_id_type=MESH)
    pl.semaphore_wait(barrier, len(names))


def loop(n, body):
    def step(i, carry):
        body(i)
        return carry

    lax.fori_loop(0, n, step, 0)


def rows_of(i, n):
    return pl.ds(pl.multiple_of(i * n, n), n)


def nn(a, b):
    return jnp.dot(a, b, preferred_element_type=F32)


def nt(a, b):
    return lax.dot_general(a, b, (((1,), (1,)), ((), ())), preferred_element_type=F32)


def tn(a, b):
    return lax.dot_general(a, b, (((0,), (0,)), ((), ())), preferred_element_type=F32)


def slope_of(h):
    return 2.0 ** (-8.0 * (h + 1) / HEADS)


def gelu_both(u):
    tanh_val = jnp.tanh(sqrt_two_pi * (u + cubic_coef * u * u * u))
    value = 0.5 * u * (1.0 + tanh_val)
    slope = 0.5 * (1.0 + tanh_val) + 0.5 * u * (1.0 - tanh_val * tanh_val) * sqrt_two_pi * (
        1.0 + 3.0 * cubic_coef * u * u
    )
    return value, slope


def center_scale(rows):
    c = rows - jnp.mean(rows, axis=-1, keepdims=True)
    s = lax.rsqrt(jnp.mean(c * c, axis=-1, keepdims=True) + eps_norm)
    return c * s, s


HALF = 512
NH = 24
GCOPIES = 20
GAP = 2


def forward_kernel(*refs):
    w_qkv, w_o, w_up, w_down, small, x_in = refs[:6]
    full_out, sm_all, block_out, act1_o, qkv_o, lse, ctx_o, act2_o, n2_o, hid_o, slope_o = refs[6:17]
    full, act1, qkv, ctx, act2, n2, hid, slope, mid, dist, vecs, qkv_bias = refs[17:29]
    act1_t, ctx_t, act2_t, hid_t = refs[29:33]
    send_sem, recv_sem, own_sem, out_sem, sm_send, sm_recv, save_sem = refs[33:]
    x, core, hi, z, peers = place()
    other = 1 - hi
    me = hi * 4 + z
    left, right, far = hi * 4 + (z + 3) % 4, hi * 4 + (z + 1) % 4, hi * 4 + (z + 2) % 4

    def own(src, m, cols):
        pltpu.make_async_copy(src, full.at[m, me, :, cols], own_sem.at[m]).start()

    wide = pl.ds(0, D)
    for c in range(3):
        own(w_qkv.at[:, pl.ds(c * D, D)], WQ + c, wide)
    own(w_o, WO, wide)
    for j in range(4):
        for s in range(8):
            own(w_up.at[:, pl.ds(s * 512 + j * 128, 128)], WUP + j, pl.ds(s * 128, 128))
    for j in range(4):
        own(w_down.at[pl.ds(j * 128, 128)], WDN + j, wide)
    sm_all[me] = small[...]
    greet(peers, ("xr", "xl", "zr", "zl", "cross", "core"))

    def remote(src, dst, ss, rs, to):
        return pltpu.make_async_remote_copy(
            src_ref=src,
            dst_ref=dst,
            send_sem=ss,
            recv_sem=rs,
            device_id=peers[to],
            device_id_type=MESH,
        )

    base, quarter = core * 64, core * 64 + x * 16
    others = pl.ds(other * 4, 4)
    sx = lambda i: base + ((x + i) % 4) * 16

    def table(m, cols):
        def view(which, first, count):
            return full.at[m, which, pl.ds(pl.multiple_of(first, 16), count), cols]

        return (
            ("z1r", view(me, base, 64), "zr", 0),
            ("z1l", view(me, base, 64), "zl", 1),
            ("y0", view(me, quarter, 16), "cross", 2),
            ("z2r", view(left, base, 32), "zr", 3),
            ("y1", view(left, quarter, 16), "cross", 2),
            ("c1", view(left, base, 64), "core", 8),
            ("z2l", view(right, base + 32, 32), "zl", 4),
            ("y2", view(right, quarter, 16), "cross", 2),
            ("c2", view(right, base, 64), "core", 8),
            ("y3", view(far, quarter, 16), "cross", 2),
            ("c3", view(far, base, 64), "core", 8),
            ("x1r", view(others, quarter, 16), "xr", 5),
            ("x1l", view(others, quarter, 16), "xl", 6),
            ("c4", view(others, quarter, 16), "core", 8),
            ("x2r", view(pl.ds(other * 4, 2), sx(3), 16), "xr", 7),
            ("c5", view(others, sx(3), 16), "core", 8),
            ("x2l", view(pl.ds(other * 4 + 2, 2), sx(1), 16), "xl", 9),
            ("c6", view(others, sx(1), 16), "core", 8),
            ("c7", view(others, sx(2), 16), "core", 8),
        )

    def copies(k):
        cols = pl.ds(pl.multiple_of((k % 2) * HALF, HALF), HALF)
        made = {
            name: remote(v, v, send_sem.at[i], recv_sem.at[k, r], to)
            for i, (name, v, to, r) in enumerate(table(k // 2, cols))
        }
        quarters = full.at[k // 2, others, pl.ds(pl.multiple_of(quarter, 16), 16), cols]
        made["y"] = remote(quarters, quarters, send_sem.at[2], recv_sem.at[k, 2], "cross")
        seven = full.at[k // 2, pl.ds(0, 7), pl.ds(pl.multiple_of(base, 64), 64), cols]
        made["c"] = remote(seven, seven, send_sem.at[5], recv_sem.at[k, 8], "core")
        return made

    def stage(waits, sends):
        def run(k):
            c = copies(k)
            for name in waits:
                c[name].wait_recv()
            for name in sends:
                c[name].start()

        return run

    def stage0(k):
        @pl.when(k % 2 == 0)
        def _():
            mine = full.at[k // 2, me]
            pltpu.make_async_copy(mine, mine, own_sem.at[k // 2]).wait()

        stage((), ("z1r", "z1l", "y0"))(k)

    def stage1(k):
        stage(("z1r",), ("z2r", "y1", "c1"))(k)
        stage(("z1l",), ("z2l", "y2", "c2"))(k)

    def stage4(k):
        stage(("x1r",), ("x2r", "c5"))(k)
        stage(("x1l",), ("x2l", "c6"))(k)

    def keep(m):
        return pltpu.make_async_copy(full.at[m], full_out.at[m], out_sem.at[m])

    def stage6(k):
        stage(("c",), ())(k)

        @pl.when(k % 2 == 1)
        def _():
            keep(k // 2).start()

    stages = (
        stage0,
        stage1,
        stage(("z2r", "z2l"), ("y3", "c3")),
        stage(("y",), ("x1r", "x1l", "c4")),
        stage4,
        stage(("x2r", "x2l"), ("c7",)),
        stage6,
    )

    def comm(t):
        for s in range(7):
            k = t - GAP * s

            @pl.when((k >= 0) & (k < NH))
            def _():
                stages[s](k)

    sm_copy = [
        remote(sm_all.at[me], sm_all.at[me], sm_send.at[0], sm_recv.at[0], "zr"),
        remote(sm_all.at[me], sm_all.at[me], sm_send.at[1], sm_recv.at[1], "zl"),
        remote(sm_all.at[left], sm_all.at[left], sm_send.at[2], sm_recv.at[2], "zr"),
        remote(sm_all.at[pl.ds(hi * 4, 4)], sm_all.at[pl.ds(hi * 4, 4)], sm_send.at[3], sm_recv.at[3], "cross"),
    ]

    def vec(i):
        return vecs[i : i + 1, :]

    def save(i, src, dst):
        return pltpu.make_async_copy(src, dst, save_sem.at[i])

    saves = [
        save(0, act1_t, act1_o),
        save(1, qkv, qkv_o),
        save(2, ctx_t, ctx_o),
        save(3, act2_t, act2_o),
        save(4, n2, n2_o),
    ]

    def turn(src, dst):
        def body(i):
            dst[rows_of(i, 256), :] = src[:, rows_of(i, 256)].T

        loop(4, body)

    def norm_one():
        for s in range(8):
            vecs[:, pl.ds(s * 128, 128)] = sm_all[s].astype(F32)
        qkv_bias[0:1, :] = vec(QB)
        qkv_bias[1:2, :] = jnp.zeros((1, D), F32)
        qkv_bias[2:3, :] = vec(VB)

        def body(i):
            r = rows_of(i, 32)
            n, s = center_scale(x_in[r, :].astype(F32))
            act1[r, :] = (n * vec(LN1G) + vec(LN1B)).astype(BF16)

        loop(10, body)
        row = lax.broadcasted_iota(jnp.int32, (SEQ, SEQ), 0)
        col = lax.broadcasted_iota(jnp.int32, (SEQ, SEQ), 1)
        dist[...] = (row - col).astype(F32)
        turn(act1, act1_t)
        saves[0].start()

    def matmul(a_ref, k, write):
        def body(i):
            cols = pl.ds(pl.multiple_of((k % 2) * HALF + i * 256, 256), 256)
            write(cols, nn(a_ref[...], full[k // 2, :, :, cols].reshape(D, 256)))

        loop(2, body)

    def project(k):
        def write(cols, res):
            qkv[k // 2, :, cols] = (res + qkv_bias[pl.ds(k // 2, 1), cols]).astype(BF16)

        matmul(act1, k, write)

    def attend(p, factor):
        cols = pl.ds(pl.multiple_of(p * 128, 128), 128)
        lane = lax.broadcasted_iota(jnp.int32, (SEQ, 128), 1)
        q_pair, k_pair, v_pair = qkv[0, :, cols], qkv[1, :, cols], qkv[2, :, cols]
        out = []
        lse_all = lse[...]
        for e in range(2):
            mine = (lane < 64) if e == 0 else (lane >= 64)
            s = nt(jnp.where(mine, q_pair, jnp.zeros_like(q_pair)), k_pair)
            d = dist[...]
            s = jnp.where(d >= 0.0, s * HEAD_DIM**-0.5 - (factor * slope_of(e)) * d, -jnp.inf)
            top = jnp.max(s, axis=-1, keepdims=True)
            s = jnp.exp(s - top)
            total = jnp.sum(s, axis=-1, keepdims=True)
            lse_all = jnp.where(lane == 2 * p + e, top + jnp.log(total), lse_all)
            out.append(nn((s / total).astype(BF16), v_pair))
        lse[...] = lse_all
        ctx[:, cols] = jnp.where(lane < 64, out[0], out[1]).astype(BF16)
        return factor * 0.5

    def attend_half(i):
        @pl.when(i == 0)
        def _():
            lse[...] = jnp.zeros_like(lse)
            saves[1].start()

        first = jnp.where(i == 0, 1.0, 0.0625).astype(F32)
        lax.fori_loop(0, 4, lambda p, f: attend(i * 4 + p, f), first)

    def out_proj():
        turn(ctx, ctx_t)
        saves[2].start()

        def body(k):
            def write(cols, res):
                mid[:, cols] = res + vecs[OB : OB + 1, cols] + x_in[:, cols].astype(F32)

            matmul(ctx, 2 * WO + k, write)

        loop(2, body)

        def norm(i):
            r = rows_of(i, 32)
            n, s = center_scale(mid[r, :])
            n2[r, pl.ds(0, D)] = n
            n2[r, pl.ds(D, 128)] = jnp.broadcast_to(s, (32, 128))
            act2[r, :] = (n * vec(LN2G) + vec(LN2B)).astype(BF16)

        loop(10, norm)
        turn(act2, act2_t)
        saves[3].start()
        saves[4].start()

    def save_up(j):
        return (
            pltpu.make_async_copy(hid_t.at[j], hid_o.at[j], save_sem.at[5 + j]),
            pltpu.make_async_copy(slope.at[j], slope_o.at[j], save_sem.at[9 + j]),
        )

    def up(k):
        j = k // 2 - WUP

        def write(cols, res):
            value, grad = gelu_both(res + vecs[pl.ds(UB + j, 1), cols])
            value = value.astype(BF16)
            hid[j, :, cols] = value
            hid_t[j, cols, :] = value.T
            slope[j, :, cols] = grad

        matmul(act2, k, write)

        @pl.when(k % 2 == 1)
        def _():
            for cp in save_up(j):
                cp.start()

    def down(k):
        j = k // 2 - WDN

        def write(cols, res):
            res = res + mid[:, cols]

            @pl.when(j < 3)
            def _():
                mid[:, cols] = res

            @pl.when(j == 3)
            def _():
                block_out[:, cols] = (res + vecs[DB : DB + 1, cols]).astype(BF16)

        matmul(hid.at[j], k, write)

    sm_copy[0].start()
    sm_copy[1].start()

    def slot(t):
        comm(t)

        @pl.when(t == 2)
        def _():
            sm_copy[0].wait_recv()
            sm_copy[1].wait_recv()
            sm_copy[2].start()

        @pl.when(t == 4)
        def _():
            sm_copy[2].wait_recv()
            sm_copy[3].start()

        @pl.when(t == 6)
        def _():
            sm_copy[3].wait_recv()
            norm_one()

        k = t - 6 * GAP

        @pl.when((k >= 0) & (k < 6))
        def _():
            project(k)

        @pl.when((k >= 6) & (k < 8))
        def _():
            attend_half(k - 6)

        @pl.when(k == 7)
        def _():
            out_proj()

        @pl.when((k >= 8) & (k < 16))
        def _():
            up(k)

        @pl.when(k >= 16)
        def _():
            down(k)

    loop(NH + 6 * GAP, slot)

    for i, (name, v, to, r) in enumerate(table(pl.ds(0, NCH), wide)):
        remote(v, v, send_sem.at[i], recv_sem.at[0, r], to).wait_send()
    for cp in sm_copy:
        cp.wait_send()
    for m in range(NCH):
        keep(m).wait()
    for cp in saves:
        cp.wait()
    for j in range(4):
        for cp in save_up(j):
            cp.wait()


def gather_forward(w_qkv, w_attn_out, w_up, w_down, small, x_in):
    vm = pl.BlockSpec(memory_space=pltpu.VMEM)
    hbm = pl.BlockSpec(memory_space=pl.ANY)
    S = jax.ShapeDtypeStruct
    V = pltpu.VMEM
    dma = pltpu.SemaphoreType.DMA
    act, turned = S((SEQ, D), BF16), S((D, SEQ), BF16)
    return pl.pallas_call(
        forward_kernel,
        out_shape=[
            S((NCH, 8, 128, D), BF16),
            S((8, 16, 128), BF16),
            act,
            turned,
            S((3, SEQ, D), BF16),
            S((SEQ, 128), F32),
            turned,
            turned,
            S((SEQ, D + 128), F32),
            S((4, D, SEQ), BF16),
            S((4, SEQ, D), F32),
        ],
        in_specs=[hbm] * 4 + [vm] * 2,
        out_specs=[hbm, vm, vm, hbm, hbm, vm, hbm, hbm, hbm, hbm, hbm],
        scratch_shapes=[
            V((NCH, 8, 128, D), BF16),
            V((SEQ, D), BF16),
            V((3, SEQ, D), BF16),
            V((SEQ, D), BF16),
            V((SEQ, D), BF16),
            V((SEQ, D + 128), F32),
            V((4, SEQ, D), BF16),
            V((4, SEQ, D), F32),
            V((SEQ, D), F32),
            V((SEQ, SEQ), F32),
            V((16, D), F32),
            V((8, D), F32),
            V((D, SEQ), BF16),
            V((D, SEQ), BF16),
            V((D, SEQ), BF16),
            V((4, D, SEQ), BF16),
            dma((GCOPIES,)),
            dma((NH, 10)),
            dma((NCH,)),
            dma((NCH,)),
            dma((4,)),
            dma((4,)),
            dma((13,)),
        ],
        compiler_params=pltpu.CompilerParams(
            collective_id=0, has_side_effects=True, vmem_limit_bytes=60 * MIB
        ),
        name="gather_forward",
    )(w_qkv, w_attn_out, w_up, w_down, small, x_in)


RCOPIES = 20
STAGED = 4
WSLOTS = 3
RGAP = 2
MADE = (
    [(m + j, h) for j in range(4) for m in (WDN, WUP) for h in range(2)]
    + [(WO, 0), (WO, 1)]
    + [(m, h) for h in range(2) for m in (WV, WK, WQ)]
)


def backward_kernel(*refs):
    full, hid_hbm, slope_hbm, sm_all, x_in, cot, act1, qkv, lse, ctx, act2, n2 = refs[:12]
    input_grad, out_qkv, out_o, out_up, out_down, fin_small = refs[12:18]
    acc, staged, rx1, rx2, ry, rz1, rz2, rp1, rp2, fin = refs[18:28]
    wbuf, hid_buf, slope_buf, cot_b, dub, dact, dmid, dmid_b, dctx, dqkv, dist, vecs = refs[28:40]
    sums, small_in = refs[40:42]
    send_sem, send_c, recv_sem, load_sem, hid_sem, sm_send, sm_recv = refs[42:]
    x, core, hi, z, peers = place()
    lo = (lax.axis_index("rep") // 2) % 2
    other = 1 - hi
    me = hi * 4 + z
    xp, xm, xo = (x + 1) % 4, (x + 3) % 4, (x + 2) % 4
    zp, zm, zo = (z + 1) % 4, (z + 3) % 4, (z + 2) % 4
    others = pl.ds(other * 4, 4)

    def remote(src, dst, ss, rs, to):
        return pltpu.make_async_remote_copy(
            src_ref=src,
            dst_ref=dst,
            send_sem=ss,
            recv_sem=rs,
            device_id=peers[to],
            device_id_type=MESH,
        )

    def sub(i):
        return pl.ds(pl.multiple_of(i * 16, 16), 16)

    def block(i):
        return pl.ds(pl.multiple_of(i * 128, 128), 128)

    def fin_rows(lo_):
        return pl.ds(pl.multiple_of(core * 64 + lo_ * 32, 32), 32)

    mine32 = pl.ds(pl.multiple_of(lo * 32, 32), 32)
    theirs32 = pl.ds(pl.multiple_of((1 - lo) * 32, 32), 32)

    def table(k):
        piece = fin.at[k, fin_rows(lo), block(x)]
        whole = fin.at[k, fin_rows(lo)]
        theirs = fin.at[k, fin_rows(1 - lo)]
        slot = k % STAGED if not isinstance(k, pl.Slice) else 0
        return (
            ("c", staged.at[slot, 1 - core], acc.at[k], "core"),
            ("x1r", acc.at[k, pl.ds(other * 4, 2), sub(xo)], rx1.at[k, 0], "xr"),
            ("x1l", acc.at[k, pl.ds(other * 4 + 2, 2), sub(xo)], rx1.at[k, 1], "xl"),
            ("x2r", acc.at[k, others, sub(xp)], rx2.at[k, 0], "xr"),
            ("x2l", acc.at[k, others, sub(xm)], rx2.at[k, 1], "xl"),
            ("y", acc.at[k, others, sub(x)], ry.at[k], "cross"),
            ("z1r", acc.at[k, hi * 4 + zo, pl.ds(0, 32)], rz1.at[k, 0], "zr"),
            ("z1l", acc.at[k, hi * 4 + zo, pl.ds(32, 32)], rz1.at[k, 1], "zl"),
            ("z2r", acc.at[k, hi * 4 + zp], rz2.at[k, 0], "zr"),
            ("z2l", acc.at[k, hi * 4 + zm], rz2.at[k, 1], "zl"),
            ("p1", acc.at[k, me, theirs32], rp1.at[k], "ylo"),
            ("p2r", acc.at[k, me, mine32, block(xp)], rp2.at[k, 0], "xr"),
            ("p2l", acc.at[k, me, mine32, block(xm)], rp2.at[k, 1], "xl"),
            ("p2o", acc.at[k, me, mine32, block(xo)], rp2.at[k, 2], "xo"),
            ("p3r", piece, piece, "xr"),
            ("p3l", piece, piece, "xl"),
            ("p3o", piece, piece, "xo"),
            ("p4y", whole, whole, "ylo"),
            ("p4c", whole, whole, "core"),
            ("p5", theirs, theirs, "core"),
        )

    def copies(k):
        return {
            name: remote(
                src, dst, send_c.at[k % STAGED] if name == "c" else send_sem.at[i], recv_sem.at[k, i], to
            )
            for i, (name, src, dst, to) in enumerate(table(k))
        }

    def got(c, *names):
        for name in names:
            c[name].wait_recv()

    def go(c, *names):
        for name in names:
            c[name].start()

    def add(idx, *terms):
        total = acc[idx].astype(F32)
        for ref, i in terms:
            total = total + ref[i].astype(F32)
        acc[idx] = total.astype(BF16)

    def s0(k):
        c = copies(k)
        got(c, "c")

        def body(i):
            add((k, i), (staged, (k % STAGED, core, i)))

        loop(8, body)
        go(c, "x1r", "x1l")

    def s1(k):
        c = copies(k)
        got(c, "x1r", "x1l")
        add((k, pl.ds(other * 4, 2), sub(xp)), (rx1, (k, 0)))
        go(c, "x2r")
        add((k, pl.ds(other * 4 + 2, 2), sub(xm)), (rx1, (k, 1)))
        go(c, "x2l")

    def s2(k):
        c = copies(k)
        got(c, "x2r", "x2l")
        add((k, others, sub(x)), (rx2, (k, 0)), (rx2, (k, 1)))
        go(c, "y")

    def s3(k):
        c = copies(k)
        got(c, "y")
        add((k, pl.ds(hi * 4, 4), sub(x)), (ry, (k,)))
        go(c, "z1r", "z1l")

    def s4(k):
        c = copies(k)
        got(c, "z1r", "z1l")
        add((k, hi * 4 + zp, pl.ds(0, 32)), (rz1, (k, 0)))
        go(c, "z2r")
        add((k, hi * 4 + zm, pl.ds(32, 32)), (rz1, (k, 1)))
        go(c, "z2l")

    def s5(k):
        c = copies(k)
        got(c, "z2r", "z2l")
        add((k, me), (rz2, (k, 0)), (rz2, (k, 1)))
        go(c, "p1")

    def s6(k):
        c = copies(k)
        got(c, "p1")
        add((k, me, mine32), (rp1, (k,)))
        go(c, "p2r", "p2l", "p2o")

    def s7(k):
        c = copies(k)
        got(c, "p2r", "p2l", "p2o")
        total = acc[k, me, mine32, block(x)].astype(F32)
        for i in range(3):
            total = total + rp2[k, i].astype(F32)
        fin[k, fin_rows(lo), block(x)] = (total * (1.0 / 128.0)).astype(BF16)
        go(c, "p3r", "p3l", "p3o")

    def s8(k):
        c = copies(k)
        got(c, "p3r", "p3l", "p3o")
        go(c, "p4y", "p4c")

    def s9(k):
        c = copies(k)
        got(c, "p4y")
        go(c, "p5")

    def s10(k):
        got(copies(k), "p4c", "p5")

    stages = (s0, s1, s2, s3, s4, s5, s6, s7, s8, s9, s10)

    def comm(t):
        for s in range(11):
            k = t - RGAP * (s + 1)

            @pl.when((k >= 0) & (k < NH))
            def _():
                stages[s](k)

    def produce(k, half, a_ref, b_ref):
        slot = k % STAGED

        @pl.when(k >= STAGED)
        def _():
            copies(k - STAGED)["c"].wait_send()

        cols = pl.ds(pl.multiple_of(half * HALF, HALF), HALF)

        def body(i):
            res = nn(a_ref[rows_of(i, 256), :], b_ref[:, cols]).astype(BF16)
            for e in range(2):
                for h in range(2):
                    first = e * 128 + h * 64
                    staged[slot, h, 2 * i + e] = res[first : first + 64]

        loop(4, body)
        copies(k)["c"].start()

    def load(m, u):
        return pltpu.make_async_copy(full.at[m], wbuf.at[u % WSLOTS], load_sem.at[u % WSLOTS])

    def bring(j):
        return (
            pltpu.make_async_copy(hid_hbm.at[j], hid_buf.at[j % 2], hid_sem.at[j % 2, 0]),
            pltpu.make_async_copy(slope_hbm.at[j], slope_buf.at[j % 2], hid_sem.at[j % 2, 1]),
        )

    def times_t(a_ref, u, write):
        def body(i):
            w = wbuf[u % WSLOTS, pl.ds(2 * i, 2)].reshape(256, D)
            write(rows_of(i, 256), nt(a_ref[...], w))

        loop(4, body)

    def bump(row, cols, rows):
        sums[row, cols] += jnp.sum(rows, axis=0, keepdims=True)

    def one(i):
        return pl.ds(i, 1)

    wide = pl.ds(0, D)
    load(WDN, 0).start()
    load(WUP, 1).start()
    load(WDN + 1, 2).start()
    for cp in bring(0):
        cp.start()
    sums[...] = jnp.zeros_like(sums)
    for s in range(8):
        vecs[:, pl.ds(s * 128, 128)] = sm_all[s].astype(F32)

    def prepare(i):
        r = rows_of(i, 32)
        rows = cot[r, :]
        cot_b[r, :] = rows.astype(BF16)
        bump(one(DB), wide, rows)

    loop(10, prepare)
    dact[...] = jnp.zeros_like(dact)
    iota_row = lax.broadcasted_iota(jnp.int32, (SEQ, SEQ), 0)
    iota_col = lax.broadcasted_iota(jnp.int32, (SEQ, SEQ), 1)
    dist[...] = (iota_row - iota_col).astype(F32)
    greet(peers, ("xr", "xl", "xo", "zr", "zl", "zo", "cross", "ylo", "yo", "core"))

    def ffn_first(j):
        for cp in bring(j):
            cp.wait()

        @pl.when(j < 3)
        def _():
            for cp in bring(j + 1):
                cp.start()

        load(WDN, 2 * j).wait()

        def write(cols, res):
            res = res * slope_buf[j % 2, :, cols]
            dub[:, cols] = res.astype(BF16)
            bump(one(UB + j), cols, res)

        times_t(cot_b, 2 * j, write)

        @pl.when(j < 3)
        def _():
            load(WUP + j + 1, 2 * j + 3).start()

        @pl.when(j == 3)
        def _():
            load(WV, 9).start()

    def ffn_second(j):
        load(WUP, 2 * j + 1).wait()

        def write(cols, res):
            dact[:, cols] += res

        times_t(dub, 2 * j + 1, write)

        @pl.when(j < 2)
        def _():
            load(WDN + j + 2, 2 * j + 4).start()

        @pl.when(j == 2)
        def _():
            load(WO, 8).start()

        @pl.when(j == 3)
        def _():
            load(WK, 10).start()

    def back(e, n):
        return e - jnp.mean(e, axis=-1, keepdims=True) - n * jnp.mean(e * n, axis=-1, keepdims=True)

    def norm_two(i):
        r = rows_of(i, 32)
        e, n, s = dact[r, :], n2[r, pl.ds(0, D)], n2[r, pl.ds(D, 128)][:, 0:1]
        bump(one(LN2G), wide, e * n)
        bump(one(LN2B), wide, e)
        m = cot[r, :] + s * back(e * vecs[LN2G : LN2G + 1, :], n)
        dmid[r, :] = m
        dmid_b[r, :] = m.astype(BF16)
        bump(one(OB), wide, m)

    def context():
        load(WO, 8).wait()

        def write(cols, res):
            dctx[:, cols] = res.astype(BF16)

        times_t(dmid_b, 8, write)
        load(WQ, 11).start()

    scale = HEAD_DIM**-0.5

    def attend_back(p, factor):
        lane = lax.broadcasted_iota(jnp.int32, (SEQ, 128), 1)
        lane_row = lax.broadcasted_iota(jnp.int32, (SEQ, 128), 1)
        cols = pl.ds(pl.multiple_of(p * 128, 128), 128)
        q_pair, k_pair, v_pair = qkv[0, :, cols], qkv[1, :, cols], qkv[2, :, cols]
        c_pair = dctx[:, cols]
        out = []
        for e in range(2):
            mine = (lane < 64) if e == 0 else (lane >= 64)
            zero = jnp.zeros_like(q_pair)
            s = nt(jnp.where(mine, q_pair, zero), k_pair)
            d = dist[...]
            s = jnp.where(d >= 0.0, s * scale - (factor * slope_of(e)) * d, -jnp.inf)
            total = jnp.sum(
                jnp.where(lane_row == 2 * p + e, lse[...], 0.0), axis=-1, keepdims=True
            )
            prob = jnp.exp(s - total)
            d_prob = nt(jnp.where(mine, c_pair, zero), v_pair)
            d_score = prob * (d_prob - jnp.sum(prob * d_prob, axis=-1, keepdims=True))
            d_score = d_score.astype(BF16)
            out.append((nn(d_score, k_pair), tn(d_score, q_pair), tn(prob.astype(BF16), c_pair)))
        low = lane < 64
        g_q = jnp.where(low, out[0][0], out[1][0]) * scale
        g_k = jnp.where(low, out[0][1], out[1][1]) * scale
        g_v = jnp.where(low, out[0][2], out[1][2])
        dqkv[2, :, cols], dqkv[1, :, cols], dqkv[0, :, cols] = (
            g_q.astype(BF16),
            g_k.astype(BF16),
            g_v.astype(BF16),
        )
        bump(one(QB), cols, g_q)
        bump(one(VB), cols, g_v)
        return factor * 0.5

    def first_grad(i):
        load(WV, 9 + i).wait()

        def write(cols, res):
            @pl.when(i == 0)
            def _():
                dact[:, cols] = res

            @pl.when(i > 0)
            def _():
                dact[:, cols] += res

        times_t(dqkv.at[i], 9 + i, write)

    def norm_one(i):
        r = rows_of(i, 32)
        n, s = center_scale(x_in[r, :].astype(F32))
        e = dact[r, :]
        bump(one(LN1G), wide, e * n)
        bump(one(LN1B), wide, e)
        input_grad[r, :] = dmid[r, :] + s * back(e * vecs[LN1G : LN1G + 1, :], n)

    rounds = (
        (core, 2, ("core",)),
        (x, 4, ("xr", "xl", "xo")),
        (hi * 2 + lo, 4, ("ylo", "cross", "yo")),
        (z, 4, ("zr", "zl", "zo")),
    )

    def small_copies(i):
        mine, n, to = rounds[i]
        view = small_in.at[i, mine]
        return [
            remote(view, view, sm_send.at[i, m], sm_recv.at[i, m], name)
            for m, name in enumerate(to)
        ]

    def small_round(i):
        if i == 0:
            small_in[0, core] = sums[...].astype(BF16)
        else:
            for cp in small_copies(i - 1):
                cp.wait_recv()
            total = small_in[i - 1, 0].astype(F32)
            for m in range(1, rounds[i - 1][1]):
                total = total + small_in[i - 1, m].astype(F32)
            if i < 4:
                small_in[i, rounds[i][0]] = total.astype(BF16)
            else:
                sums[...] = total * (1.0 / 128.0)
        if i < 4:
            for cp in small_copies(i):
                cp.start()

    def slot(t):
        comm(t)
        j, w, half = t // 4, (t // 2) % 2, t % 2

        @pl.when((t < 16) & (t % 4 == 0))
        def _():
            ffn_first(j)

        @pl.when((t < 16) & (w == 0))
        def _():
            produce(t, half, hid_buf.at[j % 2], cot_b)

        @pl.when((t < 16) & (w == 1))
        def _():
            produce(t, half, act2, dub)

        @pl.when((t < 16) & (t % 4 == 3))
        def _():
            ffn_second(j)

        @pl.when(t == 16)
        def _():
            loop(10, norm_two)

        @pl.when((t >= 16) & (t < 18))
        def _():
            produce(t, half, ctx, dmid_b)

        @pl.when(t == 17)
        def _():
            context()

        @pl.when((t >= 18) & (t < 20))
        def _():
            first = jnp.where(t == 18, 1.0, 0.0625).astype(F32)
            lax.fori_loop(0, 4, lambda p, f: attend_back((t - 18) * 4 + p, f), first)

        @pl.when((t >= 18) & (t < 24))
        def _():
            produce(t, (t - 18) // 3, act1, dqkv.at[(t - 18) % 3])

        @pl.when((t >= 24) & (t < 27))
        def _():
            first_grad(t - 24)

        @pl.when(t == 27)
        def _():
            loop(10, norm_one)

        for i in range(5):

            @pl.when(t == 28 + RGAP * i)
            def _():
                small_round(i)

    loop(NH + RGAP * 11, slot)
    fin_small[...] = sums[:, pl.ds(pl.multiple_of(me * 128, 128), 128)]
    for k in range(NH):
        m, half = MADE[k]
        cols = pl.ds(half * HALF, HALF)
        if m < WO:
            out_qkv[:, pl.ds(m * D + half * HALF, HALF)] = fin[k]
        elif m == WO:
            out_o[:, cols] = fin[k]
        elif m < WDN:
            for s in range(4):
                first = (half * 4 + s) * 512 + (m - WUP) * 128
                out_up[:, pl.ds(first, 128)] = fin[k, :, pl.ds(s * 128, 128)]
        else:
            out_down[pl.ds((m - WDN) * 128, 128), cols] = fin[k]

    for i, (name, src, dst, to) in enumerate(table(pl.ds(0, NH))):
        if name != "c":
            remote(src, dst, send_sem.at[i], recv_sem.at[0, i], to).wait_send()
    for k in range(NH - STAGED, NH):
        copies(k)["c"].wait_send()
    for i in range(4):
        for cp in small_copies(i):
            cp.wait_send()


def backward_reduce(full, hid, slope, sm, x_in, cot, act1, qkv, lse, ctx, act2, n2):
    vm = pl.BlockSpec(memory_space=pltpu.VMEM)
    hbm = pl.BlockSpec(memory_space=pl.ANY)
    S = jax.ShapeDtypeStruct
    V = pltpu.VMEM
    dma = pltpu.SemaphoreType.DMA
    return pl.pallas_call(
        backward_kernel,
        out_shape=[
            S((SEQ, D), F32),
            S((128, 3 * D), BF16),
            S((128, D), BF16),
            S((128, 4 * D), BF16),
            S((512, D), BF16),
            S((16, 128), F32),
        ],
        in_specs=[hbm] * 3 + [vm] * 9,
        out_specs=[vm] * 6,
        scratch_shapes=[
            V((NH, 8, 64, HALF), BF16),
            V((STAGED, 2, 8, 64, HALF), BF16),
            V((NH, 2, 2, 16, HALF), BF16),
            V((NH, 2, 4, 16, HALF), BF16),
            V((NH, 4, 16, HALF), BF16),
            V((NH, 2, 32, HALF), BF16),
            V((NH, 2, 64, HALF), BF16),
            V((NH, 32, HALF), BF16),
            V((NH, 3, 32, 128), BF16),
            V((NH, 128, HALF), BF16),
            V((WSLOTS, 8, 128, D), BF16),
            V((2, D, SEQ), BF16),
            V((2, SEQ, D), F32),
            V((SEQ, D), BF16),
            V((SEQ, D), BF16),
            V((SEQ, D), F32),
            V((SEQ, D), F32),
            V((SEQ, D), BF16),
            V((SEQ, D), BF16),
            V((3, SEQ, D), BF16),
            V((SEQ, SEQ), F32),
            V((16, D), F32),
            V((16, D), F32),
            V((4, 4, 16, D), BF16),
            dma((RCOPIES,)),
            dma((STAGED,)),
            dma((NH, RCOPIES)),
            dma((WSLOTS,)),
            dma((2, 2)),
            dma((4, 3)),
            dma((4, 3)),
        ],
        compiler_params=pltpu.CompilerParams(
            collective_id=1, has_side_effects=True, vmem_limit_bytes=63 * MIB
        ),
        name="backward_reduce",
    )(full, hid, slope, sm, x_in, cot, act1, qkv, lse, ctx, act2, n2)


def on_device(
    x_in,
    cotangent,
    ln1_gain,
    ln1_bias,
    w_qkv,
    q_bias,
    v_bias,
    w_attn_out,
    out_bias,
    ln2_gain,
    ln2_bias,
    w_up,
    up_bias,
    w_down,
    down_bias,
):
    rows = (ln1_gain, ln1_bias, q_bias, v_bias, out_bias, ln2_gain, ln2_bias, down_bias)
    small = jnp.pad(up_bias.reshape(4, 128), ((UB, 4), (0, 0)))
    for i, row in enumerate(rows):
        small = small + jnp.pad(row.reshape(1, 128), ((i, 15 - i), (0, 0)))
    full, sm, block_out, act1, qkv, lse, ctx, act2, n2, hid, slope = gather_forward(
        w_qkv, w_attn_out, w_up, w_down, small, x_in
    )
    input_grad, g_qkv, g_o, g_up, g_down, vals = backward_reduce(
        full, hid, slope, sm, x_in, cotangent, act1, qkv, lse, ctx, act2, n2
    )
    return (
        block_out,
        input_grad,
        vals[LN1G],
        vals[LN1B],
        g_qkv.astype(F32),
        vals[QB],
        vals[VB],
        g_o.astype(F32),
        vals[OB],
        vals[LN2G],
        vals[LN2B],
        g_up.astype(F32),
        vals[UB : UB + 4].reshape(-1),
        g_down.astype(F32),
        vals[DB],
    )


def solution(mesh):
    placed = (
        P(("rep", "shard"), None),
        P(("rep", "shard"), None),
        P("shard"),
        P("shard"),
        P("shard", None),
        P("shard"),
        P("shard"),
        P("shard", None),
        P("shard"),
        P("shard"),
        P("shard"),
        P("shard", None),
        P("shard"),
        P("shard", None),
        P("shard"),
    )
    return jax.shard_map(
        on_device,
        mesh=mesh,
        in_specs=placed,
        out_specs=(
            P(("rep", "shard"), None),
            P(("rep", "shard"), None),
            P("shard"),
            P("shard"),
            P("shard", None),
            P("shard"),
            P("shard"),
            P("shard", None),
            P("shard"),
            P("shard"),
            P("shard"),
            P("shard", None),
            P("shard"),
            P("shard", None),
            P("shard"),
        ),
        check_vma=False,
    )
```
